32 devices in a mesh: space: 8 (over z, x), chan: 4 (over y, core).
Axes of the slice: x: 2, y: 2, z: 4, core: 2. Of those that a mesh axis runs over, the one named last changes fastest.
Arguments:
- features: bfloat16 [256, 8, 1024], P('chan', 'space'), may hold values from -6 to 6
- filters: bfloat16 [27, 256, 256], P(None, 'chan'), may hold values from -0.078125 to 0.078125
- out_bias: float32 [256], P('chan'), may hold values from -1 to 1
- loss_grad: bfloat16 [256, 8, 1024], P('chan', 'space'), may hold values from -6 to 6
Outputs:
- activated: float32 [256, 8, 1024], P('chan', 'space')
- in_grad: float32 [256, 8, 1024], P('chan', 'space')
- filter_grad: float32 [27, 256, 256], P(None, 'chan')
- bias_grad: float32 [256], replicated
The draws below stay inside these ranges and needn't reach their ends.
All inputs are finite; a program needn't handle non-finite values.
Results may differ from the reference program's by a relative error of at most 0.0031.
Values may be sent and summed in bfloat16 or wider, within the bound.
No kernel may reach another device: no remote copies, remote signals or barrier semaphores. Data moves between devices by JAX's collectives and lax.ppermute only.
A program may use at most 128 MiB of HBM per device.

```python
import math
import jax
import jax.numpy as jnp
from jax import lax

CIN = 256
COUT = 256
TAPS = 27
PLANE_H = 32
PLANE_W = 32
DEPTH = 8


def shard_levels(stream_key, shape, pieces, least, largest):
    loudness, own = 1.0, jax.random.fold_in(stream_key, 6)
    for dim, blocks in pieces:
        steps = jnp.exp(jax.random.uniform(jax.random.fold_in(own, dim), (blocks,), jnp.float32, least / len(pieces), largest / len(pieces)))
        loudness = loudness * jnp.repeat(steps, shape[dim] // blocks).reshape([-1 if axis == dim else 1 for axis in range(len(shape))])
    return loudness


def scatter_about(own_key, dims, scale, limit, split=(), dtype=jnp.bfloat16):
    values = jax.random.normal(own_key, dims, jnp.float32) * scale
    if len(split) > 0:
        values = shard_levels(own_key, dims, split, -0.22, 0.18) * values
    return jnp.clip(values, min=-limit, max=limit).astype(dtype)


def setup_inputs(seed: int = 0) -> dict:
    splits = jax.random.split(jax.random.key(seed), 5)
    return {
        "features": scatter_about(splits[0], (CIN, DEPTH, PLANE_H * PLANE_W), 1.0, 6.0, ((0, 4), (1, 8))),
        "filters": scatter_about(splits[1], (TAPS, CIN, COUT), (TAPS * CIN) ** -0.5, 0.078125, ((1, 4),)),
        "out_bias": jnp.clip(jax.random.uniform(splits[2], (COUT,), jnp.float32, -1.0, 1.0) * shard_levels(splits[2], (COUT,), ((0, 4),), -0.4, 0.0), -1.0, 1.0),
        "loss_grad": scatter_about(splits[3], (COUT, DEPTH, PLANE_H * PLANE_W), 1.0, 6.0, ((0, 4), (1, 8))),
    }


def window(padded, depth_off, row_off, col_off, planes):
    chans = padded.shape[0]
    piece = lax.slice(padded, (0, depth_off, row_off, col_off), (chans, depth_off + planes, row_off + PLANE_H, col_off + PLANE_W))
    return piece.reshape(chans, planes * PLANE_H * PLANE_W)

def reference(features, filters, out_bias, loss_grad):
    cells = PLANE_H * PLANE_W
    count = DEPTH * cells
    widths = ((0, 0), (1, 1), (1, 1), (1, 1))
    padded = jnp.pad(features.reshape(CIN, DEPTH, PLANE_H, PLANE_W), widths)
    summed = jnp.zeros((COUT, count), jnp.float32)
    offsets = [(tap // 9, tap // 3 % 3, tap % 3) for tap in range(TAPS)]
    for tap_index, (depth_off, row_off, col_off) in enumerate(offsets):
        piece = window(padded, depth_off, row_off, col_off, DEPTH)
        summed = summed + jnp.dot(filters[tap_index].T, piece, preferred_element_type=jnp.float32)
    pre_act = summed + out_bias.astype(jnp.float32)[:, None]
    sigmoid = jax.nn.sigmoid(pre_act)
    activated = pre_act * sigmoid
    grad_pre = (loss_grad.reshape(COUT, count).astype(jnp.float32) * sigmoid * (1.0 + pre_act * (1.0 - sigmoid))).astype(jnp.bfloat16)
    padded_grad = jnp.pad(grad_pre.reshape(COUT, DEPTH, PLANE_H, PLANE_W), widths)
    in_total = jnp.zeros((CIN, count), jnp.float32)
    filter_list = []
    for tap_index, (depth_off, row_off, col_off) in enumerate(offsets):
        shifted = window(padded_grad, 2 - depth_off, 2 - row_off, 2 - col_off, DEPTH)
        in_total = in_total + jnp.dot(filters[tap_index], shifted, preferred_element_type=jnp.float32)
        piece = window(padded, depth_off, row_off, col_off, DEPTH)
        filter_list.append(lax.dot_general(piece, grad_pre, (((1,), (1,)), ((), ())), preferred_element_type=jnp.float32))
    factor = 1.0 / math.sqrt(count)
    filter_grad = jnp.stack(filter_list, axis=0) * factor
    bias_grad = lax.optimization_barrier(jnp.sum(grad_pre.astype(jnp.float32), axis=1)) * factor
    in_grad = in_total.reshape(CIN, DEPTH, cells)
    return (activated.reshape(COUT, DEPTH, cells), in_grad, filter_grad, bias_grad)
```

```python
import functools
import math

import jax
import jax.numpy as jnp
from jax import lax
from jax.experimental import pallas as pl
from jax.experimental.pallas import tpu as pltpu
from jax.sharding import PartitionSpec as P

TAPS = 27
PLANE_H = 32
PLANE_W = 32
CELLS = PLANE_H * PLANE_W
VMEM = pl.BlockSpec(memory_space=pltpu.VMEM)
SMEM = pl.BlockSpec(memory_space=pltpu.SMEM)
BF16 = jnp.bfloat16
F32 = jnp.float32


def cell_mask(row_off, col_off):
    cell = lax.broadcasted_iota(jnp.int32, (1, CELLS), 1)
    row = cell // PLANE_W + row_off
    col = cell % PLANE_W + col_off
    inside = (row >= 0) & (row < PLANE_H) & (col >= 0) & (col < PLANE_W)
    return jnp.where(inside, 1.0, 0.0).astype(BF16)


def moved(plane, row_off, col_off):
    if row_off == 0 and col_off == 0:
        return plane
    amount = (-(row_off * PLANE_W + col_off)) % CELLS
    return pltpu.roll(plane, amount, 1) * cell_mask(row_off, col_off)


def forward_kernel(chans, parts, index, own, below, above, weights, *rest):
    outs, (stack, total) = rest[:parts], rest[parts:]
    for a, plane in enumerate((below, own, above)):
        cells = plane[...]
        for b in range(3):
            for e in range(3):
                tap = 9 * a + 3 * b + e
                stack[tap * chans : (tap + 1) * chans, :] = moved(cells, b - 1, e - 1)
    total[...] = jnp.dot(weights[...], stack[...], preferred_element_type=F32)
    for r in range(parts):
        start = pl.multiple_of((index[0] ^ r) * chans, chans)
        outs[r][...] = total[pl.ds(start, chans), :]


def forward_parts(index, own, below, above, weights, parts):
    chans = own.shape[0]
    outs = weights.shape[0]
    return pl.pallas_call(
        functools.partial(forward_kernel, chans, parts),
        out_shape=[jax.ShapeDtypeStruct((chans, CELLS), F32)] * parts,
        in_specs=[SMEM] + [VMEM] * 4,
        out_specs=[VMEM] * parts,
        scratch_shapes=[
            pltpu.VMEM((TAPS * chans, CELLS), BF16),
            pltpu.VMEM((outs, CELLS), F32),
        ],
        compiler_params=pltpu.CompilerParams(vmem_limit_bytes=40 << 20),
        cost_estimate=pl.CostEstimate(
            flops=2 * outs * TAPS * chans * CELLS, bytes_accessed=6 << 20, transcendentals=0
        ),
        name="forward_parts",
    )(index, own, below, above, weights)


def input_kernel(chans, index, mine, theirs, weights, below, own, above, stack, left):
    half = mine.shape[0]
    outs = weights.shape[2]
    for part, first in ((mine, 0), (theirs, half)):
        for u in range(half):
            start = pl.multiple_of((index[0] ^ index[1 + first + u]) * chans, chans)
            cells = part[u]
            for b in range(3):
                for e in range(3):
                    stack[3 * b + e, pl.ds(start, chans), :] = moved(cells, 1 - b, 1 - e)
    for a in range(3):
        for k in range(9):
            left[a * chans : (a + 1) * chans, k * outs : (k + 1) * outs] = weights[9 * a + k]
    total = jnp.dot(
        left[...], stack[...].reshape(9 * outs, CELLS), preferred_element_type=F32
    )
    below[...] = total[:chans].astype(BF16)
    own[...] = total[chans : 2 * chans]
    above[...] = total[2 * chans :].astype(BF16)


def input_parts(index, mine, theirs, weights):
    chans = weights.shape[1]
    outs = weights.shape[2]
    sides = jax.ShapeDtypeStruct((chans, CELLS), BF16)
    return pl.pallas_call(
        functools.partial(input_kernel, chans),
        out_shape=[sides, jax.ShapeDtypeStruct((chans, CELLS), F32), sides],
        in_specs=[SMEM] + [VMEM] * 3,
        out_specs=[VMEM] * 3,
        scratch_shapes=[
            pltpu.VMEM((9, outs, CELLS), BF16),
            pltpu.VMEM((3 * chans, 9 * outs), BF16),
        ],
        compiler_params=pltpu.CompilerParams(vmem_limit_bytes=40 << 20),
        cost_estimate=pl.CostEstimate(
            flops=2 * 3 * chans * 9 * outs * CELLS, bytes_accessed=6 << 20, transcendentals=0
        ),
        name="input_parts",
    )(index, mine, theirs, weights)


def filter_kernel(
    factor, flags, index, near, far, mine, theirs, out, shifted, rows, total, sums
):
    planes, chans = near.shape[0] * 2, near.shape[1]
    groups, _, share, _ = mine.shape
    width = 2 * groups * share
    space, chan = index[0], index[1]
    edge = jnp.zeros((3 * chans, CELLS), BF16)
    shifted[0] = edge
    shifted[planes + 1] = edge

    def fill(part, first):
        def step(q, _):
            depth = space ^ index[2 + first + q]
            cells = part[q]
            for e in range(3):
                shifted[depth + 1, e * chans : (e + 1) * chans, :] = moved(cells, 0, e - 1)
            return 0

        lax.fori_loop(0, part.shape[0], step, 0)

    fill(near, 0)
    fill(far, planes // 2)
    total[...] = jnp.zeros_like(total)
    sums[...] = jnp.zeros_like(sums)
    ones = jnp.ones((16, CELLS), BF16)

    def step(q, _):
        depth = space ^ index[2 + planes + q]
        for part, first in ((mine, 0), (theirs, groups)):
            for u in range(groups):
                group = chan ^ index[2 + 2 * planes + first + u]
                cells = part[u, q]
                for b in range(3):
                    start = pl.multiple_of(b * width + group * share, share)
                    rows[pl.ds(start, share), :] = moved(cells, 1 - b, 0)
        left = shifted[pl.ds(depth, 3)].reshape(9 * chans, CELLS)
        contract = (((1,), (1,)), ((), ()))
        total[...] += lax.dot_general(left, rows[...], contract, preferred_element_type=F32)
        sums[...] += lax.dot_general(
            ones, rows[width : 2 * width, :], contract, preferred_element_type=F32
        )
        return 0

    lax.fori_loop(0, planes, step, 0)
    for a in range(3):
        for e in range(3):
            for b in range(3):
                tap = 9 * a + 3 * b + e
                first = (3 * a + e) * chans
                out[tap * chans : (tap + 1) * chans, :] = (
                    total[first : first + chans, b * width : (b + 1) * width] * factor
                ).astype(BF16)
    bias = sums[...] * factor
    high = bias.astype(BF16)
    low = (bias - high.astype(F32)).astype(BF16)
    out[TAPS * chans : TAPS * chans + 16, :] = high
    out[TAPS * chans + 16 :, :] = low


def filter_half(index, near, far, mine, theirs, factor):
    half, chans, _ = near.shape
    groups, _, share, _ = mine.shape
    width = 2 * groups * share
    return pl.pallas_call(
        functools.partial(filter_kernel, factor, None),
        out_shape=jax.ShapeDtypeStruct((TAPS * chans + 32, width), BF16),
        in_specs=[SMEM] + [VMEM] * 4,
        out_specs=VMEM,
        scratch_shapes=[
            pltpu.VMEM((2 * half + 2, 3 * chans, CELLS), BF16),
            pltpu.VMEM((3 * width, CELLS), BF16),
            pltpu.VMEM((9 * chans, 3 * width), F32),
            pltpu.VMEM((16, width), F32),
        ],
        compiler_params=pltpu.CompilerParams(vmem_limit_bytes=52 << 20),
        cost_estimate=pl.CostEstimate(
            flops=2 * TAPS * chans * width * 2 * half * CELLS,
            bytes_accessed=8 << 20,
            transcendentals=0,
        ),
        name="filter_half",
    )(index, near, far, mine, theirs)


def spread(index, share, lanes, total):
    lane = lax.broadcasted_iota(jnp.int32, (lanes, total), 0)
    column = lax.broadcasted_iota(jnp.int32, (lanes, total), 1)
    home = (lane // share) * (2 * share) + index * share + lane % share
    return jnp.where(column == home, 1.0, 0.0).astype(BF16)


def join_kernel(share, index, mine, theirs, out, bias):
    lanes, total = mine.shape[1], out.shape[1]
    rows = out.shape[0]
    keep = spread(index[0], share, lanes, total)
    other = spread(1 - index[0], share, lanes, total)
    whole = jnp.dot(mine[...], keep, preferred_element_type=F32) + jnp.dot(
        theirs[...], other, preferred_element_type=F32
    )
    out[...] = whole[:rows]
    bias[...] = whole[rows : rows + 1] + whole[rows + 16 : rows + 17]


def join_halves(index, mine, theirs, share):
    rows = mine.shape[0] - 32
    total = 2 * mine.shape[1]
    return pl.pallas_call(
        functools.partial(join_kernel, share),
        out_shape=[
            jax.ShapeDtypeStruct((rows, total), F32),
            jax.ShapeDtypeStruct((1, total), F32),
        ],
        in_specs=[SMEM, VMEM, VMEM],
        out_specs=[VMEM, VMEM],
        compiler_params=pltpu.CompilerParams(vmem_limit_bytes=40 << 20),
        cost_estimate=pl.CostEstimate(
            flops=2 * rows * total * total, bytes_accessed=6 << 20, transcendentals=0
        ),
        name="join_halves",
    )(index, mine, theirs)


def swapped(value, axis, mask):
    count = lax.axis_size(axis)
    return lax.ppermute(value, axis, [(i, i ^ mask) for i in range(count)])


def doubled(value, axis, masks):
    flips = [0]
    for mask in masks[:-1]:
        value = jnp.concatenate([value, swapped(value, axis, mask)], axis=0)
        flips = flips + [f ^ mask for f in flips]
    flips = flips + [f ^ masks[-1] for f in flips]
    return value, swapped(value, axis, masks[-1]), flips


def body(features, filters, out_bias, loss_grad):
    chans, planes, cells = features.shape
    total_out = filters.shape[2]
    depth = lax.axis_size("space")
    groups = lax.axis_size("chan")
    space = lax.axis_index("space")
    chan = lax.axis_index("chan")
    share = chans // 2
    high_first = [1 << k for k in range(depth.bit_length() - 2, -1, -1)]
    chan_masks = [1 << k for k in range(groups.bit_length() - 2, -1, -1)]
    factor = 1.0 / math.sqrt(cells * planes * depth)

    own = features.reshape(chans, cells)
    up = [(i, i + 1) for i in range(depth - 1)]
    down = [(i + 1, i) for i in range(depth - 1)]
    below = lax.ppermute(own, "space", up)
    above = lax.ppermute(own, "space", down)
    weights = filters.reshape(TAPS * chans, total_out)
    parts = forward_parts(chan.reshape(1), own, below, above, weights.T, groups)
    pre_act = parts[0] + out_bias[:, None]
    for r in range(1, groups):
        pre_act = pre_act + swapped(parts[r], "chan", r)

    near, far, space_flips = doubled(own[None], "space", high_first)

    sigmoid = jax.nn.sigmoid(pre_act)
    activated = pre_act * sigmoid
    grad_pre = (
        loss_grad.reshape(chans, cells).astype(F32)
        * sigmoid
        * (1.0 + pre_act * (1.0 - sigmoid))
    ).astype(BF16)

    side = space & 1
    first, second = grad_pre[:share], grad_pre[share:]
    keep = jnp.where(side == 0, first, second)
    give = jnp.where(side == 0, second, first)
    pair = jnp.stack([keep, swapped(give, "space", 1)], axis=0)
    half, rest, grad_flips = doubled(pair, "space", high_first[:-1])
    grad_flips = [f ^ g for f in grad_flips[: depth // 2] for g in (0, 1)]
    gathered = jnp.concatenate([half, rest], axis=0)
    mine, theirs, chan_flips = doubled(gathered[None], "chan", chan_masks)

    grad_mine, grad_theirs, _ = doubled(grad_pre[None], "chan", chan_masks)
    to_below, in_own, to_above = input_parts(
        jnp.concatenate([chan.reshape(1), jnp.array(chan_flips, jnp.int32)]),
        grad_mine,
        grad_theirs,
        filters,
    )
    in_grad = (
        in_own
        + lax.ppermute(to_below, "space", down).astype(F32)
        + lax.ppermute(to_above, "space", up).astype(F32)
    )

    index = jnp.concatenate(
        [
            space.reshape(1),
            chan.reshape(1),
            jnp.array(space_flips + grad_flips + chan_flips, jnp.int32),
        ]
    )
    block = filter_half(index, near, far, mine, theirs, factor)
    joined, bias = join_halves(side.reshape(1), block, swapped(block, "space", 1), share)
    return (
        activated.reshape(chans, planes, cells),
        in_grad.reshape(chans, planes, cells),
        joined.reshape(TAPS, chans, total_out),
        bias.reshape(total_out),
    )


def solution(mesh):
    in_specs = (
        P("chan", "space", None),
        P(None, "chan", None),
        P("chan"),
        P("chan", "space", None),
    )
    out_specs = (P("chan", "space", None), P("chan", "space", None), P(None, "chan", None), P())
    return jax.shard_map(body, mesh=mesh, in_specs=in_specs, out_specs=out_specs, check_vma=False)
```

```python
import functools
import math

import jax
import jax.numpy as jnp
from jax import lax
from jax.experimental import pallas as pl
from jax.experimental.pallas import tpu as pltpu
from jax.sharding import PartitionSpec as P

TAPS = 27
PLANE_H = 32
PLANE_W = 32
CELLS = PLANE_H * PLANE_W
VMEM = pl.BlockSpec(memory_space=pltpu.VMEM)
SMEM = pl.BlockSpec(memory_space=pltpu.SMEM)
BF16 = jnp.bfloat16
F32 = jnp.float32


def cell_mask(row_off, col_off):
    cell = lax.broadcasted_iota(jnp.int32, (1, CELLS), 1)
    row = cell // PLANE_W + row_off
    col = cell % PLANE_W + col_off
    inside = (row >= 0) & (row < PLANE_H) & (col >= 0) & (col < PLANE_W)
    return jnp.where(inside, 1.0, 0.0).astype(BF16)


def moved(plane, row_off, col_off):
    if row_off == 0 and col_off == 0:
        return plane
    amount = (-(row_off * PLANE_W + col_off)) % CELLS
    return pltpu.roll(plane, amount, 1) * cell_mask(row_off, col_off)


def repeat(count, step):
    if count > 8:
        lax.fori_loop(0, count, lambda q, _: (step(q), 0)[1], 0)
    else:
        for q in range(count):
            step(q)


def forward_kernel(chans, index, own, below, above, weights, keep, give, stack, total):
    for a, plane in enumerate((below, own, above)):
        cells = plane[...]
        for b in range(3):
            for e in range(3):
                tap = 9 * a + 3 * b + e
                stack[tap * chans : (tap + 1) * chans, :] = moved(cells, b - 1, e - 1)
    total[...] = jnp.dot(weights[...], stack[...], preferred_element_type=F32)
    for j in range(keep.shape[0]):
        start = pl.multiple_of((index[0] ^ (2 * j)) * chans, chans)
        keep[j] = total[pl.ds(start, chans), :]
        start = pl.multiple_of((index[0] ^ (2 * j + 1)) * chans, chans)
        give[j] = total[pl.ds(start, chans), :]


def forward_parts(index, own, below, above, weights):
    chans = own.shape[0]
    outs = weights.shape[0]
    side = jax.ShapeDtypeStruct((outs // chans // 2, chans, CELLS), F32)
    return pl.pallas_call(
        functools.partial(forward_kernel, chans),
        out_shape=[side, side],
        in_specs=[SMEM] + [VMEM] * 4,
        out_specs=[VMEM] * 2,
        scratch_shapes=[
            pltpu.VMEM((TAPS * chans, CELLS), BF16),
            pltpu.VMEM((outs, CELLS), F32),
        ],
        compiler_params=pltpu.CompilerParams(vmem_limit_bytes=20 << 20),
        cost_estimate=pl.CostEstimate(
            flops=2 * outs * TAPS * chans * CELLS, bytes_accessed=6 << 20, transcendentals=0
        ),
        name="forward_parts",
    )(index, own, below, above, weights)


def input_kernel(chans, groups, index, *refs):
    grads = refs[:groups]
    weights, below, own, above, stack, left = refs[groups:]
    outs = weights.shape[2]
    for u in range(groups):
        start = pl.multiple_of((index[0] ^ u) * chans, chans)
        cells = grads[u][...]
        for b in range(3):
            for e in range(3):
                stack[3 * b + e, pl.ds(start, chans), :] = moved(cells, 1 - b, 1 - e)
    for a in range(3):
        for k in range(9):
            left[a * chans : (a + 1) * chans, k * outs : (k + 1) * outs] = weights[9 * a + k]
    total = jnp.dot(
        left[...], stack[...].reshape(9 * outs, CELLS), preferred_element_type=F32
    )
    below[...] = total[:chans].astype(BF16)
    own[...] = total[chans : 2 * chans]
    above[...] = total[2 * chans :].astype(BF16)


def input_parts(index, grads, weights):
    chans = weights.shape[1]
    outs = weights.shape[2]
    groups = len(grads)
    sides = jax.ShapeDtypeStruct((chans, CELLS), BF16)
    return pl.pallas_call(
        functools.partial(input_kernel, chans, groups),
        out_shape=[sides, jax.ShapeDtypeStruct((chans, CELLS), F32), sides],
        in_specs=[SMEM] + [VMEM] * (groups + 1),
        out_specs=[VMEM] * 3,
        scratch_shapes=[
            pltpu.VMEM((9, outs, CELLS), BF16),
            pltpu.VMEM((3 * chans, 9 * outs), BF16),
        ],
        compiler_params=pltpu.CompilerParams(vmem_limit_bytes=20 << 20),
        cost_estimate=pl.CostEstimate(
            flops=2 * 3 * chans * 9 * outs * CELLS, bytes_accessed=6 << 20, transcendentals=0
        ),
        name="input_parts",
    )(index, *grads, weights)


def filter_kernel(factor, groups, index, near, far, *refs):
    grads = refs[:groups]
    out, shifted, rows, total, sums = refs[groups:]
    planes, share, _ = grads[0].shape
    chans = near.shape[1]
    width = groups * share
    space, chan = index[0], index[1]
    edge = jnp.zeros((3 * chans, CELLS), BF16)
    shifted[0] = edge
    shifted[planes + 1] = edge
    for part, first in ((near, 0), (far, planes // 2)):

        def fill(q):
            depth = space ^ index[2 + first + q]
            cells = part[q]
            for e in range(3):
                shifted[depth + 1, e * chans : (e + 1) * chans, :] = moved(cells, 0, e - 1)

        repeat(planes // 2, fill)
    ones = jnp.ones((16, CELLS), BF16)
    contract = (((1,), (1,)), ((), ()))
    total[...] = jnp.zeros_like(total)
    sums[...] = jnp.zeros_like(sums)

    def step(q):
        for u in range(groups):
            cells = grads[u][q]
            for b in range(3):
                rows[q & 1, b * groups + (chan ^ u)] = moved(cells, 1 - b, 0)
        right = rows[q & 1].reshape(3 * width, CELLS)
        left = shifted[pl.ds(space ^ q, 3)].reshape(9 * chans, CELLS)
        term = lax.dot_general(left, right, contract, preferred_element_type=F32)
        count = lax.dot_general(
            ones, right[width : 2 * width], contract, preferred_element_type=F32
        )
        total[...] += term
        sums[...] += count

    repeat(planes, step)
    bias = sums[...] * factor
    high = bias.astype(BF16)
    low = (bias - high.astype(F32)).astype(BF16)

    def tile(tap):
        if tap == TAPS:
            rest = jnp.zeros((chans - 32, width), BF16)
            return jnp.concatenate([high, low, rest][: 2 + (chans > 32)], axis=0)
        a, b, e = tap // 9, tap // 3 % 3, tap % 3
        first = (3 * a + e) * chans
        piece = total[first : first + chans, b * width : (b + 1) * width]
        return (piece * factor).astype(BF16)

    for pair in range((TAPS + 1) // 2):
        out[pair * chans : (pair + 1) * chans, :] = jnp.concatenate(
            [tile(2 * pair), tile(2 * pair + 1)], axis=1
        )


def filter_block(index, near, far, grads, factor):
    half, chans, _ = near.shape
    groups = len(grads)
    planes, share, _ = grads[0].shape
    width = groups * share
    return pl.pallas_call(
        functools.partial(filter_kernel, factor, groups),
        out_shape=jax.ShapeDtypeStruct(((TAPS + 1) // 2 * chans, 2 * width), BF16),
        in_specs=[SMEM] + [VMEM] * (2 + groups),
        out_specs=VMEM,
        scratch_shapes=[
            pltpu.VMEM((planes + 2, 3 * chans, CELLS), BF16),
            pltpu.VMEM((2, 3 * groups, share, CELLS), BF16),
            pltpu.VMEM((9 * chans, 3 * width), F32),
            pltpu.VMEM((16, width), F32),
        ],
        compiler_params=pltpu.CompilerParams(vmem_limit_bytes=28 << 20),
        cost_estimate=pl.CostEstimate(
            flops=2 * TAPS * chans * width * planes * CELLS,
            bytes_accessed=8 << 20,
            transcendentals=0,
        ),
        name="filter_block",
    )(index, near, far, *grads)


def join_kernel(share, chans, index, *refs):
    blocks, (out, bias, right) = refs[:4], refs[4:]
    lanes, total = blocks[0].shape[1], out.shape[2]
    width = lanes // 2
    lane = lax.broadcasted_iota(jnp.int32, (lanes, total), 0)
    column = lax.broadcasted_iota(jnp.int32, (lanes, total), 1)
    slot = lane % width
    for odd in range(2):
        for r in range(4):
            home = (slot // share) * (4 * share) + (index[0] ^ r) * share + slot % share
            hit = (column == home) & (lane // width == odd)
            right[r * lanes : (r + 1) * lanes, odd * total : (odd + 1) * total] = jnp.where(
                hit, 1.0, 0.0
            ).astype(BF16)
    for pair in range((TAPS + 1) // 2):
        at = slice(pair * chans, (pair + 1) * chans)
        left = jnp.concatenate([block[at, :] for block in blocks], axis=1)
        both = jnp.dot(left, right[...], preferred_element_type=F32)
        out[2 * pair] = both[:, :total]
        if 2 * pair + 1 < TAPS:
            out[2 * pair + 1] = both[:, total:]
        else:
            bias[...] = both[0:1, total:] + both[16:17, total:]


def join_blocks(index, blocks, share, chans):
    lanes = blocks[0].shape[1]
    total = 2 * lanes
    return pl.pallas_call(
        functools.partial(join_kernel, share, chans),
        out_shape=[
            jax.ShapeDtypeStruct((TAPS, chans, total), F32),
            jax.ShapeDtypeStruct((1, total), F32),
        ],
        in_specs=[SMEM] + [VMEM] * 4,
        out_specs=[VMEM, VMEM],
        scratch_shapes=[pltpu.VMEM((4 * lanes, 2 * total), BF16)],
        compiler_params=pltpu.CompilerParams(vmem_limit_bytes=20 << 20),
        cost_estimate=pl.CostEstimate(
            flops=4 * TAPS * chans * total * lanes * 2, bytes_accessed=4 << 20, transcendentals=0
        ),
        name="join_blocks",
    )(index, *blocks)


def swapped(value, axis, mask):
    count = lax.axis_size(axis)
    return lax.ppermute(value, axis, [(i, i ^ mask) for i in range(count)])


def other_chips(value):
    found = [value]
    for k in range(1, lax.axis_size("chan").bit_length() - 1):
        found = found + [swapped(v, "chan", 1 << k) for v in found]
    return found


def both_cores(values):
    return [v for value in values for v in (value, swapped(value, "chan", 1))]


def body(features, filters, out_bias, loss_grad):
    chans, planes, cells = features.shape
    total_out = filters.shape[2]
    depth = lax.axis_size("space")
    groups = lax.axis_size("chan")
    space = lax.axis_index("space")
    chan = lax.axis_index("chan")
    share = chans // 4
    high_masks = [1 << k for k in range(depth.bit_length() - 2, 0, -1)]
    factor = 1.0 / math.sqrt(cells * planes * depth)
    barrier = lax.optimization_barrier

    own = features.reshape(chans, cells)
    up = [(i, i + 1) for i in range(depth - 1)]
    down = [(i + 1, i) for i in range(depth - 1)]
    below = lax.ppermute(own, "space", up)
    above = lax.ppermute(own, "space", down)
    weights = filters.reshape(TAPS * chans, total_out)
    keep, give = forward_parts(chan.reshape(1), own, below, above, weights.T)

    side = space & 1
    near = jnp.stack([own, jnp.where(side == 0, above, below)], axis=0)
    flips = [0, 1]
    for mask in high_masks[:-1]:
        near = jnp.concatenate([near, swapped(near, "space", mask)], axis=0)
        flips = flips + [f ^ mask for f in flips]

    got = swapped(give, "chan", 1)
    pre_act = keep[0] + got[0] + out_bias[:, None]
    for j in range(1, groups // 2):
        pre_act = pre_act + swapped(keep[j] + got[j], "chan", 2 * j)
    pre_act, near = barrier((pre_act, near))
    far = swapped(near, "space", high_masks[-1])
    flips = flips + [f ^ high_masks[-1] for f in flips]

    sigmoid = jax.nn.sigmoid(pre_act)
    activated = pre_act * sigmoid
    grad_pre = (
        loss_grad.reshape(chans, cells).astype(F32)
        * sigmoid
        * (1.0 + pre_act * (1.0 - sigmoid))
    ).astype(BF16)

    split = grad_pre.reshape(2, 2, share, cells)
    kept = jnp.where(side == 0, split[:, 0], split[:, 1])
    given = jnp.where(side == 0, split[:, 1], split[:, 0])
    pair = jnp.stack([kept, swapped(given, "space", 1)], axis=0)
    pair, grads = barrier((pair, other_chips(grad_pre)))
    grads = both_cores(grads)
    side = (space >> 1) & 1
    kept = jnp.where(side == 0, pair[:, 0], pair[:, 1])
    given = jnp.where(side == 0, pair[:, 1], pair[:, 0])
    pieces = [kept]
    for t in range(1, depth // 2):
        pieces.append(swapped(given if t & 1 else kept, "space", 2 * t))
    block = jnp.concatenate(pieces, axis=0)

    block, far, grads = barrier((block, far, grads))
    to_below, in_own, to_above = input_parts(chan.reshape(1), grads, filters)

    blocks, to_below, in_own, to_above = barrier(
        (other_chips(block), to_below, in_own, to_above)
    )
    blocks = both_cores(blocks)
    in_grad = (
        in_own
        + lax.ppermute(to_below, "space", down).astype(F32)
        + lax.ppermute(to_above, "space", up).astype(F32)
    )

    index = jnp.concatenate([space.reshape(1), chan.reshape(1), jnp.array(flips, jnp.int32)])
    part = filter_block(index, near, far, blocks, factor)
    parts = [part] + [swapped(part, "space", r) for r in range(1, 4)]
    joined, bias = join_blocks((space & 3).reshape(1), parts, share, chans)
    return (
        activated.reshape(chans, planes, cells),
        in_grad.reshape(chans, planes, cells),
        joined,
        bias.reshape(total_out),
    )


def solution(mesh):
    in_specs = (
        P("chan", "space", None),
        P(None, "chan", None),
        P("chan"),
        P("chan", "space", None),
    )
    out_specs = (P("chan", "space", None), P("chan", "space", None), P(None, "chan", None), P())
    return jax.shard_map(body, mesh=mesh, in_specs=in_specs, out_specs=out_specs, check_vma=False)
```

```python
import functools
import math

import jax
import jax.numpy as jnp
from jax import lax
from jax.experimental import pallas as pl
from jax.experimental.pallas import tpu as pltpu
from jax.sharding import PartitionSpec as P

TAPS = 27
PLANE_H = 32
PLANE_W = 32
CELLS = PLANE_H * PLANE_W
VMEM = pl.BlockSpec(memory_space=pltpu.VMEM)
SMEM = pl.BlockSpec(memory_space=pltpu.SMEM)
BF16 = jnp.bfloat16
F32 = jnp.float32


def cell_mask(row_off, col_off):
    cell = lax.broadcasted_iota(jnp.int32, (1, CELLS), 1)
    row = cell // PLANE_W + row_off
    col = cell % PLANE_W + col_off
    inside = (row >= 0) & (row < PLANE_H) & (col >= 0) & (col < PLANE_W)
    return jnp.where(inside, 1.0, 0.0).astype(BF16)


def moved(plane, row_off, col_off):
    if row_off == 0 and col_off == 0:
        return plane
    amount = (-(row_off * PLANE_W + col_off)) % CELLS
    return pltpu.roll(plane, amount, 1) * cell_mask(row_off, col_off)


def repeat(count, step):
    if count > 8:
        lax.fori_loop(0, count, lambda q, _: (step(q), 0)[1], 0)
    else:
        for q in range(count):
            step(q)


def forward_kernel(chans, index, own, below, above, weights, keep, give, stack, total):
    for a, plane in enumerate((below, own, above)):
        cells = plane[...]
        for b in range(3):
            for e in range(3):
                tap = 9 * a + 3 * b + e
                stack[tap * chans : (tap + 1) * chans, :] = moved(cells, b - 1, e - 1)
    total[...] = jnp.dot(weights[...], stack[...], preferred_element_type=F32)
    for j in range(keep.shape[0]):
        start = pl.multiple_of((index[0] ^ (2 * j)) * chans, chans)
        keep[j] = total[pl.ds(start, chans), :]
        start = pl.multiple_of((index[0] ^ (2 * j + 1)) * chans, chans)
        give[j] = total[pl.ds(start, chans), :]


def forward_parts(index, own, below, above, weights):
    chans = own.shape[0]
    outs = weights.shape[0]
    side = jax.ShapeDtypeStruct((outs // chans // 2, chans, CELLS), F32)
    return pl.pallas_call(
        functools.partial(forward_kernel, chans),
        out_shape=[side, side],
        in_specs=[SMEM] + [VMEM] * 4,
        out_specs=[VMEM] * 2,
        scratch_shapes=[
            pltpu.VMEM((TAPS * chans, CELLS), BF16),
            pltpu.VMEM((outs, CELLS), F32),
        ],
        compiler_params=pltpu.CompilerParams(vmem_limit_bytes=20 << 20),
        cost_estimate=pl.CostEstimate(
            flops=2 * outs * TAPS * chans * CELLS, bytes_accessed=6 << 20, transcendentals=0
        ),
        name="forward_parts",
    )(index, own, below, above, weights)


def input_kernel(chans, groups, index, *refs):
    grads = refs[:groups]
    weights, below, own, above, stack, left = refs[groups:]
    outs = weights.shape[2]
    for u in range(groups):
        start = pl.multiple_of((index[0] ^ u) * chans, chans)
        cells = grads[u][...]
        for b in range(3):
            for e in range(3):
                stack[3 * b + e, pl.ds(start, chans), :] = moved(cells, 1 - b, 1 - e)
    for a in range(3):
        for k in range(9):
            left[a * chans : (a + 1) * chans, k * outs : (k + 1) * outs] = weights[9 * a + k]
    total = jnp.dot(
        left[...], stack[...].reshape(9 * outs, CELLS), preferred_element_type=F32
    )
    below[...] = total[:chans].astype(BF16)
    own[...] = total[chans : 2 * chans]
    above[...] = total[2 * chans :].astype(BF16)


def input_parts(index, grads, weights):
    chans = weights.shape[1]
    outs = weights.shape[2]
    groups = len(grads)
    sides = jax.ShapeDtypeStruct((chans, CELLS), BF16)
    return pl.pallas_call(
        functools.partial(input_kernel, chans, groups),
        out_shape=[sides, jax.ShapeDtypeStruct((chans, CELLS), F32), sides],
        in_specs=[SMEM] + [VMEM] * (groups + 1),
        out_specs=[VMEM] * 3,
        scratch_shapes=[
            pltpu.VMEM((9, outs, CELLS), BF16),
            pltpu.VMEM((3 * chans, 9 * outs), BF16),
        ],
        compiler_params=pltpu.CompilerParams(vmem_limit_bytes=20 << 20),
        cost_estimate=pl.CostEstimate(
            flops=2 * 3 * chans * 9 * outs * CELLS, bytes_accessed=6 << 20, transcendentals=0
        ),
        name="input_parts",
    )(index, *grads, weights)


def filter_kernel(factor, groups, index, own, partner, near, far, *refs):
    grads = refs[:groups]
    out, shifted, rows, total, sums = refs[groups:]
    planes, share, _ = grads[0].shape
    chans = own.shape[0]
    width = groups * share
    space, chan = index[0], index[1]
    edge = jnp.zeros((3 * chans, CELLS), BF16)
    shifted[0] = edge
    shifted[planes + 1] = edge

    def place(depth, cells):
        for e in range(3):
            shifted[depth + 1, e * chans : (e + 1) * chans, :] = moved(cells, 0, e - 1)

    count = planes // 2 - 1
    place(space, own[...])
    place(space ^ 1, partner[...])
    repeat(count, lambda q: place(space ^ index[2 + q], near[q]))
    repeat(count, lambda q: place(space ^ index[2 + count + q], far[q]))
    ones = jnp.ones((16, CELLS), BF16)
    contract = (((1,), (1,)), ((), ()))
    total[...] = jnp.zeros_like(total)
    sums[...] = jnp.zeros_like(sums)

    def step(q):
        for u in range(groups):
            cells = grads[u][q]
            for b in range(3):
                rows[q & 1, b * groups + (chan ^ u)] = moved(cells, 1 - b, 0)
        right = rows[q & 1].reshape(3 * width, CELLS)
        left = shifted[pl.ds(space ^ q, 3)].reshape(9 * chans, CELLS)
        term = lax.dot_general(left, right, contract, preferred_element_type=F32)
        count = lax.dot_general(
            ones, right[width : 2 * width], contract, preferred_element_type=F32
        )
        total[...] += term
        sums[...] += count

    repeat(planes, step)
    bias = sums[...] * factor
    high = bias.astype(BF16)
    low = (bias - high.astype(F32)).astype(BF16)

    def tile(tap):
        if tap == TAPS:
            rest = jnp.zeros((chans - 32, width), BF16)
            return jnp.concatenate([high, low, rest][: 2 + (chans > 32)], axis=0)
        a, b, e = tap // 9, tap // 3 % 3, tap % 3
        first = (3 * a + e) * chans
        piece = total[first : first + chans, b * width : (b + 1) * width]
        return (piece * factor).astype(BF16)

    for pair in range((TAPS + 1) // 2):
        out[pair * chans : (pair + 1) * chans, :] = jnp.concatenate(
            [tile(2 * pair), tile(2 * pair + 1)], axis=1
        )


def filter_block(index, own, partner, near, far, grads, factor):
    chans = own.shape[0]
    groups = len(grads)
    planes, share, _ = grads[0].shape
    width = groups * share
    return pl.pallas_call(
        functools.partial(filter_kernel, factor, groups),
        out_shape=jax.ShapeDtypeStruct(((TAPS + 1) // 2 * chans, 2 * width), BF16),
        in_specs=[SMEM] + [VMEM] * (4 + groups),
        out_specs=VMEM,
        scratch_shapes=[
            pltpu.VMEM((planes + 2, 3 * chans, CELLS), BF16),
            pltpu.VMEM((2, 3 * groups, share, CELLS), BF16),
            pltpu.VMEM((9 * chans, 3 * width), F32),
            pltpu.VMEM((16, width), F32),
        ],
        compiler_params=pltpu.CompilerParams(vmem_limit_bytes=28 << 20),
        cost_estimate=pl.CostEstimate(
            flops=2 * TAPS * chans * width * planes * CELLS,
            bytes_accessed=8 << 20,
            transcendentals=0,
        ),
        name="filter_block",
    )(index, own, partner, near, far, *grads)


def join_kernel(share, chans, index, *refs):
    blocks, (out, bias, right) = refs[:4], refs[4:]
    lanes, total = blocks[0].shape[1], out.shape[2]
    width = lanes // 2
    lane = lax.broadcasted_iota(jnp.int32, (lanes, total), 0)
    column = lax.broadcasted_iota(jnp.int32, (lanes, total), 1)
    slot = lane % width
    for odd in range(2):
        for r in range(4):
            home = (slot // share) * (4 * share) + (index[0] ^ r) * share + slot % share
            hit = (column == home) & (lane // width == odd)
            right[r * lanes : (r + 1) * lanes, odd * total : (odd + 1) * total] = jnp.where(
                hit, 1.0, 0.0
            ).astype(BF16)
    for pair in range((TAPS + 1) // 2):
        at = slice(pair * chans, (pair + 1) * chans)
        left = jnp.concatenate([block[at, :] for block in blocks], axis=1)
        both = jnp.dot(left, right[...], preferred_element_type=F32)
        out[2 * pair] = both[:, :total]
        if 2 * pair + 1 < TAPS:
            out[2 * pair + 1] = both[:, total:]
        else:
            bias[...] = both[0:1, total:] + both[16:17, total:]


def join_blocks(index, blocks, share, chans):
    lanes = blocks[0].shape[1]
    total = 2 * lanes
    return pl.pallas_call(
        functools.partial(join_kernel, share, chans),
        out_shape=[
            jax.ShapeDtypeStruct((TAPS, chans, total), F32),
            jax.ShapeDtypeStruct((1, total), F32),
        ],
        in_specs=[SMEM] + [VMEM] * 4,
        out_specs=[VMEM, VMEM],
        scratch_shapes=[pltpu.VMEM((4 * lanes, 2 * total), BF16)],
        compiler_params=pltpu.CompilerParams(vmem_limit_bytes=20 << 20),
        cost_estimate=pl.CostEstimate(
            flops=4 * TAPS * chans * total * lanes * 2, bytes_accessed=4 << 20, transcendentals=0
        ),
        name="join_blocks",
    )(index, *blocks)


def swapped(value, axis, mask):
    count = lax.axis_size(axis)
    return lax.ppermute(value, axis, [(i, i ^ mask) for i in range(count)])


def other_chips(value):
    found = [value]
    for k in range(1, lax.axis_size("chan").bit_length() - 1):
        found = found + [swapped(v, "chan", 1 << k) for v in found]
    return found


def both_cores(values):
    return [v for value in values for v in (value, swapped(value, "chan", 1))]


def body(features, filters, out_bias, loss_grad):
    chans, planes, cells = features.shape
    total_out = filters.shape[2]
    depth = lax.axis_size("space")
    groups = lax.axis_size("chan")
    space = lax.axis_index("space")
    chan = lax.axis_index("chan")
    share = chans // 4
    masks = [1 << k for k in range(depth.bit_length() - 2, -1, -1)]
    factor = 1.0 / math.sqrt(cells * planes * depth)
    barrier = lax.optimization_barrier

    own = features.reshape(chans, cells)
    up = [(i, i + 1) for i in range(depth - 1)]
    down = [(i + 1, i) for i in range(depth - 1)]
    below = lax.ppermute(own, "space", up)
    above = lax.ppermute(own, "space", down)
    near = [swapped(own, "space", mask) for mask in masks[:2]]
    below, above, near = barrier((below, above, near))
    weights = filters.reshape(TAPS * chans, total_out)
    keep, give = forward_parts(chan.reshape(1), own, below, above, weights.T)

    got = swapped(give, "chan", 1)
    partial = [keep[j] + got[j] for j in range(1, groups // 2)]
    pre_act = keep[0] + got[0] + out_bias[:, None]
    for j, term in enumerate(partial):
        pre_act = pre_act + swapped(term, "chan", 2 * (j + 1))
    pre_act, near = barrier((pre_act, near))
    near = jnp.stack(near + [swapped(near[0], "space", masks[1])], axis=0)
    flips = [masks[0], masks[1], masks[0] ^ masks[1]]
    for mask in masks[2:-1]:
        own_too = jnp.concatenate([own[None], near], axis=0)
        near = jnp.concatenate([near, swapped(own_too, "space", mask)], axis=0)
        flips = flips + [f ^ mask for f in [0] + flips]

    sigmoid = jax.nn.sigmoid(pre_act)
    activated = pre_act * sigmoid
    grad_pre = (
        loss_grad.reshape(chans, cells).astype(F32)
        * sigmoid
        * (1.0 + pre_act * (1.0 - sigmoid))
    ).astype(BF16)

    split = grad_pre.reshape(2, 2, share, cells)
    side = space & 1
    kept = jnp.where(side == 0, split[:, 0], split[:, 1])
    given = jnp.where(side == 0, split[:, 1], split[:, 0])
    pair = jnp.stack([kept, swapped(given, "space", 1)], axis=0)
    pair, near = barrier((pair, near))
    far = swapped(near, "space", masks[-1])
    flips = flips + [f ^ 1 for f in flips]
    partner = jnp.where(side == 0, above, below)
    side = (space >> 1) & 1
    kept = jnp.where(side == 0, pair[:, 0], pair[:, 1])
    given = jnp.where(side == 0, pair[:, 1], pair[:, 0])
    pieces = [kept]
    for t in range(1, depth // 2):
        pieces.append(swapped(given if t & 1 else kept, "space", 2 * t))

    grads = both_cores(other_chips(grad_pre))
    terms = input_parts(chan.reshape(1), grads, filters)
    pieces[0], (to_below, in_own, to_above) = barrier((pieces[0], terms))
    from_above = lax.ppermute(to_below, "space", down)
    from_below = lax.ppermute(to_above, "space", up)
    blocks = other_chips(jnp.concatenate(pieces, axis=0))
    blocks, far, from_above, from_below = barrier((blocks, far, from_above, from_below))
    blocks = both_cores(blocks)
    in_grad = in_own + from_above.astype(F32) + from_below.astype(F32)

    index = jnp.concatenate([space.reshape(1), chan.reshape(1), jnp.array(flips, jnp.int32)])
    part = filter_block(index, own, partner, near, far, blocks, factor)
    parts = [part] + [swapped(part, "space", r) for r in range(1, 4)]
    joined, bias = join_blocks((space & 3).reshape(1), parts, share, chans)
    return (
        activated.reshape(chans, planes, cells),
        in_grad.reshape(chans, planes, cells),
        joined,
        bias.reshape(total_out),
    )


def solution(mesh):
    in_specs = (
        P("chan", "space", None),
        P(None, "chan", None),
        P("chan"),
        P("chan", "space", None),
    )
    out_specs = (P("chan", "space", None), P("chan", "space", None), P(None, "chan", None), P())
    return jax.shard_map(body, mesh=mesh, in_specs=in_specs, out_specs=out_specs, check_vma=False)
```

```python
import functools
import math

import jax
import jax.numpy as jnp
from jax import lax
from jax.experimental import pallas as pl
from jax.experimental.pallas import tpu as pltpu
from jax.sharding import PartitionSpec as P

TAPS = 27
PLANE_H = 32
PLANE_W = 32
CELLS = PLANE_H * PLANE_W
CHUNKS = ((0, 8), (8, 16), (16, 24), (24, TAPS))
VMEM = pl.BlockSpec(memory_space=pltpu.VMEM)
SMEM = pl.BlockSpec(memory_space=pltpu.SMEM)
BF16 = jnp.bfloat16
F32 = jnp.float32


def cell_mask(row_off, col_off):
    cell = lax.broadcasted_iota(jnp.int32, (1, CELLS), 1)
    row = cell // PLANE_W + row_off
    col = cell % PLANE_W + col_off
    inside = (row >= 0) & (row < PLANE_H) & (col >= 0) & (col < PLANE_W)
    return jnp.where(inside, 1.0, 0.0).astype(BF16)


def moved(plane, row_off, col_off):
    if row_off == 0 and col_off == 0:
        return plane
    amount = (-(row_off * PLANE_W + col_off)) % CELLS
    return pltpu.roll(plane, amount, 1) * cell_mask(row_off, col_off)


def repeat(count, step):
    if count > 8:
        lax.fori_loop(0, count, lambda q, _: (step(q), 0)[1], 0)
    else:
        for q in range(count):
            step(q)


def forward_kernel(chans, index, own, partner, outer, weights, keep, give, stack, total):
    above = 2 * (1 - index[1])
    for a, plane in ((1, own), (above, partner), (2 - above, outer)):
        cells = plane[...]
        for b in range(3):
            for e in range(3):
                start = (9 * a + 3 * b + e) * chans
                if plane is not own:
                    start = pl.multiple_of(start, chans)
                stack[pl.ds(start, chans), :] = moved(cells, b - 1, e - 1)
    total[...] = jnp.dot(weights[...], stack[...], preferred_element_type=F32)
    for j in range(keep.shape[0]):
        start = pl.multiple_of((index[0] ^ (2 * j)) * chans, chans)
        keep[j] = total[pl.ds(start, chans), :]
        start = pl.multiple_of((index[0] ^ (2 * j + 1)) * chans, chans)
        give[j] = total[pl.ds(start, chans), :]


def forward_parts(index, own, partner, outer, weights):
    chans = own.shape[0]
    outs = weights.shape[0]
    side = jax.ShapeDtypeStruct((outs // chans // 2, chans, CELLS), F32)
    return pl.pallas_call(
        functools.partial(forward_kernel, chans),
        out_shape=[side, side],
        in_specs=[SMEM] + [VMEM] * 4,
        out_specs=[VMEM] * 2,
        scratch_shapes=[
            pltpu.VMEM((TAPS * chans, CELLS), BF16),
            pltpu.VMEM((outs, CELLS), F32),
        ],
        compiler_params=pltpu.CompilerParams(vmem_limit_bytes=20 << 20),
        cost_estimate=pl.CostEstimate(
            flops=2 * outs * TAPS * chans * CELLS, bytes_accessed=6 << 20, transcendentals=0
        ),
        name="forward_parts",
    )(index, own, partner, outer, weights)


def input_kernel(chans, groups, index, *refs):
    grads = refs[:groups]
    weights, own, partner, outer, stack, left, total = refs[groups:]
    outs = weights.shape[2]
    for u in range(groups):
        start = pl.multiple_of((index[0] ^ u) * chans, chans)
        cells = grads[u][...]
        for b in range(3):
            for e in range(3):
                stack[3 * b + e, pl.ds(start, chans), :] = moved(cells, 1 - b, 1 - e)
    for a in range(3):
        for k in range(9):
            left[a * chans : (a + 1) * chans, k * outs : (k + 1) * outs] = weights[9 * a + k]
    total[...] = jnp.dot(
        left[...], stack[...].reshape(9 * outs, CELLS), preferred_element_type=F32
    )
    above = pl.multiple_of(2 * (1 - index[1]) * chans, chans)
    below = pl.multiple_of(2 * index[1] * chans, chans)
    own[...] = total[chans : 2 * chans]
    partner[...] = total[pl.ds(above, chans), :].astype(BF16)
    outer[...] = total[pl.ds(below, chans), :].astype(BF16)


def input_parts(index, grads, weights):
    chans = weights.shape[1]
    outs = weights.shape[2]
    groups = len(grads)
    sides = jax.ShapeDtypeStruct((chans, CELLS), BF16)
    return pl.pallas_call(
        functools.partial(input_kernel, chans, groups),
        out_shape=[jax.ShapeDtypeStruct((chans, CELLS), F32), sides, sides],
        in_specs=[SMEM] + [VMEM] * (groups + 1),
        out_specs=[VMEM] * 3,
        scratch_shapes=[
            pltpu.VMEM((9, outs, CELLS), BF16),
            pltpu.VMEM((3 * chans, 9 * outs), BF16),
            pltpu.VMEM((3 * chans, CELLS), F32),
        ],
        compiler_params=pltpu.CompilerParams(vmem_limit_bytes=20 << 20),
        cost_estimate=pl.CostEstimate(
            flops=2 * 3 * chans * 9 * outs * CELLS, bytes_accessed=6 << 20, transcendentals=0
        ),
        name="input_parts",
    )(index, *grads, weights)


def filter_kernel(factor, groups, index, own, partner, near, far, *refs):
    grads = refs[:groups]
    out, shifted, rows, total, sums = refs[groups:]
    planes, share, _ = grads[0].shape
    chans = own.shape[0]
    width = groups * share
    space, chan = index[0], index[1]
    edge = jnp.zeros((3 * chans, CELLS), BF16)
    shifted[0] = edge
    shifted[planes + 1] = edge

    def place(depth, cells):
        for e in range(3):
            shifted[depth + 1, e * chans : (e + 1) * chans, :] = moved(cells, 0, e - 1)

    count = planes // 2 - 1
    place(space, own[...])
    place(space ^ 1, partner[...])
    repeat(count, lambda q: place(space ^ index[2 + q], near[q]))
    repeat(count, lambda q: place(space ^ index[2 + count + q], far[q]))
    ones = jnp.ones((16, CELLS), BF16)
    contract = (((1,), (1,)), ((), ()))
    total[...] = jnp.zeros_like(total)
    sums[...] = jnp.zeros_like(sums)

    def step(q):
        for u in range(groups):
            cells = grads[u][q]
            for b in range(3):
                rows[q & 1, b * groups + (chan ^ u)] = moved(cells, 1 - b, 0)
        right = rows[q & 1].reshape(3 * width, CELLS)
        left = shifted[pl.ds(space ^ q, 3)].reshape(9 * chans, CELLS)
        term = lax.dot_general(left, right, contract, preferred_element_type=F32)
        count = lax.dot_general(
            ones, right[width : 2 * width], contract, preferred_element_type=F32
        )
        total[...] += term
        sums[...] += count

    repeat(planes, step)
    bias = sums[...] * factor
    high = bias.astype(BF16)
    low = (bias - high.astype(F32)).astype(BF16)

    def tile(tap):
        if tap == TAPS:
            rest = jnp.zeros((chans - 32, width), BF16)
            return jnp.concatenate([high, low, rest][: 2 + (chans > 32)], axis=0)
        a, b, e = tap // 9, tap // 3 % 3, tap % 3
        first = (3 * a + e) * chans
        piece = total[first : first + chans, b * width : (b + 1) * width]
        return (piece * factor).astype(BF16)

    for pair in range((TAPS + 1) // 2):
        out[pair * chans : (pair + 1) * chans, :] = jnp.concatenate(
            [tile(2 * pair), tile(2 * pair + 1)], axis=1
        )


def filter_block(index, own, partner, near, far, grads, factor):
    chans = own.shape[0]
    groups = len(grads)
    planes, share, _ = grads[0].shape
    width = groups * share
    return pl.pallas_call(
        functools.partial(filter_kernel, factor, groups),
        out_shape=jax.ShapeDtypeStruct(((TAPS + 1) // 2 * chans, 2 * width), BF16),
        in_specs=[SMEM] + [VMEM] * (4 + groups),
        out_specs=VMEM,
        scratch_shapes=[
            pltpu.VMEM((planes + 2, 3 * chans, CELLS), BF16),
            pltpu.VMEM((2, 3 * groups, share, CELLS), BF16),
            pltpu.VMEM((9 * chans, 3 * width), F32),
            pltpu.VMEM((16, width), F32),
        ],
        compiler_params=pltpu.CompilerParams(vmem_limit_bytes=28 << 20),
        cost_estimate=pl.CostEstimate(
            flops=2 * TAPS * chans * width * planes * CELLS,
            bytes_accessed=8 << 20,
            transcendentals=0,
        ),
        name="filter_block",
    )(index, own, partner, near, far, *grads)


def join_kernel(share, chans, index, *refs):
    blocks, (out, bias, right, held, done) = refs[:4], refs[4:]
    lanes, total = blocks[0].shape[1], out.shape[2]
    width = lanes // 2
    lane = lax.broadcasted_iota(jnp.int32, (lanes, total), 0)
    column = lax.broadcasted_iota(jnp.int32, (lanes, total), 1)
    slot = lane % width
    for odd in range(2):
        for r in range(4):
            home = (slot // share) * (4 * share) + (index[0] ^ r) * share + slot % share
            hit = (column == home) & (lane // width == odd)
            right[r * lanes : (r + 1) * lanes, odd * total : (odd + 1) * total] = jnp.where(
                hit, 1.0, 0.0
            ).astype(BF16)
    copies = []
    for pair in range((TAPS + 1) // 2):
        at = slice(pair * chans, (pair + 1) * chans)
        left = jnp.concatenate([block[at, :] for block in blocks], axis=1)
        both = jnp.dot(left, right[...], preferred_element_type=F32)
        held[2 * pair] = both[:, :total]
        if 2 * pair + 1 < TAPS:
            held[2 * pair + 1] = both[:, total:]
        else:
            bias[...] = both[0:1, total:] + both[16:17, total:]
        for k, (first, last) in enumerate(CHUNKS):
            if last == min(2 * pair + 2, TAPS):
                part = pl.ds(first, last - first)
                copies.append(pltpu.make_async_copy(held.at[part], out.at[part], done.at[k]))
                copies[-1].start()
    for copy in copies:
        copy.wait()


def join_blocks(index, blocks, share, chans):
    lanes = blocks[0].shape[1]
    total = 2 * lanes
    return pl.pallas_call(
        functools.partial(join_kernel, share, chans),
        out_shape=[
            jax.ShapeDtypeStruct((TAPS, chans, total), F32),
            jax.ShapeDtypeStruct((1, total), F32),
        ],
        in_specs=[SMEM] + [VMEM] * 4,
        out_specs=[pl.BlockSpec(memory_space=pl.ANY), VMEM],
        scratch_shapes=[
            pltpu.VMEM((4 * lanes, 2 * total), BF16),
            pltpu.VMEM((TAPS, chans, total), F32),
            pltpu.SemaphoreType.DMA((len(CHUNKS),)),
        ],
        compiler_params=pltpu.CompilerParams(vmem_limit_bytes=20 << 20),
        cost_estimate=pl.CostEstimate(
            flops=4 * TAPS * chans * total * lanes * 2, bytes_accessed=4 << 20, transcendentals=0
        ),
        name="join_blocks",
    )(index, *blocks)


def swapped(value, axis, mask):
    count = lax.axis_size(axis)
    return lax.ppermute(value, axis, [(i, i ^ mask) for i in range(count)])


def exchanged(value):
    pairs = [(i, i + 1) for i in range(1, lax.axis_size("space") - 1, 2)]
    return lax.ppermute(value, "space", pairs + [(j, i) for i, j in pairs])


def other_chips(value):
    found = [value]
    for k in range(1, lax.axis_size("chan").bit_length() - 1):
        found = found + [swapped(v, "chan", 1 << k) for v in found]
    return found


def both_cores(values):
    return [v for value in values for v in (value, swapped(value, "chan", 1))]


def body(features, filters, out_bias, loss_grad):
    chans, planes, cells = features.shape
    total_out = filters.shape[2]
    depth = lax.axis_size("space")
    groups = lax.axis_size("chan")
    space = lax.axis_index("space")
    chan = lax.axis_index("chan")
    share = chans // 4
    factor = 1.0 / math.sqrt(cells * planes * depth)
    barrier = lax.optimization_barrier

    own = features.reshape(chans, cells)
    weights, ahead = barrier((filters.reshape(TAPS * chans, total_out).T, own))
    near = swapped(ahead, "space", 4)[None]
    partner, outer = swapped(own, "space", 1), exchanged(own)
    outer, partner, near = barrier((outer, partner, near))
    side = (space & 1).reshape(1)
    where = jnp.concatenate([chan.reshape(1), side])
    keep, give = forward_parts(where, own, partner, outer, weights)

    got = swapped(give, "chan", 1)
    flips = [4]
    for mask in [1 << k for k in range(depth.bit_length() - 2, 0, -1) if k != 2]:
        own_too = jnp.concatenate([own[None], near], axis=0)
        near = jnp.concatenate([near, swapped(own_too, "space", mask)], axis=0)
        flips = flips + [f ^ mask for f in [0] + flips]
    pre_act = keep[0] + got[0] + out_bias[:, None]
    for j in range(1, groups // 2):
        pre_act = pre_act + swapped(keep[j] + got[j], "chan", 2 * j)
    pre_act, near = barrier((pre_act, near))

    sigmoid = jax.nn.sigmoid(pre_act)
    activated = pre_act * sigmoid
    grad_pre = (
        loss_grad.reshape(chans, cells).astype(F32)
        * sigmoid
        * (1.0 + pre_act * (1.0 - sigmoid))
    ).astype(BF16)

    split = grad_pre.reshape(2, 2, share, cells)
    side = space & 1
    kept = jnp.where(side == 0, split[:, 0], split[:, 1])
    given = jnp.where(side == 0, split[:, 1], split[:, 0])
    pair = jnp.stack([kept, swapped(given, "space", 1)], axis=0)
    pair, near = barrier((pair, near))
    far = swapped(near, "space", 1)
    flips = flips + [f ^ 1 for f in flips]
    side = (space >> 1) & 1
    kept = jnp.where(side == 0, pair[:, 0], pair[:, 1])
    given = jnp.where(side == 0, pair[:, 1], pair[:, 0])
    pieces = [kept]
    for t in range(1, depth // 2):
        pieces.append(swapped(given if t & 1 else kept, "space", 2 * t))

    grads = both_cores(other_chips(grad_pre))
    pieces[0], grads = barrier((pieces[0], grads))
    blocks = other_chips(jnp.concatenate(pieces, axis=0))

    in_grad, to_partner, to_outer = input_parts(where, grads, filters)
    from_partner, from_outer = swapped(to_partner, "space", 1), exchanged(to_outer)
    blocks, far, from_partner, from_outer = barrier((blocks, far, from_partner, from_outer))
    blocks = both_cores(blocks)
    in_grad = in_grad + from_partner.astype(F32) + from_outer.astype(F32)

    index = jnp.concatenate([space.reshape(1), chan.reshape(1), jnp.array(flips, jnp.int32)])
    part = filter_block(index, own, partner, near, far, blocks, factor)
    parts = [part] + [swapped(part, "space", r) for r in range(1, 4)]
    joined, bias = join_blocks((space & 3).reshape(1), parts, share, chans)
    return (
        activated.reshape(chans, planes, cells),
        in_grad.reshape(chans, planes, cells),
        joined,
        bias.reshape(total_out),
    )


def solution(mesh):
    in_specs = (
        P("chan", "space", None),
        P(None, "chan", None),
        P("chan"),
        P("chan", "space", None),
    )
    out_specs = (P("chan", "space", None), P("chan", "space", None), P(None, "chan", None), P())
    return jax.shard_map(body, mesh=mesh, in_specs=in_specs, out_specs=out_specs, check_vma=False)
```

```python
import functools
import math

import jax
import jax.numpy as jnp
from jax import lax
from jax.experimental import pallas as pl
from jax.experimental.pallas import tpu as pltpu
from jax.sharding import PartitionSpec as P

TAPS = 27
PLANE_H = 32
PLANE_W = 32
CELLS = PLANE_H * PLANE_W
CHUNKS = ((0, 8), (8, 16), (16, 24), (24, TAPS))
VMEM = pl.BlockSpec(memory_space=pltpu.VMEM)
SMEM = pl.BlockSpec(memory_space=pltpu.SMEM)
BF16 = jnp.bfloat16
F32 = jnp.float32


def cell_mask(row_off, col_off):
    cell = lax.broadcasted_iota(jnp.int32, (1, CELLS), 1)
    row = cell // PLANE_W + row_off
    col = cell % PLANE_W + col_off
    inside = (row >= 0) & (row < PLANE_H) & (col >= 0) & (col < PLANE_W)
    return jnp.where(inside, 1.0, 0.0).astype(BF16)


def moved(plane, row_off, col_off):
    if row_off == 0 and col_off == 0:
        return plane
    amount = (-(row_off * PLANE_W + col_off)) % CELLS
    return pltpu.roll(plane, amount, 1) * cell_mask(row_off, col_off)


def repeat(count, step):
    if count > 8:
        lax.fori_loop(0, count, lambda q, _: (step(q), 0)[1], 0)
    else:
        for q in range(count):
            step(q)


def forward_kernel(chans, index, own, partner, outer, weights, keep, give, stack, total):
    low = index[1] == 0
    below = jnp.where(low, outer[...], partner[...])
    above = jnp.where(low, partner[...], outer[...])
    for a, cells in enumerate((below, own[...], above)):
        for b in range(3):
            for e in range(3):
                tap = 9 * a + 3 * b + e
                stack[tap * chans : (tap + 1) * chans, :] = moved(cells, b - 1, e - 1)
    total[...] = jnp.dot(weights[...], stack[...], preferred_element_type=F32)
    for j in range(keep.shape[0]):
        start = pl.multiple_of((index[0] ^ (2 * j)) * chans, chans)
        keep[j] = total[pl.ds(start, chans), :]
        start = pl.multiple_of((index[0] ^ (2 * j + 1)) * chans, chans)
        give[j] = total[pl.ds(start, chans), :]


def forward_parts(index, own, partner, outer, weights):
    chans = own.shape[0]
    outs = weights.shape[0]
    side = jax.ShapeDtypeStruct((outs // chans // 2, chans, CELLS), F32)
    return pl.pallas_call(
        functools.partial(forward_kernel, chans),
        out_shape=[side, side],
        in_specs=[SMEM] + [VMEM] * 4,
        out_specs=[VMEM] * 2,
        scratch_shapes=[
            pltpu.VMEM((TAPS * chans, CELLS), BF16),
            pltpu.VMEM((outs, CELLS), F32),
        ],
        compiler_params=pltpu.CompilerParams(vmem_limit_bytes=20 << 20),
        cost_estimate=pl.CostEstimate(
            flops=2 * outs * TAPS * chans * CELLS, bytes_accessed=6 << 20, transcendentals=0
        ),
        name="forward_parts",
    )(index, own, partner, outer, weights)


def input_kernel(chans, groups, index, *refs):
    grads = refs[:groups]
    weights, own, partner, outer, stack, left, total = refs[groups:]
    outs = weights.shape[2]
    for u in range(groups):
        start = pl.multiple_of((index[0] ^ u) * chans, chans)
        cells = grads[u][...]
        for b in range(3):
            for e in range(3):
                stack[3 * b + e, pl.ds(start, chans), :] = moved(cells, 1 - b, 1 - e)
    for a in range(3):
        for k in range(9):
            left[a * chans : (a + 1) * chans, k * outs : (k + 1) * outs] = weights[9 * a + k]
    total[...] = jnp.dot(
        left[...], stack[...].reshape(9 * outs, CELLS), preferred_element_type=F32
    )
    low = index[1] == 0
    below, above = total[:chans], total[2 * chans :]
    own[...] = total[chans : 2 * chans]
    partner[...] = jnp.where(low, above, below).astype(BF16)
    outer[...] = jnp.where(low, below, above).astype(BF16)


def input_parts(index, grads, weights):
    chans = weights.shape[1]
    outs = weights.shape[2]
    groups = len(grads)
    sides = jax.ShapeDtypeStruct((chans, CELLS), BF16)
    return pl.pallas_call(
        functools.partial(input_kernel, chans, groups),
        out_shape=[jax.ShapeDtypeStruct((chans, CELLS), F32), sides, sides],
        in_specs=[SMEM] + [VMEM] * (groups + 1),
        out_specs=[VMEM] * 3,
        scratch_shapes=[
            pltpu.VMEM((9, outs, CELLS), BF16),
            pltpu.VMEM((3 * chans, 9 * outs), BF16),
            pltpu.VMEM((3 * chans, CELLS), F32),
        ],
        compiler_params=pltpu.CompilerParams(vmem_limit_bytes=20 << 20),
        cost_estimate=pl.CostEstimate(
            flops=2 * 3 * chans * 9 * outs * CELLS, bytes_accessed=6 << 20, transcendentals=0
        ),
        name="input_parts",
    )(index, *grads, weights)


def filter_kernel(factor, groups, index, own, partner, near, far, *refs):
    grads = refs[:groups]
    out, shifted, rows, total, sums = refs[groups:]
    planes, share, _ = grads[0].shape
    chans = own.shape[0]
    width = groups * share
    space, chan = index[0], index[1]
    edge = jnp.zeros((3 * chans, CELLS), BF16)
    shifted[0] = edge
    shifted[planes + 1] = edge

    def place(depth, cells):
        for e in range(3):
            shifted[depth + 1, e * chans : (e + 1) * chans, :] = moved(cells, 0, e - 1)

    count = planes // 2 - 1
    place(space, own[...])
    place(space ^ 1, partner[...])
    repeat(count, lambda q: place(space ^ index[2 + q], near[q]))
    repeat(count, lambda q: place(space ^ index[2 + count + q], far[q]))
    ones = jnp.ones((16, CELLS), BF16)
    contract = (((1,), (1,)), ((), ()))
    total[...] = jnp.zeros_like(total)
    sums[...] = jnp.zeros_like(sums)

    def step(q):
        for u in range(groups):
            cells = grads[u][q]
            for b in range(3):
                rows[q & 1, b * groups + (chan ^ u)] = moved(cells, 1 - b, 0)
        right = rows[q & 1].reshape(3 * width, CELLS)
        left = shifted[pl.ds(space ^ q, 3)].reshape(9 * chans, CELLS)
        term = lax.dot_general(left, right, contract, preferred_element_type=F32)
        count = lax.dot_general(
            ones, right[width : 2 * width], contract, preferred_element_type=F32
        )
        total[...] += term
        sums[...] += count

    repeat(planes, step)
    bias = sums[...] * factor
    high = bias.astype(BF16)
    low = (bias - high.astype(F32)).astype(BF16)

    def tile(tap):
        if tap == TAPS:
            rest = jnp.zeros((chans - 32, width), BF16)
            return jnp.concatenate([high, low, rest][: 2 + (chans > 32)], axis=0)
        a, b, e = tap // 9, tap // 3 % 3, tap % 3
        first = (3 * a + e) * chans
        piece = total[first : first + chans, b * width : (b + 1) * width]
        return (piece * factor).astype(BF16)

    for pair in range((TAPS + 1) // 2):
        out[pair * chans : (pair + 1) * chans, :] = jnp.concatenate(
            [tile(2 * pair), tile(2 * pair + 1)], axis=1
        )


def filter_block(index, own, partner, near, far, grads, factor):
    chans = own.shape[0]
    groups = len(grads)
    planes, share, _ = grads[0].shape
    width = groups * share
    return pl.pallas_call(
        functools.partial(filter_kernel, factor, groups),
        out_shape=jax.ShapeDtypeStruct(((TAPS + 1) // 2 * chans, 2 * width), BF16),
        in_specs=[SMEM] + [VMEM] * (4 + groups),
        out_specs=VMEM,
        scratch_shapes=[
            pltpu.VMEM((planes + 2, 3 * chans, CELLS), BF16),
            pltpu.VMEM((2, 3 * groups, share, CELLS), BF16),
            pltpu.VMEM((9 * chans, 3 * width), F32),
            pltpu.VMEM((16, width), F32),
        ],
        compiler_params=pltpu.CompilerParams(vmem_limit_bytes=28 << 20),
        cost_estimate=pl.CostEstimate(
            flops=2 * TAPS * chans * width * planes * CELLS,
            bytes_accessed=8 << 20,
            transcendentals=0,
        ),
        name="filter_block",
    )(index, own, partner, near, far, *grads)


def join_kernel(share, chans, index, *refs):
    blocks, (out, bias, right, held, done) = refs[:4], refs[4:]
    lanes, total = blocks[0].shape[1], out.shape[2]
    width = lanes // 2
    lane = lax.broadcasted_iota(jnp.int32, (lanes, total), 0)
    column = lax.broadcasted_iota(jnp.int32, (lanes, total), 1)
    slot = lane % width
    for odd in range(2):
        for r in range(4):
            home = (slot // share) * (4 * share) + (index[0] ^ r) * share + slot % share
            hit = (column == home) & (lane // width == odd)
            right[r * lanes : (r + 1) * lanes, odd * total : (odd + 1) * total] = jnp.where(
                hit, 1.0, 0.0
            ).astype(BF16)
    copies = []
    for k, (first, last) in enumerate(CHUNKS):
        pairs = range(first // 2, (last + 1) // 2)
        at = slice(pairs[0] * chans, (pairs[-1] + 1) * chans)
        left = jnp.concatenate([block[at, :] for block in blocks], axis=1)
        both = jnp.dot(left, right[...], preferred_element_type=F32)
        for pair in pairs:
            row = (pair - pairs[0]) * chans
            held[2 * pair] = both[row : row + chans, :total]
            if 2 * pair + 1 < TAPS:
                held[2 * pair + 1] = both[row : row + chans, total:]
            else:
                bias[...] = both[row : row + 1, total:] + both[row + 16 : row + 17, total:]
        part = pl.ds(first, last - first)
        copies.append(pltpu.make_async_copy(held.at[part], out.at[part], done.at[k]))
        copies[-1].start()
    for copy in copies:
        copy.wait()


def join_blocks(index, blocks, share, chans):
    lanes = blocks[0].shape[1]
    total = 2 * lanes
    return pl.pallas_call(
        functools.partial(join_kernel, share, chans),
        out_shape=[
            jax.ShapeDtypeStruct((TAPS, chans, total), F32),
            jax.ShapeDtypeStruct((1, total), F32),
        ],
        in_specs=[SMEM] + [VMEM] * 4,
        out_specs=[pl.BlockSpec(memory_space=pl.ANY), VMEM],
        scratch_shapes=[
            pltpu.VMEM((4 * lanes, 2 * total), BF16),
            pltpu.VMEM((TAPS, chans, total), F32),
            pltpu.SemaphoreType.DMA((len(CHUNKS),)),
        ],
        compiler_params=pltpu.CompilerParams(vmem_limit_bytes=20 << 20),
        cost_estimate=pl.CostEstimate(
            flops=4 * TAPS * chans * total * lanes * 2, bytes_accessed=4 << 20, transcendentals=0
        ),
        name="join_blocks",
    )(index, *blocks)


def swapped(value, axis, mask):
    count = lax.axis_size(axis)
    return lax.ppermute(value, axis, [(i, i ^ mask) for i in range(count)])


def exchanged(value):
    pairs = [(i, i + 1) for i in range(1, lax.axis_size("space") - 1, 2)]
    return lax.ppermute(value, "space", pairs + [(j, i) for i, j in pairs])


def other_chips(value):
    found = [value]
    for k in range(1, lax.axis_size("chan").bit_length() - 1):
        found = found + [swapped(v, "chan", 1 << k) for v in found]
    return found


def both_cores(values):
    return [v for value in values for v in (value, swapped(value, "chan", 1))]


def body(features, filters, out_bias, loss_grad):
    chans, planes, cells = features.shape
    total_out = filters.shape[2]
    depth = lax.axis_size("space")
    groups = lax.axis_size("chan")
    space = lax.axis_index("space")
    chan = lax.axis_index("chan")
    share = chans // 4
    factor = 1.0 / math.sqrt(cells * planes * depth)
    barrier = lax.optimization_barrier

    own = features.reshape(chans, cells)
    weights = filters.reshape(TAPS * chans, total_out).T
    partner, outer = swapped(own, "space", 1), exchanged(own)
    outer, partner = barrier((outer, partner))
    side = (space & 1).reshape(1)
    where = jnp.concatenate([chan.reshape(1), side])
    keep, give = forward_parts(where, own, partner, outer, weights)

    got = swapped(give, "chan", 1)
    near = swapped(own, "space", 4)[None]
    flips = [4]
    for mask in [1 << k for k in range(depth.bit_length() - 2, 0, -1) if k != 2]:
        own_too = jnp.concatenate([own[None], near], axis=0)
        near = jnp.concatenate([near, swapped(own_too, "space", mask)], axis=0)
        flips = flips + [f ^ mask for f in [0] + flips]
    pre_act = keep[0] + got[0] + out_bias[:, None]
    for j in range(1, groups // 2):
        pre_act = pre_act + swapped(keep[j] + got[j], "chan", 2 * j)

    sigmoid = jax.nn.sigmoid(pre_act)
    activated = pre_act * sigmoid
    grad_pre = (
        loss_grad.reshape(chans, cells).astype(F32)
        * sigmoid
        * (1.0 + pre_act * (1.0 - sigmoid))
    ).astype(BF16)

    split = grad_pre.reshape(2, 2, share, cells)
    side = space & 1
    kept = jnp.where(side == 0, split[:, 0], split[:, 1])
    given = jnp.where(side == 0, split[:, 1], split[:, 0])
    given, grad_pre = barrier((given, grad_pre))
    pair = jnp.stack([kept, swapped(given, "space", 1)], axis=0)
    pair, near = barrier((pair, near))
    far = swapped(near, "space", 1)
    flips = flips + [f ^ 1 for f in flips]
    side = (space >> 1) & 1
    kept = jnp.where(side == 0, pair[:, 0], pair[:, 1])
    given = jnp.where(side == 0, pair[:, 1], pair[:, 0])
    pieces = [kept]
    for t in range(1, depth // 2):
        pieces.append(swapped(given if t & 1 else kept, "space", 2 * t))

    grads = both_cores(other_chips(grad_pre))
    pieces[0], grads = barrier((pieces[0], grads))
    blocks = other_chips(jnp.concatenate(pieces, axis=0))

    in_grad, to_partner, to_outer = input_parts(where, grads, filters)
    from_partner, from_outer = swapped(to_partner, "space", 1), exchanged(to_outer)
    blocks, far, from_partner, from_outer = barrier((blocks, far, from_partner, from_outer))
    blocks = both_cores(blocks)
    in_grad = in_grad + from_partner.astype(F32) + from_outer.astype(F32)

    index = jnp.concatenate([space.reshape(1), chan.reshape(1), jnp.array(flips, jnp.int32)])
    part = filter_block(index, own, partner, near, far, blocks, factor)
    parts = [part] + [swapped(part, "space", r) for r in range(1, 4)]
    joined, bias = join_blocks((space & 3).reshape(1), parts, share, chans)
    return (
        activated.reshape(chans, planes, cells),
        in_grad.reshape(chans, planes, cells),
        joined,
        bias.reshape(total_out),
    )


def solution(mesh):
    in_specs = (
        P("chan", "space", None),
        P(None, "chan", None),
        P("chan"),
        P("chan", "space", None),
    )
    out_specs = (P("chan", "space", None), P("chan", "space", None), P(None, "chan", None), P())
    return jax.shard_map(body, mesh=mesh, in_specs=in_specs, out_specs=out_specs, check_vma=False)
```

```python
import functools
import math

import jax
import jax.numpy as jnp
from jax import lax
from jax.experimental import pallas as pl
from jax.experimental.pallas import tpu as pltpu
from jax.sharding import PartitionSpec as P

TAPS = 27
PLANE_H = 32
PLANE_W = 32
CELLS = PLANE_H * PLANE_W
CHUNKS = ((0, 8), (8, 16), (16, 24), (24, TAPS))
VMEM = pl.BlockSpec(memory_space=pltpu.VMEM)
SMEM = pl.BlockSpec(memory_space=pltpu.SMEM)
BF16 = jnp.bfloat16
F32 = jnp.float32


def cell_mask(row_off, col_off):
    cell = lax.broadcasted_iota(jnp.int32, (1, CELLS), 1)
    row = cell // PLANE_W + row_off
    col = cell % PLANE_W + col_off
    inside = (row >= 0) & (row < PLANE_H) & (col >= 0) & (col < PLANE_W)
    return jnp.where(inside, 1.0, 0.0).astype(BF16)


def moved(plane, row_off, col_off):
    if row_off == 0 and col_off == 0:
        return plane
    amount = (-(row_off * PLANE_W + col_off)) % CELLS
    return pltpu.roll(plane, amount, 1) * cell_mask(row_off, col_off)


def repeat(count, step):
    if count > 8:
        lax.fori_loop(0, count, lambda q, _: (step(q), 0)[1], 0)
    else:
        for q in range(count):
            step(q)


def forward_kernel(chans, index, own, partner, outer, weights, keep, give, stack, total):
    def place(a, plane):
        cells = plane[...]
        for b in range(3):
            for e in range(3):
                tap = 9 * a + 3 * b + e
                stack[tap * chans : (tap + 1) * chans, :] = moved(cells, b - 1, e - 1)

    place(1, own)

    @pl.when(index[1] == 0)
    def _():
        place(0, outer)
        place(2, partner)

    @pl.when(index[1] != 0)
    def _():
        place(0, partner)
        place(2, outer)

    total[...] = jnp.dot(weights[...], stack[...], preferred_element_type=F32)
    for j in range(keep.shape[0]):
        start = pl.multiple_of((index[0] ^ (2 * j)) * chans, chans)
        keep[j] = total[pl.ds(start, chans), :]
        start = pl.multiple_of((index[0] ^ (2 * j + 1)) * chans, chans)
        give[j] = total[pl.ds(start, chans), :]


def forward_parts(index, own, partner, outer, weights):
    chans = own.shape[0]
    outs = weights.shape[0]
    side = jax.ShapeDtypeStruct((outs // chans // 2, chans, CELLS), F32)
    return pl.pallas_call(
        functools.partial(forward_kernel, chans),
        out_shape=[side, side],
        in_specs=[SMEM] + [VMEM] * 4,
        out_specs=[VMEM] * 2,
        scratch_shapes=[
            pltpu.VMEM((TAPS * chans, CELLS), BF16),
            pltpu.VMEM((outs, CELLS), F32),
        ],
        compiler_params=pltpu.CompilerParams(vmem_limit_bytes=20 << 20),
        cost_estimate=pl.CostEstimate(
            flops=2 * outs * TAPS * chans * CELLS, bytes_accessed=6 << 20, transcendentals=0
        ),
        name="forward_parts",
    )(index, own, partner, outer, weights)


def input_kernel(chans, chips, index, *refs):
    grads = refs[:chips]
    weights, own, partner, outer, stack, left, total = refs[chips:]
    outs = weights.shape[2]
    for u in range(2 * chips):
        start = pl.multiple_of((index[0] ^ u) * chans, chans)
        cells = grads[u // 2][u % 2]
        for b in range(3):
            for e in range(3):
                stack[3 * b + e, pl.ds(start, chans), :] = moved(cells, 1 - b, 1 - e)
    for a in range(3):
        for k in range(9):
            left[a * chans : (a + 1) * chans, k * outs : (k + 1) * outs] = weights[9 * a + k]
    total[...] = jnp.dot(
        left[...], stack[...].reshape(9 * outs, CELLS), preferred_element_type=F32
    )
    own[...] = total[chans : 2 * chans]

    @pl.when(index[1] == 0)
    def _():
        partner[...] = total[2 * chans :].astype(BF16)
        outer[...] = total[:chans].astype(BF16)

    @pl.when(index[1] != 0)
    def _():
        partner[...] = total[:chans].astype(BF16)
        outer[...] = total[2 * chans :].astype(BF16)


def input_parts(index, grads, weights):
    chans = weights.shape[1]
    outs = weights.shape[2]
    chips = len(grads)
    sides = jax.ShapeDtypeStruct((chans, CELLS), BF16)
    return pl.pallas_call(
        functools.partial(input_kernel, chans, chips),
        out_shape=[jax.ShapeDtypeStruct((chans, CELLS), F32), sides, sides],
        in_specs=[SMEM] + [VMEM] * (chips + 1),
        out_specs=[VMEM] * 3,
        scratch_shapes=[
            pltpu.VMEM((9, outs, CELLS), BF16),
            pltpu.VMEM((3 * chans, 9 * outs), BF16),
            pltpu.VMEM((3 * chans, CELLS), F32),
        ],
        compiler_params=pltpu.CompilerParams(vmem_limit_bytes=20 << 20),
        cost_estimate=pl.CostEstimate(
            flops=2 * 3 * chans * 9 * outs * CELLS, bytes_accessed=6 << 20, transcendentals=0
        ),
        name="input_parts",
    )(index, *grads, weights)


def filter_kernel(factor, groups, index, own, partner, near, far, *refs):
    grads = refs[:groups]
    out, shifted, rows, total, sums = refs[groups:]
    planes, share, _ = grads[0].shape
    chans = own.shape[0]
    width = groups * share
    space, chan = index[0], index[1]
    edge = jnp.zeros((3 * chans, CELLS), BF16)
    shifted[0] = edge
    shifted[planes + 1] = edge

    def place(depth, cells):
        for e in range(3):
            shifted[depth + 1, e * chans : (e + 1) * chans, :] = moved(cells, 0, e - 1)

    count = planes // 2 - 1
    place(space, own[...])
    place(space ^ 1, partner[...])
    repeat(count, lambda q: place(space ^ index[2 + q], near[q]))
    repeat(count, lambda q: place(space ^ index[2 + count + q], far[q]))
    ones = jnp.ones((16, CELLS), BF16)
    contract = (((1,), (1,)), ((), ()))
    total[...] = jnp.zeros_like(total)
    sums[...] = jnp.zeros_like(sums)

    def step(q):
        for u in range(groups):
            cells = grads[u][q]
            for b in range(3):
                rows[q & 1, b * groups + (chan ^ u)] = moved(cells, 1 - b, 0)
        right = rows[q & 1].reshape(3 * width, CELLS)
        left = shifted[pl.ds(space ^ q, 3)].reshape(9 * chans, CELLS)
        term = lax.dot_general(left, right, contract, preferred_element_type=F32)
        count = lax.dot_general(
            ones, right[width : 2 * width], contract, preferred_element_type=F32
        )
        total[...] += term
        sums[...] += count

    repeat(planes, step)
    bias = sums[...] * factor
    high = bias.astype(BF16)
    low = (bias - high.astype(F32)).astype(BF16)

    def tile(tap):
        if tap == TAPS:
            rest = jnp.zeros((chans - 32, width), BF16)
            return jnp.concatenate([high, low, rest][: 2 + (chans > 32)], axis=0)
        a, b, e = tap // 9, tap // 3 % 3, tap % 3
        first = (3 * a + e) * chans
        piece = total[first : first + chans, b * width : (b + 1) * width]
        return (piece * factor).astype(BF16)

    for pair in range((TAPS + 1) // 2):
        out[pair * chans : (pair + 1) * chans, :] = jnp.concatenate(
            [tile(2 * pair), tile(2 * pair + 1)], axis=1
        )


def filter_block(index, own, partner, near, far, grads, factor):
    chans = own.shape[0]
    groups = len(grads)
    planes, share, _ = grads[0].shape
    width = groups * share
    return pl.pallas_call(
        functools.partial(filter_kernel, factor, groups),
        out_shape=jax.ShapeDtypeStruct(((TAPS + 1) // 2 * chans, 2 * width), BF16),
        in_specs=[SMEM] + [VMEM] * (4 + groups),
        out_specs=VMEM,
        scratch_shapes=[
            pltpu.VMEM((planes + 2, 3 * chans, CELLS), BF16),
            pltpu.VMEM((2, 3 * groups, share, CELLS), BF16),
            pltpu.VMEM((9 * chans, 3 * width), F32),
            pltpu.VMEM((16, width), F32),
        ],
        compiler_params=pltpu.CompilerParams(vmem_limit_bytes=28 << 20),
        cost_estimate=pl.CostEstimate(
            flops=2 * TAPS * chans * width * planes * CELLS,
            bytes_accessed=8 << 20,
            transcendentals=0,
        ),
        name="filter_block",
    )(index, own, partner, near, far, *grads)


def join_kernel(share, chans, index, *refs):
    blocks, (out, bias, right, held, done) = refs[:4], refs[4:]
    lanes, total = blocks[0].shape[1], out.shape[2]
    width = lanes // 2
    lane = lax.broadcasted_iota(jnp.int32, (lanes, total), 0)
    column = lax.broadcasted_iota(jnp.int32, (lanes, total), 1)
    slot = lane % width
    for odd in range(2):
        for r in range(4):
            home = (slot // share) * (4 * share) + (index[0] ^ r) * share + slot % share
            hit = (column == home) & (lane // width == odd)
            right[r * lanes : (r + 1) * lanes, odd * total : (odd + 1) * total] = jnp.where(
                hit, 1.0, 0.0
            ).astype(BF16)
    copies = []
    for k, (first, last) in enumerate(CHUNKS):
        pairs = range(first // 2, (last + 1) // 2)
        at = slice(pairs[0] * chans, (pairs[-1] + 1) * chans)
        left = jnp.concatenate([block[at, :] for block in blocks], axis=1)
        both = jnp.dot(left, right[...], preferred_element_type=F32)
        for pair in pairs:
            row = (pair - pairs[0]) * chans
            held[2 * pair] = both[row : row + chans, :total]
            if 2 * pair + 1 < TAPS:
                held[2 * pair + 1] = both[row : row + chans, total:]
            else:
                bias[...] = both[row : row + 1, total:] + both[row + 16 : row + 17, total:]
        part = pl.ds(first, last - first)
        copies.append(pltpu.make_async_copy(held.at[part], out.at[part], done.at[k]))
        copies[-1].start()
    for copy in copies:
        copy.wait()


def join_blocks(index, blocks, share, chans):
    lanes = blocks[0].shape[1]
    total = 2 * lanes
    return pl.pallas_call(
        functools.partial(join_kernel, share, chans),
        out_shape=[
            jax.ShapeDtypeStruct((TAPS, chans, total), F32),
            jax.ShapeDtypeStruct((1, total), F32),
        ],
        in_specs=[SMEM] + [VMEM] * 4,
        out_specs=[pl.BlockSpec(memory_space=pl.ANY), VMEM],
        scratch_shapes=[
            pltpu.VMEM((4 * lanes, 2 * total), BF16),
            pltpu.VMEM((TAPS, chans, total), F32),
            pltpu.SemaphoreType.DMA((len(CHUNKS),)),
        ],
        compiler_params=pltpu.CompilerParams(vmem_limit_bytes=20 << 20),
        cost_estimate=pl.CostEstimate(
            flops=4 * TAPS * chans * total * lanes * 2, bytes_accessed=4 << 20, transcendentals=0
        ),
        name="join_blocks",
    )(index, *blocks)


def swapped(value, axis, mask):
    count = lax.axis_size(axis)
    return lax.ppermute(value, axis, [(i, i ^ mask) for i in range(count)])


def exchanged(value):
    pairs = [(i, i + 1) for i in range(1, lax.axis_size("space") - 1, 2)]
    return lax.ppermute(value, "space", pairs + [(j, i) for i, j in pairs])


def other_chips(value):
    found = [value]
    for k in range(1, lax.axis_size("chan").bit_length() - 1):
        found = found + [swapped(v, "chan", 1 << k) for v in found]
    return found


def both_cores(values):
    return [v for value in values for v in (value, swapped(value, "chan", 1))]


def body(features, filters, out_bias, loss_grad):
    chans, planes, cells = features.shape
    total_out = filters.shape[2]
    depth = lax.axis_size("space")
    groups = lax.axis_size("chan")
    space = lax.axis_index("space")
    chan = lax.axis_index("chan")
    share = chans // 4
    factor = 1.0 / math.sqrt(cells * planes * depth)
    barrier = lax.optimization_barrier

    own = features.reshape(chans, cells)
    weights = filters.reshape(TAPS * chans, total_out).T
    partner, outer = swapped(own, "space", 1), exchanged(own)
    outer, partner = barrier((outer, partner))
    side = (space & 1).reshape(1)
    where = jnp.concatenate([chan.reshape(1), side])
    keep, give = forward_parts(where, own, partner, outer, weights)

    got = swapped(give, "chan", 1)
    near = [swapped(own, "space", 4), swapped(own, "space", 2)]
    pre_act = keep[0] + got[0] + out_bias[:, None]
    for j in range(1, groups // 2):
        pre_act = pre_act + swapped(keep[j] + got[j], "chan", 2 * j)

    pre_act, near = barrier((pre_act, near))
    near = jnp.stack(near + [swapped(near[0], "space", 2)], axis=0)
    flips = [4, 2, 6]
    for mask in [1 << k for k in range(3, depth.bit_length() - 1)]:
        own_too = jnp.concatenate([own[None], near], axis=0)
        near = jnp.concatenate([near, swapped(own_too, "space", mask)], axis=0)
        flips = flips + [f ^ mask for f in [0] + flips]

    sigmoid = jax.nn.sigmoid(pre_act)
    activated = pre_act * sigmoid
    grad_pre = (
        loss_grad.reshape(chans, cells).astype(F32)
        * sigmoid
        * (1.0 + pre_act * (1.0 - sigmoid))
    ).astype(BF16)

    split = grad_pre.reshape(2, 2, share, cells)
    side = space & 1
    kept = jnp.where(side == 0, split[:, 0], split[:, 1])
    given = jnp.where(side == 0, split[:, 1], split[:, 0])
    given, grad_pre = barrier((given, grad_pre))
    pair = jnp.stack([kept, swapped(given, "space", 1)], axis=0)
    far = swapped(near, "space", 1)
    flips = flips + [f ^ 1 for f in flips]
    side = (space >> 1) & 1
    kept = jnp.where(side == 0, pair[:, 0], pair[:, 1])
    given = jnp.where(side == 0, pair[:, 1], pair[:, 0])
    pieces = [kept]
    for t in range(1, depth // 2):
        pieces.append(swapped(given if t & 1 else kept, "space", 2 * t))

    grads = other_chips(jnp.stack([grad_pre, swapped(grad_pre, "chan", 1)], axis=0))
    pieces[0], grads = barrier((pieces[0], grads))
    blocks = other_chips(jnp.concatenate(pieces, axis=0))

    in_grad, to_partner, to_outer = input_parts(where, grads, filters)
    from_partner, from_outer = swapped(to_partner, "space", 1), exchanged(to_outer)
    blocks, far, from_partner, from_outer = barrier((blocks, far, from_partner, from_outer))
    blocks = both_cores(blocks)
    in_grad = in_grad + from_partner.astype(F32) + from_outer.astype(F32)

    index = jnp.concatenate([space.reshape(1), chan.reshape(1), jnp.array(flips, jnp.int32)])
    part = filter_block(index, own, partner, near, far, blocks, factor)
    parts = [part] + [swapped(part, "space", r) for r in range(1, 4)]
    joined, bias = join_blocks((space & 3).reshape(1), parts, share, chans)
    return (
        activated.reshape(chans, planes, cells),
        in_grad.reshape(chans, planes, cells),
        joined,
        bias.reshape(total_out),
    )


def solution(mesh):
    in_specs = (
        P("chan", "space", None),
        P(None, "chan", None),
        P("chan"),
        P("chan", "space", None),
    )
    out_specs = (P("chan", "space", None), P("chan", "space", None), P(None, "chan", None), P())
    return jax.shard_map(body, mesh=mesh, in_specs=in_specs, out_specs=out_specs, check_vma=False)
```

```python
import functools
import math

import jax
import jax.numpy as jnp
from jax import lax
from jax.experimental import pallas as pl
from jax.experimental.pallas import tpu as pltpu
from jax.sharding import PartitionSpec as P

TAPS = 27
PLANE_H = 32
PLANE_W = 32
CELLS = PLANE_H * PLANE_W
CHUNKS = ((0, 8), (8, 16), (16, 24), (24, TAPS))
VMEM = pl.BlockSpec(memory_space=pltpu.VMEM)
SMEM = pl.BlockSpec(memory_space=pltpu.SMEM)
BF16 = jnp.bfloat16
F32 = jnp.float32


def cell_mask(row_off, col_off):
    cell = lax.broadcasted_iota(jnp.int32, (1, CELLS), 1)
    row = cell // PLANE_W + row_off
    col = cell % PLANE_W + col_off
    inside = (row >= 0) & (row < PLANE_H) & (col >= 0) & (col < PLANE_W)
    return jnp.where(inside, 1.0, 0.0).astype(BF16)


def moved(plane, row_off, col_off):
    if row_off == 0 and col_off == 0:
        return plane
    amount = (-(row_off * PLANE_W + col_off)) % CELLS
    return pltpu.roll(plane, amount, 1) * cell_mask(row_off, col_off)


def repeat(count, step):
    if count > 8:
        lax.fori_loop(0, count, lambda q, _: (step(q), 0)[1], 0)
    else:
        for q in range(count):
            step(q)


def forward_kernel(chans, index, own, partner, outer, weights, keep, give, stack, total):
    for k, plane in enumerate((own, partner, outer)):
        cells = plane[...]
        for b in range(3):
            for e in range(3):
                start = (9 * k + 3 * b + e) * chans
                stack[start : start + chans, :] = moved(cells, b - 1, e - 1)
    total[...] = jnp.dot(weights[...], stack[...], preferred_element_type=F32)
    for j in range(keep.shape[0]):
        start = pl.multiple_of((index[0] ^ (2 * j)) * chans, chans)
        keep[j] = total[pl.ds(start, chans), :]
        start = pl.multiple_of((index[0] ^ (2 * j + 1)) * chans, chans)
        give[j] = total[pl.ds(start, chans), :]


def forward_parts(index, own, partner, outer, weights):
    chans = own.shape[0]
    outs = weights.shape[0]
    side = jax.ShapeDtypeStruct((outs // chans // 2, chans, CELLS), F32)
    return pl.pallas_call(
        functools.partial(forward_kernel, chans),
        out_shape=[side, side],
        in_specs=[SMEM] + [VMEM] * 4,
        out_specs=[VMEM] * 2,
        scratch_shapes=[
            pltpu.VMEM((TAPS * chans, CELLS), BF16),
            pltpu.VMEM((outs, CELLS), F32),
        ],
        compiler_params=pltpu.CompilerParams(vmem_limit_bytes=20 << 20),
        cost_estimate=pl.CostEstimate(
            flops=2 * outs * TAPS * chans * CELLS, bytes_accessed=6 << 20, transcendentals=0
        ),
        name="forward_parts",
    )(index, own, partner, outer, weights)


def input_kernel(chans, chips, index, *refs):
    grads = refs[:chips]
    weights, own, partner, outer, stack, left = refs[chips:]
    outs = weights.shape[2]
    for u in range(2 * chips):
        start = pl.multiple_of((index[0] ^ u) * chans, chans)
        cells = grads[u // 2][u % 2]
        for b in range(3):
            for e in range(3):
                stack[3 * b + e, pl.ds(start, chans), :] = moved(cells, 1 - b, 1 - e)
    for row, a in enumerate((1, 2 * (1 - index[1]), 2 * index[1])):
        for k in range(9):
            left[row * chans : (row + 1) * chans, k * outs : (k + 1) * outs] = weights[9 * a + k]
    total = jnp.dot(
        left[...], stack[...].reshape(9 * outs, CELLS), preferred_element_type=F32
    )
    own[...] = total[:chans]
    partner[...] = total[chans : 2 * chans].astype(BF16)
    outer[...] = total[2 * chans :].astype(BF16)


def input_parts(index, grads, weights):
    chans = weights.shape[1]
    outs = weights.shape[2]
    chips = len(grads)
    sides = jax.ShapeDtypeStruct((chans, CELLS), BF16)
    return pl.pallas_call(
        functools.partial(input_kernel, chans, chips),
        out_shape=[jax.ShapeDtypeStruct((chans, CELLS), F32), sides, sides],
        in_specs=[SMEM] + [VMEM] * (chips + 1),
        out_specs=[VMEM] * 3,
        scratch_shapes=[
            pltpu.VMEM((9, outs, CELLS), BF16),
            pltpu.VMEM((3 * chans, 9 * outs), BF16),
        ],
        compiler_params=pltpu.CompilerParams(vmem_limit_bytes=20 << 20),
        cost_estimate=pl.CostEstimate(
            flops=2 * 3 * chans * 9 * outs * CELLS, bytes_accessed=6 << 20, transcendentals=0
        ),
        name="input_parts",
    )(index, *grads, weights)


def filter_kernel(factor, groups, index, own, partner, near, far, *refs):
    grads = refs[:groups]
    out, shifted, rows, total, sums = refs[groups:]
    planes, share, _ = grads[0].shape
    chans = own.shape[0]
    width = groups * share
    space, chan = index[0], index[1]
    edge = jnp.zeros((3 * chans, CELLS), BF16)
    shifted[0] = edge
    shifted[planes + 1] = edge

    def place(depth, cells):
        for e in range(3):
            shifted[depth + 1, e * chans : (e + 1) * chans, :] = moved(cells, 0, e - 1)

    count = planes // 2 - 1
    place(space, own[...])
    place(space ^ 1, partner[...])
    repeat(count, lambda q: place(space ^ index[2 + q], near[q]))
    repeat(count, lambda q: place(space ^ index[2 + count + q], far[q]))
    ones = jnp.ones((16, CELLS), BF16)
    contract = (((1,), (1,)), ((), ()))
    total[...] = jnp.zeros_like(total)
    sums[...] = jnp.zeros_like(sums)

    def step(q):
        for u in range(groups):
            cells = grads[u][q]
            for b in range(3):
                rows[q & 1, b * groups + (chan ^ u)] = moved(cells, 1 - b, 0)
        right = rows[q & 1].reshape(3 * width, CELLS)
        left = shifted[pl.ds(space ^ q, 3)].reshape(9 * chans, CELLS)
        term = lax.dot_general(left, right, contract, preferred_element_type=F32)
        count = lax.dot_general(
            ones, right[width : 2 * width], contract, preferred_element_type=F32
        )
        total[...] += term
        sums[...] += count

    repeat(planes, step)
    bias = sums[...] * factor
    high = bias.astype(BF16)
    low = (bias - high.astype(F32)).astype(BF16)

    def tile(tap):
        if tap == TAPS:
            rest = jnp.zeros((chans - 32, width), BF16)
            return jnp.concatenate([high, low, rest][: 2 + (chans > 32)], axis=0)
        a, b, e = tap // 9, tap // 3 % 3, tap % 3
        first = (3 * a + e) * chans
        piece = total[first : first + chans, b * width : (b + 1) * width]
        return (piece * factor).astype(BF16)

    for pair in range((TAPS + 1) // 2):
        out[pair * chans : (pair + 1) * chans, :] = jnp.concatenate(
            [tile(2 * pair), tile(2 * pair + 1)], axis=1
        )


def filter_block(index, own, partner, near, far, grads, factor):
    chans = own.shape[0]
    groups = len(grads)
    planes, share, _ = grads[0].shape
    width = groups * share
    return pl.pallas_call(
        functools.partial(filter_kernel, factor, groups),
        out_shape=jax.ShapeDtypeStruct(((TAPS + 1) // 2 * chans, 2 * width), BF16),
        in_specs=[SMEM] + [VMEM] * (4 + groups),
        out_specs=VMEM,
        scratch_shapes=[
            pltpu.VMEM((planes + 2, 3 * chans, CELLS), BF16),
            pltpu.VMEM((2, 3 * groups, share, CELLS), BF16),
            pltpu.VMEM((9 * chans, 3 * width), F32),
            pltpu.VMEM((16, width), F32),
        ],
        compiler_params=pltpu.CompilerParams(vmem_limit_bytes=28 << 20),
        cost_estimate=pl.CostEstimate(
            flops=2 * TAPS * chans * width * planes * CELLS,
            bytes_accessed=8 << 20,
            transcendentals=0,
        ),
        name="filter_block",
    )(index, own, partner, near, far, *grads)


def join_kernel(share, chans, index, *refs):
    blocks, (out, bias, right, held, done) = refs[:4], refs[4:]
    lanes, total = blocks[0].shape[1], out.shape[2]
    width = lanes // 2
    lane = lax.broadcasted_iota(jnp.int32, (lanes, total), 0)
    column = lax.broadcasted_iota(jnp.int32, (lanes, total), 1)
    slot = lane % width
    for odd in range(2):
        for r in range(4):
            home = (slot // share) * (4 * share) + (index[0] ^ r) * share + slot % share
            hit = (column == home) & (lane // width == odd)
            right[r * lanes : (r + 1) * lanes, odd * total : (odd + 1) * total] = jnp.where(
                hit, 1.0, 0.0
            ).astype(BF16)
    copies = []
    for k, (first, last) in enumerate(CHUNKS):
        pairs = range(first // 2, (last + 1) // 2)
        at = slice(pairs[0] * chans, (pairs[-1] + 1) * chans)
        left = jnp.concatenate([block[at, :] for block in blocks], axis=1)
        both = jnp.dot(left, right[...], preferred_element_type=F32)
        for pair in pairs:
            row = (pair - pairs[0]) * chans
            held[2 * pair] = both[row : row + chans, :total]
            if 2 * pair + 1 < TAPS:
                held[2 * pair + 1] = both[row : row + chans, total:]
            else:
                bias[...] = both[row : row + 1, total:] + both[row + 16 : row + 17, total:]
        part = pl.ds(first, last - first)
        copies.append(pltpu.make_async_copy(held.at[part], out.at[part], done.at[k]))
        copies[-1].start()
    for copy in copies:
        copy.wait()


def join_blocks(index, blocks, share, chans):
    lanes = blocks[0].shape[1]
    total = 2 * lanes
    return pl.pallas_call(
        functools.partial(join_kernel, share, chans),
        out_shape=[
            jax.ShapeDtypeStruct((TAPS, chans, total), F32),
            jax.ShapeDtypeStruct((1, total), F32),
        ],
        in_specs=[SMEM] + [VMEM] * 4,
        out_specs=[pl.BlockSpec(memory_space=pl.ANY), VMEM],
        scratch_shapes=[
            pltpu.VMEM((4 * lanes, 2 * total), BF16),
            pltpu.VMEM((TAPS, chans, total), F32),
            pltpu.SemaphoreType.DMA((len(CHUNKS),)),
        ],
        compiler_params=pltpu.CompilerParams(vmem_limit_bytes=20 << 20),
        cost_estimate=pl.CostEstimate(
            flops=4 * TAPS * chans * total * lanes * 2, bytes_accessed=4 << 20, transcendentals=0
        ),
        name="join_blocks",
    )(index, *blocks)


def swapped(value, axis, mask):
    count = lax.axis_size(axis)
    return lax.ppermute(value, axis, [(i, i ^ mask) for i in range(count)])


def exchanged(value):
    pairs = [(i, i + 1) for i in range(1, lax.axis_size("space") - 1, 2)]
    return lax.ppermute(value, "space", pairs + [(j, i) for i, j in pairs])


def other_chips(value):
    found = [value]
    for k in range(1, lax.axis_size("chan").bit_length() - 1):
        found = found + [swapped(v, "chan", 1 << k) for v in found]
    return found


def both_cores(values):
    return [v for value in values for v in (value, swapped(value, "chan", 1))]


def body(features, filters, out_bias, loss_grad):
    chans, planes, cells = features.shape
    total_out = filters.shape[2]
    depth = lax.axis_size("space")
    groups = lax.axis_size("chan")
    space = lax.axis_index("space")
    chan = lax.axis_index("chan")
    share = chans // 4
    factor = 1.0 / math.sqrt(cells * planes * depth)
    barrier = lax.optimization_barrier

    own = features.reshape(chans, cells)
    partner, outer = swapped(own, "space", 1), exchanged(own)
    outer, partner = barrier((outer, partner))
    side = space & 1
    where = jnp.stack([chan, side])
    slabs = filters.reshape(3, 9 * chans, total_out)
    weights = jnp.concatenate(
        [slabs[1], slabs[2 * (1 - side)], slabs[2 * side]], axis=0
    ).T
    keep, give = forward_parts(where, own, partner, outer, weights)

    got = swapped(give, "chan", 1)
    near = [swapped(own, "space", 4), swapped(own, "space", 2)]
    pre_act = keep[0] + got[0] + out_bias[:, None]
    for j in range(1, groups // 2):
        pre_act = pre_act + swapped(keep[j] + got[j], "chan", 2 * j)

    pre_act, near = barrier((pre_act, near))
    near = jnp.stack(near + [swapped(near[0], "space", 2)], axis=0)
    flips = [4, 2, 6]
    for mask in [1 << k for k in range(3, depth.bit_length() - 1)]:
        own_too = jnp.concatenate([own[None], near], axis=0)
        near = jnp.concatenate([near, swapped(own_too, "space", mask)], axis=0)
        flips = flips + [f ^ mask for f in [0] + flips]

    sigmoid = jax.nn.sigmoid(pre_act)
    activated = pre_act * sigmoid
    grad_pre = (
        loss_grad.reshape(chans, cells).astype(F32)
        * sigmoid
        * (1.0 + pre_act * (1.0 - sigmoid))
    ).astype(BF16)

    split = grad_pre.reshape(2, 2, share, cells)
    side = space & 1
    kept = jnp.where(side == 0, split[:, 0], split[:, 1])
    given = jnp.where(side == 0, split[:, 1], split[:, 0])
    given, grad_pre = barrier((given, grad_pre))
    pair = jnp.stack([kept, swapped(given, "space", 1)], axis=0)
    far = swapped(near, "space", 1)
    flips = flips + [f ^ 1 for f in flips]
    side = (space >> 1) & 1
    kept = jnp.where(side == 0, pair[:, 0], pair[:, 1])
    given = jnp.where(side == 0, pair[:, 1], pair[:, 0])
    pieces = [kept]
    for t in range(1, depth // 2):
        pieces.append(swapped(given if t & 1 else kept, "space", 2 * t))

    grads = other_chips(jnp.stack([grad_pre, swapped(grad_pre, "chan", 1)], axis=0))
    in_grad, to_partner, to_outer = input_parts(where, grads, filters)
    pieces[0], to_partner, to_outer = barrier((pieces[0], to_partner, to_outer))
    blocks = other_chips(jnp.concatenate(pieces, axis=0))
    from_partner, from_outer = swapped(to_partner, "space", 1), exchanged(to_outer)
    blocks, far, from_partner, from_outer = barrier((blocks, far, from_partner, from_outer))
    blocks = both_cores(blocks)
    in_grad = in_grad + from_partner.astype(F32) + from_outer.astype(F32)

    index = jnp.concatenate([space.reshape(1), chan.reshape(1), jnp.array(flips, jnp.int32)])
    part = filter_block(index, own, partner, near, far, blocks, factor)
    parts = [part] + [swapped(part, "space", r) for r in range(1, 4)]
    joined, bias = join_blocks((space & 3).reshape(1), parts, share, chans)
    return (
        activated.reshape(chans, planes, cells),
        in_grad.reshape(chans, planes, cells),
        joined,
        bias.reshape(total_out),
    )


def solution(mesh):
    in_specs = (
        P("chan", "space", None),
        P(None, "chan", None),
        P("chan"),
        P("chan", "space", None),
    )
    out_specs = (P("chan", "space", None), P("chan", "space", None), P(None, "chan", None), P())
    return jax.shard_map(body, mesh=mesh, in_specs=in_specs, out_specs=out_specs, check_vma=False)
```

```python
import functools
import math

import jax
import jax.numpy as jnp
from jax import lax
from jax.experimental import pallas as pl
from jax.experimental.pallas import tpu as pltpu
from jax.sharding import PartitionSpec as P

TAPS = 27
PLANE_H = 32
PLANE_W = 32
CELLS = PLANE_H * PLANE_W
CHUNKS = ((0, 8), (8, 16), (16, 24), (24, TAPS))
VMEM = pl.BlockSpec(memory_space=pltpu.VMEM)
SMEM = pl.BlockSpec(memory_space=pltpu.SMEM)
BF16 = jnp.bfloat16
F32 = jnp.float32


def cell_mask(row_off, col_off):
    cell = lax.broadcasted_iota(jnp.int32, (1, CELLS), 1)
    row = cell // PLANE_W + row_off
    col = cell % PLANE_W + col_off
    inside = (row >= 0) & (row < PLANE_H) & (col >= 0) & (col < PLANE_W)
    return jnp.where(inside, 1.0, 0.0).astype(BF16)


def moved(plane, row_off, col_off):
    if row_off == 0 and col_off == 0:
        return plane
    amount = (-(row_off * PLANE_W + col_off)) % CELLS
    return pltpu.roll(plane, amount, 1) * cell_mask(row_off, col_off)


def repeat(count, step):
    if count > 8:
        lax.fori_loop(0, count, lambda q, _: (step(q), 0)[1], 0)
    else:
        for q in range(count):
            step(q)


def forward_kernel(chans, index, own, partner, outer, weights, keep, give, stack, total):
    for k, plane in enumerate((own, partner, outer)):
        cells = plane[...]
        for b in range(3):
            for e in range(3):
                start = (9 * k + 3 * b + e) * chans
                stack[start : start + chans, :] = moved(cells, b - 1, e - 1)
    total[...] = jnp.dot(weights[...], stack[...], preferred_element_type=F32)
    for j in range(keep.shape[0]):
        start = pl.multiple_of((index[0] ^ (2 * j)) * chans, chans)
        keep[j] = total[pl.ds(start, chans), :]
        start = pl.multiple_of((index[0] ^ (2 * j + 1)) * chans, chans)
        give[j] = total[pl.ds(start, chans), :]


def forward_parts(index, own, partner, outer, weights):
    chans = own.shape[0]
    outs = weights.shape[0]
    side = jax.ShapeDtypeStruct((outs // chans // 2, chans, CELLS), F32)
    return pl.pallas_call(
        functools.partial(forward_kernel, chans),
        out_shape=[side, side],
        in_specs=[SMEM] + [VMEM] * 4,
        out_specs=[VMEM] * 2,
        scratch_shapes=[
            pltpu.VMEM((TAPS * chans, CELLS), BF16),
            pltpu.VMEM((outs, CELLS), F32),
        ],
        compiler_params=pltpu.CompilerParams(vmem_limit_bytes=20 << 20),
        cost_estimate=pl.CostEstimate(
            flops=2 * outs * TAPS * chans * CELLS, bytes_accessed=6 << 20, transcendentals=0
        ),
        name="forward_parts",
    )(index, own, partner, outer, weights)


def input_kernel(chans, chips, index, *refs):
    grads = refs[:chips]
    weights, own, partner, outer, stack, left = refs[chips:]
    outs = weights.shape[2]
    for u in range(2 * chips):
        start = pl.multiple_of((index[0] ^ u) * chans, chans)
        cells = grads[u // 2][u % 2]
        for b in range(3):
            for e in range(3):
                stack[3 * b + e, pl.ds(start, chans), :] = moved(cells, 1 - b, 1 - e)
    for row, a in enumerate((1, 2 * (1 - index[1]), 2 * index[1])):
        for k in range(9):
            left[row * chans : (row + 1) * chans, k * outs : (k + 1) * outs] = weights[9 * a + k]
    total = jnp.dot(
        left[...], stack[...].reshape(9 * outs, CELLS), preferred_element_type=F32
    )
    own[...] = total[:chans]
    partner[...] = total[chans : 2 * chans].astype(BF16)
    outer[...] = total[2 * chans :].astype(BF16)


def input_parts(index, grads, weights):
    chans = weights.shape[1]
    outs = weights.shape[2]
    chips = len(grads)
    sides = jax.ShapeDtypeStruct((chans, CELLS), BF16)
    return pl.pallas_call(
        functools.partial(input_kernel, chans, chips),
        out_shape=[jax.ShapeDtypeStruct((chans, CELLS), F32), sides, sides],
        in_specs=[SMEM] + [VMEM] * (chips + 1),
        out_specs=[VMEM] * 3,
        scratch_shapes=[
            pltpu.VMEM((9, outs, CELLS), BF16),
            pltpu.VMEM((3 * chans, 9 * outs), BF16),
        ],
        compiler_params=pltpu.CompilerParams(vmem_limit_bytes=20 << 20),
        cost_estimate=pl.CostEstimate(
            flops=2 * 3 * chans * 9 * outs * CELLS, bytes_accessed=6 << 20, transcendentals=0
        ),
        name="input_parts",
    )(index, *grads, weights)


def filter_kernel(factor, groups, flips, index, *refs):
    held, refs = refs[: len(flips)], refs[len(flips) :]
    grads = refs[:groups]
    out, shifted, rows, total, sums = refs[groups:]
    planes, share, _ = grads[0].shape
    chans = held[0].shape[1]
    width = groups * share
    space, chan = index[0], index[1]
    edge = jnp.zeros((3 * chans, CELLS), BF16)
    shifted[0] = edge
    shifted[planes + 1] = edge

    for part, its_flips in zip(held, flips):
        for q, flip in enumerate(its_flips):
            at = (space ^ flip) + 1
            for e in range(3):
                shifted[at, e * chans : (e + 1) * chans, :] = moved(part[q], 0, e - 1)
    ones = jnp.ones((16, CELLS), BF16)
    contract = (((1,), (1,)), ((), ()))
    total[...] = jnp.zeros_like(total)
    sums[...] = jnp.zeros_like(sums)

    def step(q):
        for u in range(groups):
            cells = grads[u][q]
            for b in range(3):
                rows[q & 1, b * groups + (chan ^ u)] = moved(cells, 1 - b, 0)
        right = rows[q & 1].reshape(3 * width, CELLS)
        left = shifted[pl.ds(space ^ q, 3)].reshape(9 * chans, CELLS)
        term = lax.dot_general(left, right, contract, preferred_element_type=F32)
        count = lax.dot_general(
            ones, right[width : 2 * width], contract, preferred_element_type=F32
        )
        total[...] += term
        sums[...] += count

    repeat(planes, step)
    bias = sums[...] * factor
    high = bias.astype(BF16)
    low = (bias - high.astype(F32)).astype(BF16)

    def tile(tap):
        if tap == TAPS:
            rest = jnp.zeros((chans - 32, width), BF16)
            return jnp.concatenate([high, low, rest][: 2 + (chans > 32)], axis=0)
        a, b, e = tap // 9, tap // 3 % 3, tap % 3
        first = (3 * a + e) * chans
        piece = total[first : first + chans, b * width : (b + 1) * width]
        return (piece * factor).astype(BF16)

    for pair in range((TAPS + 1) // 2):
        out[pair * chans : (pair + 1) * chans, :] = jnp.concatenate(
            [tile(2 * pair), tile(2 * pair + 1)], axis=1
        )


def filter_block(index, held, flips, grads, factor):
    chans = held[0].shape[1]
    groups = len(grads)
    planes, share, _ = grads[0].shape
    width = groups * share
    return pl.pallas_call(
        functools.partial(filter_kernel, factor, groups, flips),
        out_shape=jax.ShapeDtypeStruct(((TAPS + 1) // 2 * chans, 2 * width), BF16),
        in_specs=[SMEM] + [VMEM] * (len(flips) + groups),
        out_specs=VMEM,
        scratch_shapes=[
            pltpu.VMEM((planes + 2, 3 * chans, CELLS), BF16),
            pltpu.VMEM((2, 3 * groups, share, CELLS), BF16),
            pltpu.VMEM((9 * chans, 3 * width), F32),
            pltpu.VMEM((16, width), F32),
        ],
        compiler_params=pltpu.CompilerParams(vmem_limit_bytes=28 << 20),
        cost_estimate=pl.CostEstimate(
            flops=2 * TAPS * chans * width * planes * CELLS,
            bytes_accessed=8 << 20,
            transcendentals=0,
        ),
        name="filter_block",
    )(index, *held, *grads)


def join_kernel(share, chans, index, *refs):
    blocks, (out, bias, right, held, done) = refs[:4], refs[4:]
    lanes, total = blocks[0].shape[1], out.shape[2]
    width = lanes // 2
    lane = lax.broadcasted_iota(jnp.int32, (lanes, total), 0)
    column = lax.broadcasted_iota(jnp.int32, (lanes, total), 1)
    slot = lane % width
    for odd in range(2):
        for r in range(4):
            home = (slot // share) * (4 * share) + (index[0] ^ r) * share + slot % share
            hit = (column == home) & (lane // width == odd)
            right[r * lanes : (r + 1) * lanes, odd * total : (odd + 1) * total] = jnp.where(
                hit, 1.0, 0.0
            ).astype(BF16)
    copies = []
    for k, (first, last) in enumerate(CHUNKS):
        pairs = range(first // 2, (last + 1) // 2)
        at = slice(pairs[0] * chans, (pairs[-1] + 1) * chans)
        left = jnp.concatenate([block[at, :] for block in blocks], axis=1)
        both = jnp.dot(left, right[...], preferred_element_type=F32)
        for pair in pairs:
            row = (pair - pairs[0]) * chans
            held[2 * pair] = both[row : row + chans, :total]
            if 2 * pair + 1 < TAPS:
                held[2 * pair + 1] = both[row : row + chans, total:]
            else:
                bias[...] = both[row : row + 1, total:] + both[row + 16 : row + 17, total:]
        part = pl.ds(first, last - first)
        copies.append(pltpu.make_async_copy(held.at[part], out.at[part], done.at[k]))
        copies[-1].start()
    for copy in copies:
        copy.wait()


def join_blocks(index, blocks, share, chans):
    lanes = blocks[0].shape[1]
    total = 2 * lanes
    return pl.pallas_call(
        functools.partial(join_kernel, share, chans),
        out_shape=[
            jax.ShapeDtypeStruct((TAPS, chans, total), F32),
            jax.ShapeDtypeStruct((1, total), F32),
        ],
        in_specs=[SMEM] + [VMEM] * 4,
        out_specs=[pl.BlockSpec(memory_space=pl.ANY), VMEM],
        scratch_shapes=[
            pltpu.VMEM((4 * lanes, 2 * total), BF16),
            pltpu.VMEM((TAPS, chans, total), F32),
            pltpu.SemaphoreType.DMA((len(CHUNKS),)),
        ],
        compiler_params=pltpu.CompilerParams(vmem_limit_bytes=20 << 20),
        cost_estimate=pl.CostEstimate(
            flops=4 * TAPS * chans * total * lanes * 2, bytes_accessed=4 << 20, transcendentals=0
        ),
        name="join_blocks",
    )(index, *blocks)


def swapped(value, axis, mask):
    count = lax.axis_size(axis)
    return lax.ppermute(value, axis, [(i, i ^ mask) for i in range(count)])


def exchanged(value):
    pairs = [(i, i + 1) for i in range(1, lax.axis_size("space") - 1, 2)]
    return lax.ppermute(value, "space", pairs + [(j, i) for i, j in pairs])


def other_chips(value):
    found = [value]
    for k in range(1, lax.axis_size("chan").bit_length() - 1):
        found = found + [swapped(v, "chan", 1 << k) for v in found]
    return found


def both_cores(values):
    return [v for value in values for v in (value, swapped(value, "chan", 1))]


def body(features, filters, out_bias, loss_grad):
    chans, planes, cells = features.shape
    total_out = filters.shape[2]
    depth = lax.axis_size("space")
    groups = lax.axis_size("chan")
    space = lax.axis_index("space")
    chan = lax.axis_index("chan")
    share = chans // 4
    factor = 1.0 / math.sqrt(cells * planes * depth)
    barrier = lax.optimization_barrier

    own = features.reshape(chans, cells)
    partner, outer = swapped(own, "space", 1), exchanged(own)
    outer, partner = barrier((outer, partner))
    side = space & 1
    where = jnp.stack([chan, side])
    slabs = filters.reshape(3, 9 * chans, total_out)
    weights = jnp.concatenate(
        [slabs[1], slabs[2 * (1 - side)], slabs[2 * side]], axis=0
    ).T
    keep, give = forward_parts(where, own, partner, outer, weights)

    got = swapped(give, "chan", 1)
    near = [swapped(own, "space", flip) for flip in (4, 2, 3)]
    pre_act = keep[0] + got[0] + out_bias[:, None]
    for j in range(1, groups // 2):
        pre_act = pre_act + swapped(keep[j] + got[j], "chan", 2 * j)

    pre_act, near = barrier((pre_act, near))
    sigmoid = jax.nn.sigmoid(pre_act)
    activated = pre_act * sigmoid
    grad_pre = (
        loss_grad.reshape(chans, cells).astype(F32)
        * sigmoid
        * (1.0 + pre_act * (1.0 - sigmoid))
    ).astype(BF16)

    split = grad_pre.reshape(2, 2, share, cells)
    side = space & 1
    kept = jnp.where(side == 0, split[:, 0], split[:, 1])
    given = jnp.where(side == 0, split[:, 1], split[:, 0])
    given, grad_pre = barrier((given, grad_pre))
    pair = jnp.stack([kept, swapped(given, "space", 1)], axis=0)
    ahead = swapped(near[0], "space", 1)
    last = swapped(jnp.stack([near[0], ahead], axis=0), "space", 2)
    side = (space >> 1) & 1
    kept = jnp.where(side == 0, pair[:, 0], pair[:, 1])
    given = jnp.where(side == 0, pair[:, 1], pair[:, 0])
    pieces = [kept]
    for t in range(1, depth // 2):
        pieces.append(swapped(given if t & 1 else kept, "space", 2 * t))

    grads = other_chips(jnp.stack([grad_pre, swapped(grad_pre, "chan", 1)], axis=0))
    in_grad, to_partner, to_outer = input_parts(where, grads, filters)
    pieces[0], to_partner, to_outer = barrier((pieces[0], to_partner, to_outer))
    blocks = other_chips(jnp.concatenate(pieces, axis=0))
    from_partner, from_outer = swapped(to_partner, "space", 1), exchanged(to_outer)
    blocks, last, from_partner, from_outer = barrier((blocks, last, from_partner, from_outer))
    blocks = both_cores(blocks)
    in_grad = in_grad + from_partner.astype(F32) + from_outer.astype(F32)

    held = [v[None] for v in (own, partner, *near, ahead)] + [last]
    flips = [(0,), (1,), (4,), (2,), (3,), (5,), (6, 7)]
    for mask in [1 << k for k in range(3, depth.bit_length() - 1)]:
        held.append(swapped(jnp.concatenate(held, axis=0), "space", mask))
        flips.append(tuple(f ^ mask for some in flips for f in some))
    part = filter_block(jnp.stack([space, chan]), held, flips, blocks, factor)
    parts = [part] + [swapped(part, "space", r) for r in range(1, 4)]
    joined, bias = join_blocks((space & 3).reshape(1), parts, share, chans)
    return (
        activated.reshape(chans, planes, cells),
        in_grad.reshape(chans, planes, cells),
        joined,
        bias.reshape(total_out),
    )


def solution(mesh):
    in_specs = (
        P("chan", "space", None),
        P(None, "chan", None),
        P("chan"),
        P("chan", "space", None),
    )
    out_specs = (P("chan", "space", None), P("chan", "space", None), P(None, "chan", None), P())
    return jax.shard_map(body, mesh=mesh, in_specs=in_specs, out_specs=out_specs, check_vma=False)
```

```python
import functools
import math

import jax
import jax.numpy as jnp
from jax import lax
from jax.experimental import pallas as pl
from jax.experimental.pallas import tpu as pltpu
from jax.sharding import PartitionSpec as P

TAPS = 27
PLANE_H = 32
PLANE_W = 32
CELLS = PLANE_H * PLANE_W
CHUNKS = ((0, 8), (8, 16), (16, 24), (24, TAPS))
VMEM = pl.BlockSpec(memory_space=pltpu.VMEM)
SMEM = pl.BlockSpec(memory_space=pltpu.SMEM)
BF16 = jnp.bfloat16
F32 = jnp.float32


def cell_mask(row_off, col_off):
    cell = lax.broadcasted_iota(jnp.int32, (1, CELLS), 1)
    row = cell // PLANE_W + row_off
    col = cell % PLANE_W + col_off
    inside = (row >= 0) & (row < PLANE_H) & (col >= 0) & (col < PLANE_W)
    return jnp.where(inside, 1.0, 0.0).astype(BF16)


def moved(plane, row_off, col_off):
    if row_off == 0 and col_off == 0:
        return plane
    amount = (-(row_off * PLANE_W + col_off)) % CELLS
    return pltpu.roll(plane, amount, 1) * cell_mask(row_off, col_off)


def repeat(count, step):
    if count > 8:
        lax.fori_loop(0, count, lambda q, _: (step(q), 0)[1], 0)
    else:
        for q in range(count):
            step(q)


def forward_kernel(chans, index, own, partner, outer, weights, keep, give, stack, total):
    for k, plane in enumerate((own, partner, outer)):
        cells = plane[...]
        for b in range(3):
            for e in range(3):
                start = (9 * k + 3 * b + e) * chans
                stack[start : start + chans, :] = moved(cells, b - 1, e - 1)
    total[...] = jnp.dot(weights[...], stack[...], preferred_element_type=F32)
    for j in range(keep.shape[0]):
        start = pl.multiple_of((index[0] ^ (2 * j)) * chans, chans)
        keep[j] = total[pl.ds(start, chans), :]
        start = pl.multiple_of((index[0] ^ (2 * j + 1)) * chans, chans)
        give[j] = total[pl.ds(start, chans), :]


def forward_parts(index, own, partner, outer, weights):
    chans = own.shape[0]
    outs = weights.shape[0]
    side = jax.ShapeDtypeStruct((outs // chans // 2, chans, CELLS), F32)
    return pl.pallas_call(
        functools.partial(forward_kernel, chans),
        out_shape=[side, side],
        in_specs=[SMEM] + [VMEM] * 4,
        out_specs=[VMEM] * 2,
        scratch_shapes=[
            pltpu.VMEM((TAPS * chans, CELLS), BF16),
            pltpu.VMEM((outs, CELLS), F32),
        ],
        compiler_params=pltpu.CompilerParams(vmem_limit_bytes=20 << 20),
        cost_estimate=pl.CostEstimate(
            flops=2 * outs * TAPS * chans * CELLS, bytes_accessed=6 << 20, transcendentals=0
        ),
        name="forward_parts",
    )(index, own, partner, outer, weights)


def input_kernel(chans, chips, index, *refs):
    grads = refs[:chips]
    weights, own, partner, outer, stack, left = refs[chips:]
    outs = weights.shape[2]
    for u in range(2 * chips):
        start = pl.multiple_of((index[0] ^ u) * chans, chans)
        cells = grads[u // 2][u % 2]
        for b in range(3):
            for e in range(3):
                stack[3 * b + e, pl.ds(start, chans), :] = moved(cells, 1 - b, 1 - e)
    for row, a in enumerate((1, 2 * (1 - index[1]), 2 * index[1])):
        for k in range(9):
            left[row * chans : (row + 1) * chans, k * outs : (k + 1) * outs] = weights[9 * a + k]
    total = jnp.dot(
        left[...], stack[...].reshape(9 * outs, CELLS), preferred_element_type=F32
    )
    own[...] = total[:chans]
    partner[...] = total[chans : 2 * chans].astype(BF16)
    outer[...] = total[2 * chans :].astype(BF16)


def input_parts(index, grads, weights):
    chans = weights.shape[1]
    outs = weights.shape[2]
    chips = len(grads)
    sides = jax.ShapeDtypeStruct((chans, CELLS), BF16)
    return pl.pallas_call(
        functools.partial(input_kernel, chans, chips),
        out_shape=[jax.ShapeDtypeStruct((chans, CELLS), F32), sides, sides],
        in_specs=[SMEM] + [VMEM] * (chips + 1),
        out_specs=[VMEM] * 3,
        scratch_shapes=[
            pltpu.VMEM((9, outs, CELLS), BF16),
            pltpu.VMEM((3 * chans, 9 * outs), BF16),
        ],
        compiler_params=pltpu.CompilerParams(vmem_limit_bytes=20 << 20),
        cost_estimate=pl.CostEstimate(
            flops=2 * 3 * chans * 9 * outs * CELLS, bytes_accessed=6 << 20, transcendentals=0
        ),
        name="input_parts",
    )(index, *grads, weights)


def filter_kernel(factor, groups, flips, index, *refs):
    held, refs = refs[: len(flips)], refs[len(flips) :]
    grads = refs[:groups]
    out, shifted, rows, total, sums = refs[groups:]
    planes, share, _ = grads[0].shape
    chans = held[0].shape[1]
    width = groups * share
    space, chan = index[0], index[1]
    edge = jnp.zeros((3 * chans, CELLS), BF16)
    shifted[0] = edge
    shifted[planes + 1] = edge

    for part, its_flips in zip(held, flips):
        for q, flip in enumerate(its_flips):
            at = (space ^ flip) + 1
            for e in range(3):
                shifted[at, e * chans : (e + 1) * chans, :] = moved(part[q], 0, e - 1)
    ones = jnp.ones((16, CELLS), BF16)
    contract = (((1,), (1,)), ((), ()))
    total[...] = jnp.zeros_like(total)
    sums[...] = jnp.zeros_like(sums)

    def step(q):
        for u in range(groups):
            cells = grads[u][q]
            for b in range(3):
                rows[q & 1, b * groups + (chan ^ u)] = moved(cells, 1 - b, 0)
        right = rows[q & 1].reshape(3 * width, CELLS)
        left = shifted[pl.ds(space ^ q, 3)].reshape(9 * chans, CELLS)
        term = lax.dot_general(left, right, contract, preferred_element_type=F32)
        count = lax.dot_general(
            ones, right[width : 2 * width], contract, preferred_element_type=F32
        )
        total[...] += term
        sums[...] += count

    repeat(planes, step)
    bias = sums[...] * factor
    high = bias.astype(BF16)
    low = (bias - high.astype(F32)).astype(BF16)

    def tile(tap):
        if tap == TAPS:
            rest = jnp.zeros((chans - 32, width), BF16)
            return jnp.concatenate([high, low, rest][: 2 + (chans > 32)], axis=0)
        a, b, e = tap // 9, tap // 3 % 3, tap % 3
        first = (3 * a + e) * chans
        piece = total[first : first + chans, b * width : (b + 1) * width]
        return (piece * factor).astype(BF16)

    for pair in range((TAPS + 1) // 2):
        out[pair * chans : (pair + 1) * chans, :] = jnp.concatenate(
            [tile(2 * pair), tile(2 * pair + 1)], axis=1
        )


def filter_block(index, held, flips, grads, factor):
    chans = held[0].shape[1]
    groups = len(grads)
    planes, share, _ = grads[0].shape
    width = groups * share
    return pl.pallas_call(
        functools.partial(filter_kernel, factor, groups, flips),
        out_shape=jax.ShapeDtypeStruct(((TAPS + 1) // 2 * chans, 2 * width), BF16),
        in_specs=[SMEM] + [VMEM] * (len(flips) + groups),
        out_specs=VMEM,
        scratch_shapes=[
            pltpu.VMEM((planes + 2, 3 * chans, CELLS), BF16),
            pltpu.VMEM((2, 3 * groups, share, CELLS), BF16),
            pltpu.VMEM((9 * chans, 3 * width), F32),
            pltpu.VMEM((16, width), F32),
        ],
        compiler_params=pltpu.CompilerParams(vmem_limit_bytes=28 << 20),
        cost_estimate=pl.CostEstimate(
            flops=2 * TAPS * chans * width * planes * CELLS,
            bytes_accessed=8 << 20,
            transcendentals=0,
        ),
        name="filter_block",
    )(index, *held, *grads)


def join_kernel(share, chans, index, *refs):
    blocks, (out, bias, right, held, done) = refs[:4], refs[4:]
    lanes, total = blocks[0].shape[1], out.shape[2]
    width = lanes // 2
    lane = lax.broadcasted_iota(jnp.int32, (lanes, total), 0)
    column = lax.broadcasted_iota(jnp.int32, (lanes, total), 1)
    slot = lane % width
    for odd in range(2):
        for r in range(4):
            home = (slot // share) * (4 * share) + (index[0] ^ r) * share + slot % share
            hit = (column == home) & (lane // width == odd)
            right[r * lanes : (r + 1) * lanes, odd * total : (odd + 1) * total] = jnp.where(
                hit, 1.0, 0.0
            ).astype(BF16)
    copies = []
    for k, (first, last) in enumerate(CHUNKS):
        pairs = range(first // 2, (last + 1) // 2)
        at = slice(pairs[0] * chans, (pairs[-1] + 1) * chans)
        left = jnp.concatenate([block[at, :] for block in blocks], axis=1)
        both = jnp.dot(left, right[...], preferred_element_type=F32)
        for pair in pairs:
            row = (pair - pairs[0]) * chans
            held[2 * pair] = both[row : row + chans, :total]
            if 2 * pair + 1 < TAPS:
                held[2 * pair + 1] = both[row : row + chans, total:]
            else:
                bias[...] = both[row : row + 1, total:] + both[row + 16 : row + 17, total:]
        part = pl.ds(first, last - first)
        copies.append(pltpu.make_async_copy(held.at[part], out.at[part], done.at[k]))
        copies[-1].start()
    for copy in copies:
        copy.wait()


def join_blocks(index, blocks, share, chans):
    lanes = blocks[0].shape[1]
    total = 2 * lanes
    return pl.pallas_call(
        functools.partial(join_kernel, share, chans),
        out_shape=[
            jax.ShapeDtypeStruct((TAPS, chans, total), F32),
            jax.ShapeDtypeStruct((1, total), F32),
        ],
        in_specs=[SMEM] + [VMEM] * 4,
        out_specs=[pl.BlockSpec(memory_space=pl.ANY), VMEM],
        scratch_shapes=[
            pltpu.VMEM((4 * lanes, 2 * total), BF16),
            pltpu.VMEM((TAPS, chans, total), F32),
            pltpu.SemaphoreType.DMA((len(CHUNKS),)),
        ],
        compiler_params=pltpu.CompilerParams(vmem_limit_bytes=20 << 20),
        cost_estimate=pl.CostEstimate(
            flops=4 * TAPS * chans * total * lanes * 2, bytes_accessed=4 << 20, transcendentals=0
        ),
        name="join_blocks",
    )(index, *blocks)


def swapped(value, axis, mask):
    count = lax.axis_size(axis)
    return lax.ppermute(value, axis, [(i, i ^ mask) for i in range(count)])


def exchanged(value):
    pairs = [(i, i + 1) for i in range(1, lax.axis_size("space") - 1, 2)]
    return lax.ppermute(value, "space", pairs + [(j, i) for i, j in pairs])


def other_chips(value):
    found = [value]
    for k in range(1, lax.axis_size("chan").bit_length() - 1):
        found = found + [swapped(v, "chan", 1 << k) for v in found]
    return found


def both_cores(values):
    return [v for value in values for v in (value, swapped(value, "chan", 1))]


def body(features, filters, out_bias, loss_grad):
    chans, planes, cells = features.shape
    total_out = filters.shape[2]
    depth = lax.axis_size("space")
    groups = lax.axis_size("chan")
    space = lax.axis_index("space")
    chan = lax.axis_index("chan")
    share = chans // 4
    factor = 1.0 / math.sqrt(cells * planes * depth)
    barrier = lax.optimization_barrier

    own = features.reshape(chans, cells)
    partner, outer = swapped(own, "space", 1), exchanged(own)
    outer, partner = barrier((outer, partner))
    side = space & 1
    where = jnp.stack([chan, side])
    slabs = filters.reshape(3, 9 * chans, total_out)
    weights = jnp.concatenate(
        [slabs[1], slabs[2 * (1 - side)], slabs[2 * side]], axis=0
    ).T
    keep, give = forward_parts(where, own, partner, outer, weights)

    got = swapped(give, "chan", 1)
    near = [swapped(own, "space", flip) for flip in (4, 2)]
    pre_act = keep[0] + got[0] + out_bias[:, None]
    for j in range(1, groups // 2):
        pre_act = pre_act + swapped(keep[j] + got[j], "chan", 2 * j)

    pre_act, near = barrier((pre_act, near))
    sigmoid = jax.nn.sigmoid(pre_act)
    activated = pre_act * sigmoid
    grad_pre = (
        loss_grad.reshape(chans, cells).astype(F32)
        * sigmoid
        * (1.0 + pre_act * (1.0 - sigmoid))
    ).astype(BF16)

    split = grad_pre.reshape(2, 2, share, cells)
    side = space & 1
    kept = jnp.where(side == 0, split[:, 0], split[:, 1])
    given = jnp.where(side == 0, split[:, 1], split[:, 0])
    given, grad_pre = barrier((given, grad_pre))
    pair = jnp.stack([kept, swapped(given, "space", 1)], axis=0)
    ahead = swapped(jnp.stack(near, axis=0), "space", 1)
    last = swapped(jnp.stack([near[0], ahead[0]], axis=0), "space", 2)
    side = (space >> 1) & 1
    kept = jnp.where(side == 0, pair[:, 0], pair[:, 1])
    given = jnp.where(side == 0, pair[:, 1], pair[:, 0])
    pieces = [kept]
    for t in range(1, depth // 2):
        pieces.append(swapped(given if t & 1 else kept, "space", 2 * t))

    grads = other_chips(jnp.stack([grad_pre, swapped(grad_pre, "chan", 1)], axis=0))
    in_grad, to_partner, to_outer = input_parts(where, grads, filters)
    pieces[0], to_partner, to_outer = barrier((pieces[0], to_partner, to_outer))
    blocks = other_chips(jnp.concatenate(pieces, axis=0))
    from_partner, from_outer = swapped(to_partner, "space", 1), exchanged(to_outer)
    blocks, last, from_partner, from_outer = barrier((blocks, last, from_partner, from_outer))
    blocks = both_cores(blocks)
    in_grad = in_grad + from_partner.astype(F32) + from_outer.astype(F32)

    held = [v[None] for v in (own, partner, *near)] + [ahead, last]
    flips = [(0,), (1,), (4,), (2,), (5, 3), (6, 7)]
    for mask in [1 << k for k in range(3, depth.bit_length() - 1)]:
        held.append(swapped(jnp.concatenate(held, axis=0), "space", mask))
        flips.append(tuple(f ^ mask for some in flips for f in some))
    part = filter_block(jnp.stack([space, chan]), held, flips, blocks, factor)
    parts = [part] + [swapped(part, "space", r) for r in range(1, 4)]
    joined, bias = join_blocks((space & 3).reshape(1), parts, share, chans)
    return (
        activated.reshape(chans, planes, cells),
        in_grad.reshape(chans, planes, cells),
        joined,
        bias.reshape(total_out),
    )


def solution(mesh):
    in_specs = (
        P("chan", "space", None),
        P(None, "chan", None),
        P("chan"),
        P("chan", "space", None),
    )
    out_specs = (P("chan", "space", None), P("chan", "space", None), P(None, "chan", None), P())
    return jax.shard_map(body, mesh=mesh, in_specs=in_specs, out_specs=out_specs, check_vma=False)
```

```python
import functools
import math

import jax
import jax.numpy as jnp
from jax import lax
from jax.experimental import pallas as pl
from jax.experimental.pallas import tpu as pltpu
from jax.sharding import PartitionSpec as P

TAPS = 27
PLANE_H = 32
PLANE_W = 32
CELLS = PLANE_H * PLANE_W
CHUNKS = ((0, 8), (8, 16), (16, 24), (24, TAPS))
VMEM = pl.BlockSpec(memory_space=pltpu.VMEM)
SMEM = pl.BlockSpec(memory_space=pltpu.SMEM)
BF16 = jnp.bfloat16
F32 = jnp.float32


def cell_mask(row_off, col_off):
    cell = lax.broadcasted_iota(jnp.int32, (1, CELLS), 1)
    row = cell // PLANE_W + row_off
    col = cell % PLANE_W + col_off
    inside = (row >= 0) & (row < PLANE_H) & (col >= 0) & (col < PLANE_W)
    return jnp.where(inside, 1.0, 0.0).astype(BF16)


def moved(plane, row_off, col_off):
    if row_off == 0 and col_off == 0:
        return plane
    amount = (-(row_off * PLANE_W + col_off)) % CELLS
    return pltpu.roll(plane, amount, 1) * cell_mask(row_off, col_off)


def repeat(count, step):
    if count > 8:
        lax.fori_loop(0, count, lambda q, _: (step(q), 0)[1], 0)
    else:
        for q in range(count):
            step(q)


def forward_kernel(chans, index, own, partner, outer, weights, keep, give, stack, total):
    for k, plane in enumerate((own, partner, outer)):
        cells = plane[...]
        for b in range(3):
            for e in range(3):
                start = (9 * k + 3 * b + e) * chans
                stack[start : start + chans, :] = moved(cells, b - 1, e - 1)
    total[...] = jnp.dot(weights[...], stack[...], preferred_element_type=F32)
    for j in range(keep.shape[0]):
        start = pl.multiple_of((index[0] ^ (2 * j)) * chans, chans)
        keep[j] = total[pl.ds(start, chans), :]
        start = pl.multiple_of((index[0] ^ (2 * j + 1)) * chans, chans)
        give[j] = total[pl.ds(start, chans), :]


def forward_parts(index, own, partner, outer, weights):
    chans = own.shape[0]
    outs = weights.shape[0]
    side = jax.ShapeDtypeStruct((outs // chans // 2, chans, CELLS), F32)
    return pl.pallas_call(
        functools.partial(forward_kernel, chans),
        out_shape=[side, side],
        in_specs=[SMEM] + [VMEM] * 4,
        out_specs=[VMEM] * 2,
        scratch_shapes=[
            pltpu.VMEM((TAPS * chans, CELLS), BF16),
            pltpu.VMEM((outs, CELLS), F32),
        ],
        compiler_params=pltpu.CompilerParams(vmem_limit_bytes=20 << 20),
        cost_estimate=pl.CostEstimate(
            flops=2 * outs * TAPS * chans * CELLS, bytes_accessed=6 << 20, transcendentals=0
        ),
        name="forward_parts",
    )(index, own, partner, outer, weights)


def input_kernel(chans, chips, index, *refs):
    grads = refs[:chips]
    weights, own, partner, outer, stack, left = refs[chips:]
    outs = weights.shape[2]
    for u in range(2 * chips):
        start = pl.multiple_of((index[0] ^ u) * chans, chans)
        cells = grads[u // 2][u % 2]
        for b in range(3):
            for e in range(3):
                stack[3 * b + e, pl.ds(start, chans), :] = moved(cells, 1 - b, 1 - e)
    for row, a in enumerate((1, 2 * (1 - index[1]), 2 * index[1])):
        for k in range(9):
            left[row * chans : (row + 1) * chans, k * outs : (k + 1) * outs] = weights[9 * a + k]
    total = jnp.dot(
        left[...], stack[...].reshape(9 * outs, CELLS), preferred_element_type=F32
    )
    own[...] = total[:chans]
    partner[...] = total[chans : 2 * chans].astype(BF16)
    outer[...] = total[2 * chans :].astype(BF16)


def input_parts(index, grads, weights):
    chans = weights.shape[1]
    outs = weights.shape[2]
    chips = len(grads)
    sides = jax.ShapeDtypeStruct((chans, CELLS), BF16)
    return pl.pallas_call(
        functools.partial(input_kernel, chans, chips),
        out_shape=[jax.ShapeDtypeStruct((chans, CELLS), F32), sides, sides],
        in_specs=[SMEM] + [VMEM] * (chips + 1),
        out_specs=[VMEM] * 3,
        scratch_shapes=[
            pltpu.VMEM((9, outs, CELLS), BF16),
            pltpu.VMEM((3 * chans, 9 * outs), BF16),
        ],
        compiler_params=pltpu.CompilerParams(vmem_limit_bytes=20 << 20),
        cost_estimate=pl.CostEstimate(
            flops=2 * 3 * chans * 9 * outs * CELLS, bytes_accessed=6 << 20, transcendentals=0
        ),
        name="input_parts",
    )(index, *grads, weights)


def filter_kernel(factor, groups, flips, index, *refs):
    held, refs = refs[: len(flips)], refs[len(flips) :]
    grads = refs[:groups]
    out, shifted, rows, total, sums = refs[groups:]
    planes, share, _ = grads[0].shape
    chans = held[0].shape[1]
    width = groups * share
    space, chan = index[0], index[1]
    edge = jnp.zeros((3 * chans, CELLS), BF16)
    shifted[0] = edge
    shifted[planes + 1] = edge

    for part, its_flips in zip(held, flips):
        for q, flip in enumerate(its_flips):
            at = (space ^ flip) + 1
            for e in range(3):
                shifted[at, e * chans : (e + 1) * chans, :] = moved(part[q], 0, e - 1)
    ones = jnp.ones((16, CELLS), BF16)
    contract = (((1,), (1,)), ((), ()))
    total[...] = jnp.zeros_like(total)
    sums[...] = jnp.zeros_like(sums)

    def step(q):
        for u in range(groups):
            cells = grads[u][q]
            for b in range(3):
                rows[q & 1, b * groups + (chan ^ u)] = moved(cells, 1 - b, 0)
        right = rows[q & 1].reshape(3 * width, CELLS)
        left = shifted[pl.ds(space ^ q, 3)].reshape(9 * chans, CELLS)
        term = lax.dot_general(left, right, contract, preferred_element_type=F32)
        count = lax.dot_general(
            ones, right[width : 2 * width], contract, preferred_element_type=F32
        )
        total[...] += term
        sums[...] += count

    repeat(planes, step)
    bias = sums[...] * factor
    high = bias.astype(BF16)
    low = (bias - high.astype(F32)).astype(BF16)

    def tile(tap):
        if tap == TAPS:
            rest = jnp.zeros((chans - 32, width), BF16)
            return jnp.concatenate([high, low, rest][: 2 + (chans > 32)], axis=0)
        a, b, e = tap // 9, tap // 3 % 3, tap % 3
        first = (3 * a + e) * chans
        piece = total[first : first + chans, b * width : (b + 1) * width]
        return (piece * factor).astype(BF16)

    for pair in range((TAPS + 1) // 2):
        out[pair * chans : (pair + 1) * chans, :] = jnp.concatenate(
            [tile(2 * pair), tile(2 * pair + 1)], axis=1
        )


def filter_block(index, held, flips, grads, factor):
    chans = held[0].shape[1]
    groups = len(grads)
    planes, share, _ = grads[0].shape
    width = groups * share
    return pl.pallas_call(
        functools.partial(filter_kernel, factor, groups, flips),
        out_shape=jax.ShapeDtypeStruct(((TAPS + 1) // 2 * chans, 2 * width), BF16),
        in_specs=[SMEM] + [VMEM] * (len(flips) + groups),
        out_specs=VMEM,
        scratch_shapes=[
            pltpu.VMEM((planes + 2, 3 * chans, CELLS), BF16),
            pltpu.VMEM((2, 3 * groups, share, CELLS), BF16),
            pltpu.VMEM((9 * chans, 3 * width), F32),
            pltpu.VMEM((16, width), F32),
        ],
        compiler_params=pltpu.CompilerParams(vmem_limit_bytes=28 << 20),
        cost_estimate=pl.CostEstimate(
            flops=2 * TAPS * chans * width * planes * CELLS,
            bytes_accessed=8 << 20,
            transcendentals=0,
        ),
        name="filter_block",
    )(index, *held, *grads)


def join_kernel(share, chans, index, *refs):
    blocks, (out, bias, right, held, done) = refs[:4], refs[4:]
    lanes, total = blocks[0].shape[1], out.shape[2]
    width = lanes // 2
    lane = lax.broadcasted_iota(jnp.int32, (lanes, total), 0)
    column = lax.broadcasted_iota(jnp.int32, (lanes, total), 1)
    slot = lane % width
    for odd in range(2):
        for r in range(4):
            home = (slot // share) * (4 * share) + (index[0] ^ r) * share + slot % share
            hit = (column == home) & (lane // width == odd)
            right[r * lanes : (r + 1) * lanes, odd * total : (odd + 1) * total] = jnp.where(
                hit, 1.0, 0.0
            ).astype(BF16)
    copies = []
    for k, (first, last) in enumerate(CHUNKS):
        pairs = range(first // 2, (last + 1) // 2)
        at = slice(pairs[0] * chans, (pairs[-1] + 1) * chans)
        left = jnp.concatenate([block[at, :] for block in blocks], axis=1)
        both = jnp.dot(left, right[...], preferred_element_type=F32)
        for pair in pairs:
            row = (pair - pairs[0]) * chans
            held[2 * pair] = both[row : row + chans, :total]
            if 2 * pair + 1 < TAPS:
                held[2 * pair + 1] = both[row : row + chans, total:]
            else:
                bias[...] = both[row : row + 1, total:] + both[row + 16 : row + 17, total:]
        part = pl.ds(first, last - first)
        copies.append(pltpu.make_async_copy(held.at[part], out.at[part], done.at[k]))
        copies[-1].start()
    for copy in copies:
        copy.wait()


def join_blocks(index, blocks, share, chans):
    lanes = blocks[0].shape[1]
    total = 2 * lanes
    return pl.pallas_call(
        functools.partial(join_kernel, share, chans),
        out_shape=[
            jax.ShapeDtypeStruct((TAPS, chans, total), F32),
            jax.ShapeDtypeStruct((1, total), F32),
        ],
        in_specs=[SMEM] + [VMEM] * 4,
        out_specs=[pl.BlockSpec(memory_space=pl.ANY), VMEM],
        scratch_shapes=[
            pltpu.VMEM((4 * lanes, 2 * total), BF16),
            pltpu.VMEM((TAPS, chans, total), F32),
            pltpu.SemaphoreType.DMA((len(CHUNKS),)),
        ],
        compiler_params=pltpu.CompilerParams(vmem_limit_bytes=20 << 20),
        cost_estimate=pl.CostEstimate(
            flops=4 * TAPS * chans * total * lanes * 2, bytes_accessed=4 << 20, transcendentals=0
        ),
        name="join_blocks",
    )(index, *blocks)


def swapped(value, axis, mask):
    count = lax.axis_size(axis)
    return lax.ppermute(value, axis, [(i, i ^ mask) for i in range(count)])


def exchanged(value):
    pairs = [(i, i + 1) for i in range(1, lax.axis_size("space") - 1, 2)]
    return lax.ppermute(value, "space", pairs + [(j, i) for i, j in pairs])


def other_chips(value):
    found = [value]
    for k in range(1, lax.axis_size("chan").bit_length() - 1):
        found = found + [swapped(v, "chan", 1 << k) for v in found]
    return found


def both_cores(values):
    return [v for value in values for v in (value, swapped(value, "chan", 1))]


def body(features, filters, out_bias, loss_grad):
    chans, planes, cells = features.shape
    total_out = filters.shape[2]
    depth = lax.axis_size("space")
    groups = lax.axis_size("chan")
    space = lax.axis_index("space")
    chan = lax.axis_index("chan")
    share = chans // 4
    factor = 1.0 / math.sqrt(cells * planes * depth)
    barrier = lax.optimization_barrier

    own = features.reshape(chans, cells)
    partner, outer = swapped(own, "space", 1), exchanged(own)
    outer, partner = barrier((outer, partner))
    side = space & 1
    where = jnp.stack([chan, side])
    slabs = filters.reshape(3, 9 * chans, total_out)
    weights = jnp.concatenate(
        [slabs[1], slabs[2 * (1 - side)], slabs[2 * side]], axis=0
    ).T
    keep, give = forward_parts(where, own, partner, outer, weights)

    got = swapped(give, "chan", 1)
    near = [swapped(own, "space", flip) for flip in (4, 2)]
    pre_act = keep[0] + got[0] + out_bias[:, None]
    for j in range(1, groups // 2):
        term = (keep[j] + got[j]).astype(BF16)
        pre_act = pre_act + swapped(term, "chan", 2 * j).astype(F32)

    sigmoid = jax.nn.sigmoid(pre_act)
    activated = pre_act * sigmoid
    grad_pre = (
        loss_grad.reshape(chans, cells).astype(F32)
        * sigmoid
        * (1.0 + pre_act * (1.0 - sigmoid))
    ).astype(BF16)

    split = grad_pre.reshape(2, 2, share, cells)
    side = space & 1
    kept = jnp.where(side == 0, split[:, 0], split[:, 1])
    given = jnp.where(side == 0, split[:, 1], split[:, 0])
    given, grad_pre = barrier((given, grad_pre))
    beside, near = barrier((swapped(grad_pre, "chan", 1), near))
    pair = jnp.stack([kept, swapped(given, "space", 1)], axis=0)
    ahead = swapped(jnp.stack(near, axis=0), "space", 1)
    last = swapped(jnp.stack([near[0], ahead[0]], axis=0), "space", 2)
    side = (space >> 1) & 1
    kept = jnp.where(side == 0, pair[:, 0], pair[:, 1])
    given = jnp.where(side == 0, pair[:, 1], pair[:, 0])
    pieces = [kept]
    for t in range(1, depth // 2):
        pieces.append(swapped(given if t & 1 else kept, "space", 2 * t))

    grads = other_chips(jnp.stack([grad_pre, beside], axis=0))
    in_grad, to_partner, to_outer = input_parts(where, grads, filters)
    pieces[0], to_partner, to_outer = barrier((pieces[0], to_partner, to_outer))
    blocks = other_chips(jnp.concatenate(pieces, axis=0))
    from_partner, from_outer = swapped(to_partner, "space", 1), exchanged(to_outer)
    blocks, last, from_partner, from_outer = barrier((blocks, last, from_partner, from_outer))
    blocks = both_cores(blocks)
    in_grad = in_grad + from_partner.astype(F32) + from_outer.astype(F32)

    held = [v[None] for v in (own, partner, *near)] + [ahead, last]
    flips = [(0,), (1,), (4,), (2,), (5, 3), (6, 7)]
    for mask in [1 << k for k in range(3, depth.bit_length() - 1)]:
        held.append(swapped(jnp.concatenate(held, axis=0), "space", mask))
        flips.append(tuple(f ^ mask for some in flips for f in some))
    part = filter_block(jnp.stack([space, chan]), held, flips, blocks, factor)
    parts = [part] + [swapped(part, "space", r) for r in range(1, 4)]
    joined, bias = join_blocks((space & 3).reshape(1), parts, share, chans)
    return (
        activated.reshape(chans, planes, cells),
        in_grad.reshape(chans, planes, cells),
        joined,
        bias.reshape(total_out),
    )


def solution(mesh):
    in_specs = (
        P("chan", "space", None),
        P(None, "chan", None),
        P("chan"),
        P("chan", "space", None),
    )
    out_specs = (P("chan", "space", None), P("chan", "space", None), P(None, "chan", None), P())
    return jax.shard_map(body, mesh=mesh, in_specs=in_specs, out_specs=out_specs, check_vma=False)
```

```python
import functools
import math

import jax
import jax.numpy as jnp
from jax import lax
from jax.experimental import pallas as pl
from jax.experimental.pallas import tpu as pltpu
from jax.sharding import PartitionSpec as P
import numpy as np

TAPS = 27
PLANE_H = 32
PLANE_W = 32
CELLS = PLANE_H * PLANE_W
CHUNKS = ((0, 8), (8, 16), (16, 24), (24, TAPS))
VMEM = pl.BlockSpec(memory_space=pltpu.VMEM)
SMEM = pl.BlockSpec(memory_space=pltpu.SMEM)
BF16 = jnp.bfloat16
F32 = jnp.float32


def cell_mask(row_off, col_off):
    cell = lax.broadcasted_iota(jnp.int32, (1, CELLS), 1)
    row = cell // PLANE_W + row_off
    col = cell % PLANE_W + col_off
    inside = (row >= 0) & (row < PLANE_H) & (col >= 0) & (col < PLANE_W)
    return jnp.where(inside, 1.0, 0.0).astype(BF16)


def moved(plane, row_off, col_off):
    if row_off == 0 and col_off == 0:
        return plane
    amount = (-(row_off * PLANE_W + col_off)) % CELLS
    return pltpu.roll(plane, amount, 1) * cell_mask(row_off, col_off)


def repeat(count, step):
    if count > 8:
        lax.fori_loop(0, count, lambda q, _: (step(q), 0)[1], 0)
    else:
        for q in range(count):
            step(q)


def forward_kernel(chans, index, own, partner, outer, weights, keep, give, stack, total):
    for k, plane in enumerate((own, partner, outer)):
        cells = plane[...]
        for b in range(3):
            for e in range(3):
                start = (9 * k + 3 * b + e) * chans
                stack[start : start + chans, :] = moved(cells, b - 1, e - 1)
    total[...] = jnp.dot(weights[...], stack[...], preferred_element_type=F32)
    for j in range(keep.shape[0]):
        start = pl.multiple_of((index[0] ^ (2 * j)) * chans, chans)
        keep[j] = total[pl.ds(start, chans), :]
        start = pl.multiple_of((index[0] ^ (2 * j + 1)) * chans, chans)
        give[j] = total[pl.ds(start, chans), :]


def forward_parts(index, own, partner, outer, weights):
    chans = own.shape[0]
    outs = weights.shape[0]
    side = jax.ShapeDtypeStruct((outs // chans // 2, chans, CELLS), F32)
    return pl.pallas_call(
        functools.partial(forward_kernel, chans),
        out_shape=[side, side],
        in_specs=[SMEM] + [VMEM] * 4,
        out_specs=[VMEM] * 2,
        scratch_shapes=[
            pltpu.VMEM((TAPS * chans, CELLS), BF16),
            pltpu.VMEM((outs, CELLS), F32),
        ],
        compiler_params=pltpu.CompilerParams(vmem_limit_bytes=20 << 20),
        cost_estimate=pl.CostEstimate(
            flops=2 * outs * TAPS * chans * CELLS, bytes_accessed=6 << 20, transcendentals=0
        ),
        name="forward_parts",
    )(index, own, partner, outer, weights)


def input_kernel(chans, chips, index, *refs):
    grads = refs[:chips]
    weights, own, partner, outer, stack, left = refs[chips:]
    outs = weights.shape[2]
    for u in range(2 * chips):
        start = pl.multiple_of((index[0] ^ u) * chans, chans)
        cells = grads[u // 2][u % 2]
        for b in range(3):
            for e in range(3):
                stack[3 * b + e, pl.ds(start, chans), :] = moved(cells, 1 - b, 1 - e)
    for row, a in enumerate((1, 2 * (1 - index[1]), 2 * index[1])):
        for k in range(9):
            left[row * chans : (row + 1) * chans, k * outs : (k + 1) * outs] = weights[9 * a + k]
    total = jnp.dot(
        left[...], stack[...].reshape(9 * outs, CELLS), preferred_element_type=F32
    )
    own[...] = total[:chans]
    partner[...] = total[chans : 2 * chans].astype(BF16)
    outer[...] = total[2 * chans :].astype(BF16)


def input_parts(index, grads, weights):
    chans = weights.shape[1]
    outs = weights.shape[2]
    chips = len(grads)
    sides = jax.ShapeDtypeStruct((chans, CELLS), BF16)
    return pl.pallas_call(
        functools.partial(input_kernel, chans, chips),
        out_shape=[jax.ShapeDtypeStruct((chans, CELLS), F32), sides, sides],
        in_specs=[SMEM] + [VMEM] * (chips + 1),
        out_specs=[VMEM] * 3,
        scratch_shapes=[
            pltpu.VMEM((9, outs, CELLS), BF16),
            pltpu.VMEM((3 * chans, 9 * outs), BF16),
        ],
        compiler_params=pltpu.CompilerParams(vmem_limit_bytes=20 << 20),
        cost_estimate=pl.CostEstimate(
            flops=2 * 3 * chans * 9 * outs * CELLS, bytes_accessed=6 << 20, transcendentals=0
        ),
        name="input_parts",
    )(index, *grads, weights)


def filter_kernel(factor, groups, flips, index, *refs):
    held, refs = refs[: len(flips)], refs[len(flips) :]
    grads = refs[:groups]
    out, shifted, rows, total, sums = refs[groups:]
    planes, share, _ = grads[0].shape
    chans = held[0].shape[1]
    width = groups * share
    space, chan = index[0], index[1]
    edge = jnp.zeros((3 * chans, CELLS), BF16)
    shifted[0] = edge
    shifted[planes + 1] = edge

    for part, its_flips in zip(held, flips):
        for q, flip in enumerate(its_flips):
            at = (space ^ flip) + 1
            for e in range(3):
                shifted[at, e * chans : (e + 1) * chans, :] = moved(part[q], 0, e - 1)
    ones = jnp.ones((16, CELLS), BF16)
    contract = (((1,), (1,)), ((), ()))
    total[...] = jnp.zeros_like(total)
    sums[...] = jnp.zeros_like(sums)

    def step(q):
        for u in range(groups):
            cells = grads[u][q]
            for b in range(3):
                rows[q & 1, b * groups + (chan ^ u)] = moved(cells, 1 - b, 0)
        right = rows[q & 1].reshape(3 * width, CELLS)
        left = shifted[pl.ds(space ^ q, 3)].reshape(9 * chans, CELLS)
        term = lax.dot_general(left, right, contract, preferred_element_type=F32)
        count = lax.dot_general(
            ones, right[width : 2 * width], contract, preferred_element_type=F32
        )
        total[...] += term
        sums[...] += count

    repeat(planes, step)
    bias = sums[...] * factor
    high = bias.astype(BF16)
    low = (bias - high.astype(F32)).astype(BF16)

    def tile(tap):
        if tap == TAPS:
            rest = jnp.zeros((chans - 32, width), BF16)
            return jnp.concatenate([high, low, rest][: 2 + (chans > 32)], axis=0)
        a, b, e = tap // 9, tap // 3 % 3, tap % 3
        first = (3 * a + e) * chans
        piece = total[first : first + chans, b * width : (b + 1) * width]
        return (piece * factor).astype(BF16)

    for pair in range((TAPS + 1) // 2):
        out[pair * chans : (pair + 1) * chans, :] = jnp.concatenate(
            [tile(2 * pair), tile(2 * pair + 1)], axis=1
        )


def filter_block(index, held, flips, grads, factor):
    chans = held[0].shape[1]
    groups = len(grads)
    planes, share, _ = grads[0].shape
    width = groups * share
    return pl.pallas_call(
        functools.partial(filter_kernel, factor, groups, flips),
        out_shape=jax.ShapeDtypeStruct(((TAPS + 1) // 2 * chans, 2 * width), BF16),
        in_specs=[SMEM] + [VMEM] * (len(flips) + groups),
        out_specs=VMEM,
        scratch_shapes=[
            pltpu.VMEM((planes + 2, 3 * chans, CELLS), BF16),
            pltpu.VMEM((2, 3 * groups, share, CELLS), BF16),
            pltpu.VMEM((9 * chans, 3 * width), F32),
            pltpu.VMEM((16, width), F32),
        ],
        compiler_params=pltpu.CompilerParams(vmem_limit_bytes=28 << 20),
        cost_estimate=pl.CostEstimate(
            flops=2 * TAPS * chans * width * planes * CELLS,
            bytes_accessed=8 << 20,
            transcendentals=0,
        ),
        name="filter_block",
    )(index, *held, *grads)


def spread(share, lanes, total):
    slot = np.arange(4 * lanes) % (lanes // 2)
    quarter, odd = np.arange(4 * lanes) // lanes, np.arange(4 * lanes) % lanes // (lanes // 2)
    home = odd * total + (slot // share) * (4 * share) + quarter * share + slot % share
    return jnp.asarray(home[:, None] == np.arange(2 * total), BF16)


def join_kernel(chans, index, *refs):
    blocks, (right, out, bias, left, held, done) = refs[:4], refs[4:]
    lanes, total = blocks[0].shape[1], out.shape[2]
    for r in range(4):
        at = pl.multiple_of((index[0] ^ r) * lanes, lanes)
        left[:, pl.ds(at, lanes)] = blocks[r][...]
    copies = []
    for k, (first, last) in enumerate(CHUNKS):
        pairs = range(first // 2, (last + 1) // 2)
        at = slice(pairs[0] * chans, (pairs[-1] + 1) * chans)
        both = jnp.dot(left[at, :], right[...], preferred_element_type=F32)
        for pair in pairs:
            row = (pair - pairs[0]) * chans
            held[2 * pair] = both[row : row + chans, :total]
            if 2 * pair + 1 < TAPS:
                held[2 * pair + 1] = both[row : row + chans, total:]
            else:
                bias[...] = both[row : row + 1, total:] + both[row + 16 : row + 17, total:]
        part = pl.ds(first, last - first)
        copies.append(pltpu.make_async_copy(held.at[part], out.at[part], done.at[k]))
        copies[-1].start()
    for copy in copies:
        copy.wait()


def join_blocks(index, blocks, share, chans):
    lanes = blocks[0].shape[1]
    total = 2 * lanes
    return pl.pallas_call(
        functools.partial(join_kernel, chans),
        out_shape=[
            jax.ShapeDtypeStruct((TAPS, chans, total), F32),
            jax.ShapeDtypeStruct((1, total), F32),
        ],
        in_specs=[SMEM] + [VMEM] * 5,
        out_specs=[pl.BlockSpec(memory_space=pl.ANY), VMEM],
        scratch_shapes=[
            pltpu.VMEM((blocks[0].shape[0], 4 * lanes), BF16),
            pltpu.VMEM((TAPS, chans, total), F32),
            pltpu.SemaphoreType.DMA((len(CHUNKS),)),
        ],
        compiler_params=pltpu.CompilerParams(vmem_limit_bytes=20 << 20),
        cost_estimate=pl.CostEstimate(
            flops=4 * TAPS * chans * total * lanes * 2, bytes_accessed=4 << 20, transcendentals=0
        ),
        name="join_blocks",
    )(index, *blocks, spread(share, lanes, total))


def swapped(value, axis, mask):
    count = lax.axis_size(axis)
    return lax.ppermute(value, axis, [(i, i ^ mask) for i in range(count)])


def exchanged(value):
    pairs = [(i, i + 1) for i in range(1, lax.axis_size("space") - 1, 2)]
    return lax.ppermute(value, "space", pairs + [(j, i) for i, j in pairs])


def other_chips(value):
    found = [value]
    for k in range(1, lax.axis_size("chan").bit_length() - 1):
        found = found + [swapped(v, "chan", 1 << k) for v in found]
    return found


def both_cores(values):
    return [v for value in values for v in (value, swapped(value, "chan", 1))]


def body(features, filters, out_bias, loss_grad):
    chans, planes, cells = features.shape
    total_out = filters.shape[2]
    depth = lax.axis_size("space")
    groups = lax.axis_size("chan")
    space = lax.axis_index("space")
    chan = lax.axis_index("chan")
    share = chans // 4
    factor = 1.0 / math.sqrt(cells * planes * depth)
    barrier = lax.optimization_barrier

    own = features.reshape(chans, cells)
    partner, outer = swapped(own, "space", 1), exchanged(own)
    outer, partner = barrier((outer, partner))
    side = space & 1
    where = jnp.stack([chan, side])
    slabs = filters.reshape(3, 9 * chans, total_out)
    weights = jnp.concatenate(
        [slabs[1], slabs[2 * (1 - side)], slabs[2 * side]], axis=0
    ).T
    keep, give = forward_parts(where, own, partner, outer, weights)

    got = swapped(give, "chan", 1)
    near = [swapped(own, "space", flip) for flip in (4, 2)]
    pre_act = keep[0] + got[0] + out_bias[:, None]
    for j in range(1, groups // 2):
        term = (keep[j] + got[j]).astype(BF16)
        pre_act = pre_act + swapped(term, "chan", 2 * j).astype(F32)

    sigmoid = jax.nn.sigmoid(pre_act)
    activated = pre_act * sigmoid
    grad_pre = (
        loss_grad.reshape(chans, cells).astype(F32)
        * sigmoid
        * (1.0 + pre_act * (1.0 - sigmoid))
    ).astype(BF16)

    split = grad_pre.reshape(2, 2, share, cells)
    side = space & 1
    kept = jnp.where(side == 0, split[:, 0], split[:, 1])
    given = jnp.where(side == 0, split[:, 1], split[:, 0])
    given, grad_pre = barrier((given, grad_pre))
    beside, near = barrier((swapped(grad_pre, "chan", 1), near))
    pair = jnp.stack([kept, swapped(given, "space", 1)], axis=0)
    ahead = swapped(jnp.stack(near, axis=0), "space", 1)
    side = (space >> 1) & 1
    kept = jnp.where(side == 0, pair[:, 0], pair[:, 1])
    given = jnp.where(side == 0, pair[:, 1], pair[:, 0])
    pieces = [kept]
    for t in range(1, depth // 2):
        pieces.append(swapped(given if t & 1 else kept, "space", 2 * t))

    grads = other_chips(jnp.stack([grad_pre, beside], axis=0))
    in_grad, to_partner, to_outer = input_parts(where, grads, filters)
    pieces[0], to_partner, to_outer, ahead = barrier((pieces[0], to_partner, to_outer, ahead))
    last = swapped(jnp.stack([near[0], ahead[0]], axis=0), "space", 2)
    blocks = other_chips(jnp.concatenate(pieces, axis=0))
    from_partner, from_outer = swapped(to_partner, "space", 1), exchanged(to_outer)
    blocks, from_partner, from_outer = barrier((blocks, from_partner, from_outer))
    blocks = both_cores(blocks)
    in_grad = in_grad + from_partner.astype(F32) + from_outer.astype(F32)

    held = [v[None] for v in (own, partner, *near)] + [ahead, last]
    flips = [(0,), (1,), (4,), (2,), (5, 3), (6, 7)]
    for mask in [1 << k for k in range(3, depth.bit_length() - 1)]:
        held.append(swapped(jnp.concatenate(held, axis=0), "space", mask))
        flips.append(tuple(f ^ mask for some in flips for f in some))
    part = filter_block(jnp.stack([space, chan]), held, flips, blocks, factor)
    parts = [part] + [swapped(part, "space", r) for r in range(1, 4)]
    joined, bias = join_blocks((space & 3).reshape(1), parts, share, chans)
    return (
        activated.reshape(chans, planes, cells),
        in_grad.reshape(chans, planes, cells),
        joined,
        bias.reshape(total_out),
    )


def solution(mesh):
    in_specs = (
        P("chan", "space", None),
        P(None, "chan", None),
        P("chan"),
        P("chan", "space", None),
    )
    out_specs = (P("chan", "space", None), P("chan", "space", None), P(None, "chan", None), P())
    return jax.shard_map(body, mesh=mesh, in_specs=in_specs, out_specs=out_specs, check_vma=False)
```

```python
import functools
import math

import jax
import jax.numpy as jnp
from jax import lax
from jax.experimental import pallas as pl
from jax.experimental.pallas import tpu as pltpu
from jax.sharding import PartitionSpec as P
import numpy as np

TAPS = 27
PLANE_H = 32
PLANE_W = 32
CELLS = PLANE_H * PLANE_W
CHUNKS = ((0, 8), (8, 16), (16, 24), (24, TAPS))
VMEM = pl.BlockSpec(memory_space=pltpu.VMEM)
SMEM = pl.BlockSpec(memory_space=pltpu.SMEM)
BF16 = jnp.bfloat16
F32 = jnp.float32


def cell_mask(row_off, col_off):
    cell = lax.broadcasted_iota(jnp.int32, (1, CELLS), 1)
    row = cell // PLANE_W + row_off
    col = cell % PLANE_W + col_off
    inside = (row >= 0) & (row < PLANE_H) & (col >= 0) & (col < PLANE_W)
    return jnp.where(inside, 1.0, 0.0).astype(BF16)


def moved(plane, row_off, col_off):
    if row_off == 0 and col_off == 0:
        return plane
    amount = (-(row_off * PLANE_W + col_off)) % CELLS
    return pltpu.roll(plane, amount, 1) * cell_mask(row_off, col_off)


def repeat(count, step):
    if count > 8:
        lax.fori_loop(0, count, lambda q, _: (step(q), 0)[1], 0)
    else:
        for q in range(count):
            step(q)


def stacked(stack, planes):
    for k, plane in enumerate(planes):
        cells = plane[...]
        chans = cells.shape[0]
        for b in range(3):
            for e in range(3):
                start = (9 * k + 3 * b + e) * chans
                stack[start : start + chans, :] = moved(cells, b - 1, e - 1)
    return stack[...]


def near_kernel(own, partner, weights, total, stack):
    total[...] = jnp.dot(
        weights[...], stacked(stack, (own, partner)), preferred_element_type=F32
    )


def near_part(own, partner, weights):
    outs, depth = weights.shape
    return pl.pallas_call(
        near_kernel,
        out_shape=jax.ShapeDtypeStruct((outs, CELLS), F32),
        in_specs=[VMEM] * 3,
        out_specs=VMEM,
        scratch_shapes=[pltpu.VMEM((depth, CELLS), BF16)],
        compiler_params=pltpu.CompilerParams(vmem_limit_bytes=16 << 20),
        cost_estimate=pl.CostEstimate(
            flops=2 * outs * depth * CELLS, bytes_accessed=4 << 20, transcendentals=0
        ),
        name="near_part",
    )(own, partner, weights)


def forward_kernel(chans, index, most, outer, weights, keep, give, stack, total):
    total[...] = most[...] + jnp.dot(
        weights[...], stacked(stack, (outer,)), preferred_element_type=F32
    )
    for j in range(keep.shape[0]):
        start = pl.multiple_of((index[0] ^ (2 * j)) * chans, chans)
        keep[j] = total[pl.ds(start, chans), :]
        start = pl.multiple_of((index[0] ^ (2 * j + 1)) * chans, chans)
        give[j] = total[pl.ds(start, chans), :]


def forward_parts(index, most, outer, weights):
    chans = outer.shape[0]
    outs, depth = weights.shape
    side = jax.ShapeDtypeStruct((outs // chans // 2, chans, CELLS), F32)
    return pl.pallas_call(
        functools.partial(forward_kernel, chans),
        out_shape=[side, side],
        in_specs=[SMEM] + [VMEM] * 3,
        out_specs=[VMEM] * 2,
        scratch_shapes=[pltpu.VMEM((depth, CELLS), BF16), pltpu.VMEM((outs, CELLS), F32)],
        compiler_params=pltpu.CompilerParams(vmem_limit_bytes=16 << 20),
        cost_estimate=pl.CostEstimate(
            flops=2 * outs * depth * CELLS, bytes_accessed=4 << 20, transcendentals=0
        ),
        name="forward_parts",
    )(index, most, outer, weights)


def input_kernel(chans, chips, index, *refs):
    grads = refs[:chips]
    weights, own, partner, outer, stack, left = refs[chips:]
    outs = weights.shape[2]
    for u in range(2 * chips):
        start = pl.multiple_of((index[0] ^ u) * chans, chans)
        cells = grads[u // 2][u % 2]
        for b in range(3):
            for e in range(3):
                stack[3 * b + e, pl.ds(start, chans), :] = moved(cells, 1 - b, 1 - e)
    for row, a in enumerate((1, 2 * (1 - index[1]), 2 * index[1])):
        for k in range(9):
            left[row * chans : (row + 1) * chans, k * outs : (k + 1) * outs] = weights[9 * a + k]
    total = jnp.dot(
        left[...], stack[...].reshape(9 * outs, CELLS), preferred_element_type=F32
    )
    own[...] = total[:chans]
    partner[...] = total[chans : 2 * chans].astype(BF16)
    outer[...] = total[2 * chans :].astype(BF16)


def input_parts(index, grads, weights):
    chans = weights.shape[1]
    outs = weights.shape[2]
    chips = len(grads)
    sides = jax.ShapeDtypeStruct((chans, CELLS), BF16)
    return pl.pallas_call(
        functools.partial(input_kernel, chans, chips),
        out_shape=[jax.ShapeDtypeStruct((chans, CELLS), F32), sides, sides],
        in_specs=[SMEM] + [VMEM] * (chips + 1),
        out_specs=[VMEM] * 3,
        scratch_shapes=[
            pltpu.VMEM((9, outs, CELLS), BF16),
            pltpu.VMEM((3 * chans, 9 * outs), BF16),
        ],
        compiler_params=pltpu.CompilerParams(vmem_limit_bytes=20 << 20),
        cost_estimate=pl.CostEstimate(
            flops=2 * 3 * chans * 9 * outs * CELLS, bytes_accessed=6 << 20, transcendentals=0
        ),
        name="input_parts",
    )(index, *grads, weights)


def filter_kernel(factor, groups, flips, index, *refs):
    held, refs = refs[: len(flips)], refs[len(flips) :]
    grads = refs[:groups]
    out, shifted, rows, total, sums = refs[groups:]
    planes, share, _ = grads[0].shape
    chans = held[0].shape[1]
    width = groups * share
    space, chan = index[0], index[1]
    edge = jnp.zeros((3 * chans, CELLS), BF16)
    shifted[0] = edge
    shifted[planes + 1] = edge

    for part, its_flips in zip(held, flips):
        for q, flip in enumerate(its_flips):
            at = (space ^ flip) + 1
            for e in range(3):
                shifted[at, e * chans : (e + 1) * chans, :] = moved(part[q], 0, e - 1)
    ones = jnp.ones((16, CELLS), BF16)
    contract = (((1,), (1,)), ((), ()))
    total[...] = jnp.zeros_like(total)
    sums[...] = jnp.zeros_like(sums)

    def step(q):
        for u in range(groups):
            cells = grads[u][q]
            for b in range(3):
                rows[q & 1, b * groups + (chan ^ u)] = moved(cells, 1 - b, 0)
        right = rows[q & 1].reshape(3 * width, CELLS)
        left = shifted[pl.ds(space ^ q, 3)].reshape(9 * chans, CELLS)
        term = lax.dot_general(left, right, contract, preferred_element_type=F32)
        count = lax.dot_general(
            ones, right[width : 2 * width], contract, preferred_element_type=F32
        )
        total[...] += term
        sums[...] += count

    repeat(planes, step)
    bias = sums[...] * factor
    high = bias.astype(BF16)
    low = (bias - high.astype(F32)).astype(BF16)

    def tile(tap):
        if tap == TAPS:
            rest = jnp.zeros((chans - 32, width), BF16)
            return jnp.concatenate([high, low, rest][: 2 + (chans > 32)], axis=0)
        a, b, e = tap // 9, tap // 3 % 3, tap % 3
        first = (3 * a + e) * chans
        piece = total[first : first + chans, b * width : (b + 1) * width]
        return (piece * factor).astype(BF16)

    for pair in range((TAPS + 1) // 2):
        out[pair * chans : (pair + 1) * chans, :] = jnp.concatenate(
            [tile(2 * pair), tile(2 * pair + 1)], axis=1
        )


def filter_block(index, held, flips, grads, factor):
    chans = held[0].shape[1]
    groups = len(grads)
    planes, share, _ = grads[0].shape
    width = groups * share
    return pl.pallas_call(
        functools.partial(filter_kernel, factor, groups, flips),
        out_shape=jax.ShapeDtypeStruct(((TAPS + 1) // 2 * chans, 2 * width), BF16),
        in_specs=[SMEM] + [VMEM] * (len(flips) + groups),
        out_specs=VMEM,
        scratch_shapes=[
            pltpu.VMEM((planes + 2, 3 * chans, CELLS), BF16),
            pltpu.VMEM((2, 3 * groups, share, CELLS), BF16),
            pltpu.VMEM((9 * chans, 3 * width), F32),
            pltpu.VMEM((16, width), F32),
        ],
        compiler_params=pltpu.CompilerParams(vmem_limit_bytes=28 << 20),
        cost_estimate=pl.CostEstimate(
            flops=2 * TAPS * chans * width * planes * CELLS,
            bytes_accessed=8 << 20,
            transcendentals=0,
        ),
        name="filter_block",
    )(index, *held, *grads)


def spread(share, lanes, total):
    slot = np.arange(4 * lanes) % (lanes // 2)
    quarter, odd = np.arange(4 * lanes) // lanes, np.arange(4 * lanes) % lanes // (lanes // 2)
    home = odd * total + (slot // share) * (4 * share) + quarter * share + slot % share
    return jnp.asarray(home[:, None] == np.arange(2 * total), BF16)


def join_kernel(chans, index, *refs):
    blocks, (right, out, bias, left, held, done) = refs[:4], refs[4:]
    lanes, total = blocks[0].shape[1], out.shape[2]
    for r in range(4):
        at = pl.multiple_of((index[0] ^ r) * lanes, lanes)
        left[:, pl.ds(at, lanes)] = blocks[r][...]
    copies = []
    for k, (first, last) in enumerate(CHUNKS):
        pairs = range(first // 2, (last + 1) // 2)
        at = slice(pairs[0] * chans, (pairs[-1] + 1) * chans)
        both = jnp.dot(left[at, :], right[...], preferred_element_type=F32)
        for pair in pairs:
            row = (pair - pairs[0]) * chans
            held[2 * pair] = both[row : row + chans, :total]
            if 2 * pair + 1 < TAPS:
                held[2 * pair + 1] = both[row : row + chans, total:]
            else:
                bias[...] = both[row : row + 1, total:] + both[row + 16 : row + 17, total:]
        part = pl.ds(first, last - first)
        copies.append(pltpu.make_async_copy(held.at[part], out.at[part], done.at[k]))
        copies[-1].start()
    for copy in copies:
        copy.wait()


def join_blocks(index, blocks, share, chans):
    lanes = blocks[0].shape[1]
    total = 2 * lanes
    return pl.pallas_call(
        functools.partial(join_kernel, chans),
        out_shape=[
            jax.ShapeDtypeStruct((TAPS, chans, total), F32),
            jax.ShapeDtypeStruct((1, total), F32),
        ],
        in_specs=[SMEM] + [VMEM] * 5,
        out_specs=[pl.BlockSpec(memory_space=pl.ANY), VMEM],
        scratch_shapes=[
            pltpu.VMEM((blocks[0].shape[0], 4 * lanes), BF16),
            pltpu.VMEM((TAPS, chans, total), F32),
            pltpu.SemaphoreType.DMA((len(CHUNKS),)),
        ],
        compiler_params=pltpu.CompilerParams(vmem_limit_bytes=20 << 20),
        cost_estimate=pl.CostEstimate(
            flops=4 * TAPS * chans * total * lanes * 2, bytes_accessed=4 << 20, transcendentals=0
        ),
        name="join_blocks",
    )(index, *blocks, spread(share, lanes, total))


def swapped(value, axis, mask):
    count = lax.axis_size(axis)
    return lax.ppermute(value, axis, [(i, i ^ mask) for i in range(count)])


def exchanged(value):
    pairs = [(i, i + 1) for i in range(1, lax.axis_size("space") - 1, 2)]
    return lax.ppermute(value, "space", pairs + [(j, i) for i, j in pairs])


def other_chips(value):
    found = [value]
    for k in range(1, lax.axis_size("chan").bit_length() - 1):
        found = found + [swapped(v, "chan", 1 << k) for v in found]
    return found


def both_cores(values):
    return [v for value in values for v in (value, swapped(value, "chan", 1))]


def body(features, filters, out_bias, loss_grad):
    chans, planes, cells = features.shape
    total_out = filters.shape[2]
    depth = lax.axis_size("space")
    groups = lax.axis_size("chan")
    space = lax.axis_index("space")
    chan = lax.axis_index("chan")
    share = chans // 4
    factor = 1.0 / math.sqrt(cells * planes * depth)
    barrier = lax.optimization_barrier

    own = features.reshape(chans, cells)
    partner = swapped(own, "space", 1)
    side = space & 1
    where = jnp.stack([chan, side])
    again, where = lax.optimization_barrier((own, where))
    outer = exchanged(again)
    slabs = filters.reshape(3, 9 * chans, total_out)
    inner = jnp.concatenate([slabs[1], slabs[2 * (1 - side)]], axis=0).T
    most = near_part(own, partner, inner)
    keep, give = forward_parts(where, most, outer, slabs[2 * side].T)

    got = swapped(give, "chan", 1)
    near = [swapped(own, "space", flip) for flip in (4, 2)]
    pre_act = keep[0] + got[0] + out_bias[:, None]
    for j in range(1, groups // 2):
        term = (keep[j] + got[j]).astype(BF16)
        pre_act = pre_act + swapped(term, "chan", 2 * j).astype(F32)

    sigmoid = jax.nn.sigmoid(pre_act)
    activated = pre_act * sigmoid
    grad_pre = (
        loss_grad.reshape(chans, cells).astype(F32)
        * sigmoid
        * (1.0 + pre_act * (1.0 - sigmoid))
    ).astype(BF16)

    split = grad_pre.reshape(2, 2, share, cells)
    side = space & 1
    kept = jnp.where(side == 0, split[:, 0], split[:, 1])
    given = jnp.where(side == 0, split[:, 1], split[:, 0])
    given, grad_pre = barrier((given, grad_pre))
    beside, near = barrier((swapped(grad_pre, "chan", 1), near))
    pair = jnp.stack([kept, swapped(given, "space", 1)], axis=0)
    ahead = swapped(jnp.stack(near, axis=0), "space", 1)
    side = (space >> 1) & 1
    kept = jnp.where(side == 0, pair[:, 0], pair[:, 1])
    given = jnp.where(side == 0, pair[:, 1], pair[:, 0])
    pieces = [kept]
    for t in range(1, depth // 2):
        pieces.append(swapped(given if t & 1 else kept, "space", 2 * t))

    grads = other_chips(jnp.stack([grad_pre, beside], axis=0))
    in_grad, to_partner, to_outer = input_parts(where, grads, filters)
    pieces[0], to_partner, to_outer, ahead = barrier((pieces[0], to_partner, to_outer, ahead))
    last = swapped(jnp.stack([near[0], ahead[0]], axis=0), "space", 2)
    blocks = other_chips(jnp.concatenate(pieces, axis=0))
    from_partner, from_outer = swapped(to_partner, "space", 1), exchanged(to_outer)
    blocks, from_partner, from_outer = barrier((blocks, from_partner, from_outer))
    blocks = both_cores(blocks)
    in_grad = in_grad + from_partner.astype(F32) + from_outer.astype(F32)

    held = [v[None] for v in (own, partner, *near)] + [ahead, last]
    flips = [(0,), (1,), (4,), (2,), (5, 3), (6, 7)]
    for mask in [1 << k for k in range(3, depth.bit_length() - 1)]:
        held.append(swapped(jnp.concatenate(held, axis=0), "space", mask))
        flips.append(tuple(f ^ mask for some in flips for f in some))
    part = filter_block(jnp.stack([space, chan]), held, flips, blocks, factor)
    parts = [part] + [swapped(part, "space", r) for r in range(1, 4)]
    joined, bias = join_blocks((space & 3).reshape(1), parts, share, chans)
    return (
        activated.reshape(chans, planes, cells),
        in_grad.reshape(chans, planes, cells),
        joined,
        bias.reshape(total_out),
    )


def solution(mesh):
    in_specs = (
        P("chan", "space", None),
        P(None, "chan", None),
        P("chan"),
        P("chan", "space", None),
    )
    out_specs = (P("chan", "space", None), P("chan", "space", None), P(None, "chan", None), P())
    return jax.shard_map(body, mesh=mesh, in_specs=in_specs, out_specs=out_specs, check_vma=False)
```

```python
import functools
import math

import jax
import jax.numpy as jnp
from jax import lax
from jax.experimental import pallas as pl
from jax.experimental.pallas import tpu as pltpu
from jax.sharding import PartitionSpec as P
import numpy as np

TAPS = 27
PLANE_H = 32
PLANE_W = 32
CELLS = PLANE_H * PLANE_W
CHUNKS = ((0, 8), (8, 16), (16, 24), (24, TAPS))
VMEM = pl.BlockSpec(memory_space=pltpu.VMEM)
SMEM = pl.BlockSpec(memory_space=pltpu.SMEM)
BF16 = jnp.bfloat16
F32 = jnp.float32


def cell_mask(row_off, col_off):
    cell = lax.broadcasted_iota(jnp.int32, (1, CELLS), 1)
    row = cell // PLANE_W + row_off
    col = cell % PLANE_W + col_off
    inside = (row >= 0) & (row < PLANE_H) & (col >= 0) & (col < PLANE_W)
    return jnp.where(inside, 1.0, 0.0).astype(BF16)


def moved(plane, row_off, col_off):
    if row_off == 0 and col_off == 0:
        return plane
    amount = (-(row_off * PLANE_W + col_off)) % CELLS
    return pltpu.roll(plane, amount, 1) * cell_mask(row_off, col_off)


def repeat(count, step):
    if count > 8:
        lax.fori_loop(0, count, lambda q, _: (step(q), 0)[1], 0)
    else:
        for q in range(count):
            step(q)


def stacked(stack, planes):
    for k, plane in enumerate(planes):
        cells = plane[...]
        chans = cells.shape[0]
        for b in range(3):
            for e in range(3):
                start = (9 * k + 3 * b + e) * chans
                stack[start : start + chans, :] = moved(cells, b - 1, e - 1)
    return stack[...]


def near_kernel(own, partner, weights, total, stack):
    total[...] = jnp.dot(
        weights[...], stacked(stack, (own, partner)), preferred_element_type=F32
    )


def near_part(own, partner, weights):
    outs, depth = weights.shape
    return pl.pallas_call(
        near_kernel,
        out_shape=jax.ShapeDtypeStruct((outs, CELLS), F32),
        in_specs=[VMEM] * 3,
        out_specs=VMEM,
        scratch_shapes=[pltpu.VMEM((depth, CELLS), BF16)],
        compiler_params=pltpu.CompilerParams(vmem_limit_bytes=16 << 20),
        cost_estimate=pl.CostEstimate(
            flops=2 * outs * depth * CELLS, bytes_accessed=4 << 20, transcendentals=0
        ),
        name="near_part",
    )(own, partner, weights)


def forward_kernel(chans, index, most, outer, weights, keep, give, stack, total):
    total[...] = most[...] + jnp.dot(
        weights[...], stacked(stack, (outer,)), preferred_element_type=F32
    )
    for j in range(keep.shape[0]):
        start = pl.multiple_of((index[0] ^ (2 * j)) * chans, chans)
        keep[j] = total[pl.ds(start, chans), :]
        start = pl.multiple_of((index[0] ^ (2 * j + 1)) * chans, chans)
        give[j] = total[pl.ds(start, chans), :]


def forward_parts(index, most, outer, weights):
    chans = outer.shape[0]
    outs, depth = weights.shape
    side = jax.ShapeDtypeStruct((outs // chans // 2, chans, CELLS), F32)
    return pl.pallas_call(
        functools.partial(forward_kernel, chans),
        out_shape=[side, side],
        in_specs=[SMEM] + [VMEM] * 3,
        out_specs=[VMEM] * 2,
        scratch_shapes=[pltpu.VMEM((depth, CELLS), BF16), pltpu.VMEM((outs, CELLS), F32)],
        compiler_params=pltpu.CompilerParams(vmem_limit_bytes=16 << 20),
        cost_estimate=pl.CostEstimate(
            flops=2 * outs * depth * CELLS, bytes_accessed=4 << 20, transcendentals=0
        ),
        name="forward_parts",
    )(index, most, outer, weights)


def input_kernel(chans, chips, index, *refs):
    grads = refs[:chips]
    weights, own, partner, outer, stack, left = refs[chips:]
    outs = weights.shape[2]
    for u in range(2 * chips):
        start = pl.multiple_of((index[0] ^ u) * chans, chans)
        cells = grads[u // 2][u % 2]
        for b in range(3):
            for e in range(3):
                stack[3 * b + e, pl.ds(start, chans), :] = moved(cells, 1 - b, 1 - e)
    for row, a in enumerate((1, 2 * (1 - index[1]), 2 * index[1])):
        for k in range(9):
            left[row * chans : (row + 1) * chans, k * outs : (k + 1) * outs] = weights[9 * a + k]
    total = jnp.dot(
        left[...], stack[...].reshape(9 * outs, CELLS), preferred_element_type=F32
    )
    own[...] = total[:chans]
    partner[...] = total[chans : 2 * chans].astype(BF16)
    outer[...] = total[2 * chans :].astype(BF16)


def input_parts(index, grads, weights):
    chans = weights.shape[1]
    outs = weights.shape[2]
    chips = len(grads)
    sides = jax.ShapeDtypeStruct((chans, CELLS), BF16)
    return pl.pallas_call(
        functools.partial(input_kernel, chans, chips),
        out_shape=[jax.ShapeDtypeStruct((chans, CELLS), F32), sides, sides],
        in_specs=[SMEM] + [VMEM] * (chips + 1),
        out_specs=[VMEM] * 3,
        scratch_shapes=[
            pltpu.VMEM((9, outs, CELLS), BF16),
            pltpu.VMEM((3 * chans, 9 * outs), BF16),
        ],
        compiler_params=pltpu.CompilerParams(vmem_limit_bytes=20 << 20),
        cost_estimate=pl.CostEstimate(
            flops=2 * 3 * chans * 9 * outs * CELLS, bytes_accessed=6 << 20, transcendentals=0
        ),
        name="input_parts",
    )(index, *grads, weights)


def filter_kernel(factor, groups, flips, index, *refs):
    held, refs = refs[: len(flips)], refs[len(flips) :]
    grads = refs[:groups]
    out, shifted, rows, total, sums = refs[groups:]
    planes, share, _ = grads[0].shape
    chans = held[0].shape[1]
    width = groups * share
    space, chan = index[0], index[1]
    edge = jnp.zeros((3 * chans, CELLS), BF16)
    shifted[0] = edge
    shifted[planes + 1] = edge

    for part, its_flips in zip(held, flips):
        for q, flip in enumerate(its_flips):
            at = (space ^ flip) + 1
            for e in range(3):
                shifted[at, e * chans : (e + 1) * chans, :] = moved(part[q], 0, e - 1)
    ones = jnp.ones((16, CELLS), BF16)
    contract = (((1,), (1,)), ((), ()))
    total[...] = jnp.zeros_like(total)
    sums[...] = jnp.zeros_like(sums)

    def step(q):
        for u in range(groups):
            cells = grads[u][q]
            for b in range(3):
                rows[q & 1, b * groups + (chan ^ u)] = moved(cells, 1 - b, 0)
        right = rows[q & 1].reshape(3 * width, CELLS)
        left = shifted[pl.ds(space ^ q, 3)].reshape(9 * chans, CELLS)
        term = lax.dot_general(left, right, contract, preferred_element_type=F32)
        count = lax.dot_general(
            ones, right[width : 2 * width], contract, preferred_element_type=F32
        )
        total[...] += term
        sums[...] += count

    repeat(planes, step)
    bias = sums[...] * factor
    high = bias.astype(BF16)
    low = (bias - high.astype(F32)).astype(BF16)

    def tile(tap):
        if tap == TAPS:
            rest = jnp.zeros((chans - 32, width), BF16)
            return jnp.concatenate([high, low, rest][: 2 + (chans > 32)], axis=0)
        a, b, e = tap // 9, tap // 3 % 3, tap % 3
        first = (3 * a + e) * chans
        piece = total[first : first + chans, b * width : (b + 1) * width]
        return (piece * factor).astype(BF16)

    for pair in range((TAPS + 1) // 2):
        out[pair * chans : (pair + 1) * chans, :] = jnp.concatenate(
            [tile(2 * pair), tile(2 * pair + 1)], axis=1
        )


def filter_block(index, held, flips, grads, factor):
    chans = held[0].shape[1]
    groups = len(grads)
    planes, share, _ = grads[0].shape
    width = groups * share
    return pl.pallas_call(
        functools.partial(filter_kernel, factor, groups, flips),
        out_shape=jax.ShapeDtypeStruct(((TAPS + 1) // 2 * chans, 2 * width), BF16),
        in_specs=[SMEM] + [VMEM] * (len(flips) + groups),
        out_specs=VMEM,
        scratch_shapes=[
            pltpu.VMEM((planes + 2, 3 * chans, CELLS), BF16),
            pltpu.VMEM((2, 3 * groups, share, CELLS), BF16),
            pltpu.VMEM((9 * chans, 3 * width), F32),
            pltpu.VMEM((16, width), F32),
        ],
        compiler_params=pltpu.CompilerParams(vmem_limit_bytes=28 << 20),
        cost_estimate=pl.CostEstimate(
            flops=2 * TAPS * chans * width * planes * CELLS,
            bytes_accessed=8 << 20,
            transcendentals=0,
        ),
        name="filter_block",
    )(index, *held, *grads)


def spread(share, lanes, total):
    slot = np.arange(4 * lanes) % (lanes // 2)
    quarter, odd = np.arange(4 * lanes) // lanes, np.arange(4 * lanes) % lanes // (lanes // 2)
    home = odd * total + (slot // share) * (4 * share) + quarter * share + slot % share
    return jnp.asarray(home[:, None] == np.arange(2 * total), BF16)


def join_kernel(chans, index, *refs):
    blocks, (right, out, bias, left, held, done) = refs[:4], refs[4:]
    lanes, total = blocks[0].shape[1], out.shape[2]
    for r in range(4):
        at = pl.multiple_of((index[0] ^ r) * lanes, lanes)
        left[:, pl.ds(at, lanes)] = blocks[r][...]
    copies = []
    for k, (first, last) in enumerate(CHUNKS):
        pairs = range(first // 2, (last + 1) // 2)
        at = slice(pairs[0] * chans, (pairs[-1] + 1) * chans)
        both = jnp.dot(left[at, :], right[...], preferred_element_type=F32)
        for pair in pairs:
            row = (pair - pairs[0]) * chans
            held[2 * pair] = both[row : row + chans, :total]
            if 2 * pair + 1 < TAPS:
                held[2 * pair + 1] = both[row : row + chans, total:]
            else:
                bias[...] = both[row : row + 1, total:] + both[row + 16 : row + 17, total:]
        part = pl.ds(first, last - first)
        copies.append(pltpu.make_async_copy(held.at[part], out.at[part], done.at[k]))
        copies[-1].start()
    for copy in copies:
        copy.wait()


def join_blocks(index, blocks, share, chans):
    lanes = blocks[0].shape[1]
    total = 2 * lanes
    return pl.pallas_call(
        functools.partial(join_kernel, chans),
        out_shape=[
            jax.ShapeDtypeStruct((TAPS, chans, total), F32),
            jax.ShapeDtypeStruct((1, total), F32),
        ],
        in_specs=[SMEM] + [VMEM] * 5,
        out_specs=[pl.BlockSpec(memory_space=pl.ANY), VMEM],
        scratch_shapes=[
            pltpu.VMEM((blocks[0].shape[0], 4 * lanes), BF16),
            pltpu.VMEM((TAPS, chans, total), F32),
            pltpu.SemaphoreType.DMA((len(CHUNKS),)),
        ],
        compiler_params=pltpu.CompilerParams(vmem_limit_bytes=20 << 20),
        cost_estimate=pl.CostEstimate(
            flops=4 * TAPS * chans * total * lanes * 2, bytes_accessed=4 << 20, transcendentals=0
        ),
        name="join_blocks",
    )(index, *blocks, spread(share, lanes, total))


def swapped(value, axis, mask):
    count = lax.axis_size(axis)
    return lax.ppermute(value, axis, [(i, i ^ mask) for i in range(count)])


def exchanged(value):
    pairs = [(i, i + 1) for i in range(1, lax.axis_size("space") - 1, 2)]
    return lax.ppermute(value, "space", pairs + [(j, i) for i, j in pairs])


def other_chips(value):
    found = [value]
    for k in range(1, lax.axis_size("chan").bit_length() - 1):
        found = found + [swapped(v, "chan", 1 << k) for v in found]
    return found


def both_cores(values):
    return [v for value in values for v in (value, swapped(value, "chan", 1))]


def body(features, filters, out_bias, loss_grad):
    chans, planes, cells = features.shape
    total_out = filters.shape[2]
    depth = lax.axis_size("space")
    groups = lax.axis_size("chan")
    space = lax.axis_index("space")
    chan = lax.axis_index("chan")
    share = chans // 4
    factor = 1.0 / math.sqrt(cells * planes * depth)
    barrier = lax.optimization_barrier

    own = features.reshape(chans, cells)
    partner = swapped(own, "space", 1)
    side = space & 1
    where = jnp.stack([chan, side])
    again, where = lax.optimization_barrier((own, where))
    outer = exchanged(again)
    slabs = filters.reshape(3, 9 * chans, total_out)
    inner = jnp.concatenate([slabs[1], slabs[2 * (1 - side)]], axis=0).T
    most = near_part(own, partner, inner)
    keep, give = forward_parts(where, most, outer, slabs[2 * side].T)

    got = swapped(give, "chan", 1)
    near = [swapped(own, "space", flip) for flip in (4, 2)]
    pre_act = keep[0] + got[0] + out_bias[:, None]
    for j in range(1, groups // 2):
        term = (keep[j] + got[j]).astype(BF16)
        pre_act = pre_act + swapped(term, "chan", 2 * j).astype(F32)

    sigmoid = jax.nn.sigmoid(pre_act)
    activated = pre_act * sigmoid
    grad_pre = (
        loss_grad.reshape(chans, cells).astype(F32)
        * sigmoid
        * (1.0 + pre_act * (1.0 - sigmoid))
    ).astype(BF16)

    split = grad_pre.reshape(2, 2, share, cells)
    side = space & 1
    kept = jnp.where(side == 0, split[:, 0], split[:, 1])
    given = jnp.where(side == 0, split[:, 1], split[:, 0])
    given, grad_pre = barrier((given, grad_pre))
    beside, near = barrier((swapped(grad_pre, "chan", 1), near))
    pair = jnp.stack([kept, swapped(given, "space", 1)], axis=0)
    ahead = swapped(jnp.stack(near, axis=0), "space", 1)
    side = (space >> 1) & 1
    kept = jnp.where(side == 0, pair[:, 0], pair[:, 1])
    given = jnp.where(side == 0, pair[:, 1], pair[:, 0])
    pieces = [kept]
    for t in range(1, depth // 2):
        pieces.append(swapped(given if t & 1 else kept, "space", 2 * t))

    grads = other_chips(jnp.stack([grad_pre, beside], axis=0))
    in_grad, to_partner, to_outer = input_parts(where, grads, filters)
    pieces[0], to_partner, to_outer, ahead = barrier((pieces[0], to_partner, to_outer, ahead))
    last = swapped(jnp.stack([near[0], ahead[0]], axis=0), "space", 2)
    blocks = other_chips(jnp.concatenate(pieces, axis=0))
    from_partner = swapped(to_partner, "space", 1)
    blocks, from_partner = barrier((blocks, from_partner))
    blocks = both_cores(blocks)
    held = [v[None] for v in (own, partner, *near)] + [ahead, last]
    flips = [(0,), (1,), (4,), (2,), (5, 3), (6, 7)]
    for mask in [1 << k for k in range(3, depth.bit_length() - 1)]:
        held.append(swapped(jnp.concatenate(held, axis=0), "space", mask))
        flips.append(tuple(f ^ mask for some in flips for f in some))
    part = filter_block(jnp.stack([space, chan]), held, flips, blocks, factor)
    part, to_outer = barrier((part, to_outer))
    parts = [part] + [swapped(part, "space", r) for r in range(1, 4)]
    in_grad = in_grad + from_partner.astype(F32) + exchanged(to_outer).astype(F32)
    joined, bias = join_blocks((space & 3).reshape(1), parts, share, chans)
    return (
        activated.reshape(chans, planes, cells),
        in_grad.reshape(chans, planes, cells),
        joined,
        bias.reshape(total_out),
    )


def solution(mesh):
    in_specs = (
        P("chan", "space", None),
        P(None, "chan", None),
        P("chan"),
        P("chan", "space", None),
    )
    out_specs = (P("chan", "space", None), P("chan", "space", None), P(None, "chan", None), P())
    return jax.shard_map(body, mesh=mesh, in_specs=in_specs, out_specs=out_specs, check_vma=False)
```
